32 devices in a mesh: dp: 16 (over z, y, x), head: 2 (over core).
Axes of the slice: x: 2, y: 2, z: 4, core: 2. Of those that a mesh axis runs over, the one named last changes fastest.
Arguments:
- inputs: bfloat16 [64, 512, 1024], P('dp'), may hold values from -6 to 6
- cotangent: bfloat16 [64, 512, 1024], P('dp'), may hold values from -6 to 6
- lengths: int32 [64], P('dp'), may hold values from 128 to 512, as said below
- memory: bfloat16 [64, 2, 512, 1024], P('dp', None, None, 'head'), may hold values from -6 to 6
- compressed: bfloat16 [64, 2, 512, 1024], P('dp', None, None, 'head'), may hold values from -6 to 6
- query_key_value_weight: bfloat16 [1024, 3, 1024], P(None, None, 'head'), may hold values from -0.1875 to 0.1875
- output_weight: bfloat16 [1024, 1024], P('head'), may hold values from -1.5 to 1.5
- up_weight: bfloat16 [1024, 4096], P(None, 'head'), may hold values from -0.1875 to 0.1875
- down_weight: bfloat16 [4096, 1024], P('head'), may hold values from -0.09375 to 0.09375
- gain_one: float32 [1024], replicated, may hold values from 0.5 to 1.5
- gain_two: float32 [1024], replicated, may hold values from 0.5 to 1.5
- slope_rates: float32 [8], P('head'), may hold values from 0.00013020834 to 0.00390625
- conv_weight: bfloat16 [8, 2, 3, 128, 128], P('head'), may hold values from -0.3125 to 0.3125
Outputs:
- outputs: float32 [64, 512, 1024], P('dp')
- grad_inputs: float32 [64, 512, 1024], P('dp')
- memory_next: bfloat16 [64, 2, 512, 1024], P('dp', None, None, 'head')
- compressed_next: bfloat16 [64, 2, 512, 1024], P('dp', None, None, 'head')
- grad_w_qkv: float32 [1024, 3, 1024], P('dp', None, 'head')
- grad_w_out: float32 [1024, 1024], P('head', 'dp')
- grad_w_up: float32 [1024, 4096], P('dp', 'head')
- grad_w_down: float32 [4096, 1024], P('head', 'dp')
- grad_gain_one: float32 [1024], P('dp')
- grad_gain_two: float32 [1024], P('dp')
- grad_slopes: float32 [8], P('head')
- grad_conv: float32 [8, 2, 3, 128, 128], P('head', None, None, 'dp')
The draws below stay inside these ranges and needn't reach their ends.
Inputs may be any that keep to these rules, and one draw needn't show every extreme that they name: `lengths`: each stream's length is 128, 256 or 512; some stream has 512 and some has 128.
All inputs are finite; a program needn't handle non-finite values.
Results may differ from the reference program's by a relative error of at most 0.013.
Values may be sent and summed in bfloat16 or wider, within the bound.
No kernel may reach another device: no remote copies, remote signals or barrier semaphores. Data moves between devices by JAX's collectives and lax.ppermute only.
A program may use at most 320 MiB of HBM per device.

```python
import math
import jax
import jax.numpy as jnp
from jax import lax

D = 1024
H = 8
HD = 128
FF = 4096
L = 512
M = 512
CM = 512
CE = 170
STREAMS = 64


def draw_lengths(key, part):
    picks = jax.random.randint(jax.random.fold_in(key, 11), (STREAMS,), 0, 8)
    quarters = jnp.where(picks < 2, 1, jnp.where(picks < 4, 2, 4))
    chosen = quarters * (L // 4)
    positions = jnp.arange(STREAMS)
    longest = jax.random.randint(jax.random.fold_in(key, 12), (), 0, STREAMS)
    shortest = (longest + 1 + jax.random.randint(jax.random.fold_in(key, 13), (), 0, STREAMS - 1)) % STREAMS
    chosen = jnp.where(positions == longest, L, chosen)
    chosen = jnp.where(positions == shortest, L // 4, chosen)
    return chosen.astype(jnp.int32)


def level_of(rng, extent, shards, low, largest):
    level = 1.0
    for dim, shards_of in shards:
        steps = jax.random.uniform(jax.random.fold_in(jax.random.fold_in(rng, 6), dim), (shards_of,), jnp.float32, low / len(shards), largest / len(shards))
        level = level * jnp.repeat(jnp.exp(steps), extent[dim] // shards_of).reshape((-1,) + (1,) * (len(extent) - 1 - dim))
    return level


def bell_draw(stream_key, dims, deviation, most, cuts=(), held_as=jnp.bfloat16):
    factor_of = level_of(stream_key, dims, cuts, -0.22, 0.18) if cuts else 1.0
    values = jax.random.normal(stream_key, dims, jnp.float32) * deviation * factor_of
    return jnp.minimum(jnp.maximum(values, -most), most).astype(held_as)


def setup_inputs(seed: int = 0) -> dict:
    key_of = jax.random.split(jax.random.key(seed), 14)
    return {
        "inputs": bell_draw(key_of[0], (STREAMS, L, D), 1.0, 6.0, ((0, 16),)),
        "cotangent": bell_draw(key_of[1], (STREAMS, L, D), 1.0, 6.0, ((0, 16),)),
        "lengths": draw_lengths(jax.random.fold_in(key_of[13], 71), 0),
        "memory": bell_draw(key_of[3], (STREAMS, 2, M, D), 1.0, 6.0, ((0, 16), (3, 2))),
        "compressed": bell_draw(key_of[4], (STREAMS, 2, CM, D), 1.0, 6.0, ((0, 16), (3, 2))),
        "query_key_value_weight": bell_draw(key_of[5], (D, 3, D), D ** -0.5, 0.1875, ((2, 2),)),
        "output_weight": bell_draw(key_of[6], (D, D), (D // 64) ** -0.5, 1.5, ((0, 2),)),
        "up_weight": bell_draw(key_of[7], (D, FF), D ** -0.5, 0.1875, ((1, 2),)),
        "down_weight": bell_draw(key_of[8], (FF, D), FF ** -0.5, 0.09375, ((0, 2),)),
        "gain_one": jnp.clip(1.0 + 0.1 * jax.random.normal(key_of[9], (D,), jnp.float32), 0.5, 1.5),
        "gain_two": jnp.clip(1.0 + 0.1 * jax.random.normal(key_of[10], (D,), jnp.float32), 0.5, 1.5),
        "slope_rates": jnp.clip(jnp.exp(math.log(0.00390625) - 3.40119733 * jax.random.uniform(key_of[11], (H,), jnp.float32) ** level_of(key_of[11], (H,), ((0, 2),), -0.2, 0.2)), 0.00013020834, 0.00390625),
        "conv_weight": bell_draw(key_of[12], (H, 2, 3, HD, HD), (3 * HD) ** -0.5, 0.3125, ((0, 2),)),
    }


highest_exactness = lax.Precision.HIGHEST
epsilon = 1e-05

@jax.custom_vjp
def lowered_input(v):
    return lax.optimization_barrier(v.astype(jnp.bfloat16)).astype(jnp.float32)

@jax.custom_vjp
def lowered_input_backward(v):
    return v

def low_keep(v):
    return (lowered_input(v), None)

def low_pass(kept, grad):
    return (grad,)

def back_keep(v):
    return (v, None)

def back_low(kept, grad):
    return (lowered_input(grad),)
lowered_input.defvjp(low_keep, low_pass)
lowered_input_backward.defvjp(back_keep, back_low)

def layer_norm(values, scale_gain):
    centred = values - lax.optimization_barrier(jnp.mean(values, axis=-1, keepdims=True))
    spread = lax.optimization_barrier(jnp.mean(centred * centred, axis=-1, keepdims=True))
    return centred * lax.rsqrt(spread + epsilon) * scale_gain

def attend_stream(pieces, slope_values):
    queries, keys, values, length = pieces
    key_count = keys.shape[0]
    offset = key_count - L
    head_scale = 1.0 / math.sqrt(HD)
    row_index = lax.broadcasted_iota(jnp.int32, (L, key_count), 0)
    col_index = lax.broadcasted_iota(jnp.int32, (L, key_count), 1)
    distance = (row_index + offset - col_index).astype(jnp.float32)
    allowed = (col_index < offset) | (col_index - offset <= row_index) & (col_index - offset < length)
    scores = jnp.einsum('qhe,khe->hqk', queries, keys, precision=highest_exactness) * head_scale
    scores = scores - slope_values[:, None, None] * distance[None]
    scores = jnp.where(allowed[None], lowered_input_backward(scores), -1e+30)
    row_top = lax.optimization_barrier(jnp.max(scores, axis=-1, keepdims=True))
    weights = jnp.exp(scores - row_top)
    probabilities = lowered_input(weights / lax.optimization_barrier(jnp.sum(weights, axis=-1, keepdims=True)))
    return jnp.einsum('hqk,khe->qhe', probabilities, values, precision=highest_exactness)

def forward(params, inputs, lengths, memory, compressed):
    query_key_value_weight, output_weight, up_weight, down_weight, gain_one, gain_two, slope_rates = params
    streams = inputs.shape[0]
    row_validity = (lax.broadcasted_iota(jnp.int32, (streams, L), 1) < lengths[:, None]).astype(jnp.float32)[..., None]
    first_normalized = lowered_input(layer_norm(inputs, gain_one))
    joint_query_key_value = lowered_input(lowered_input_backward(jnp.einsum('huj,jwq->huwq', first_normalized, query_key_value_weight, precision=highest_exactness)))
    queries = joint_query_key_value[:, :, 0].reshape(streams, L, H, HD)
    keys_now = joint_query_key_value[:, :, 1]
    values_now = joint_query_key_value[:, :, 2]
    keys_all = jnp.concatenate([compressed[:, 0], memory[:, 0], keys_now], axis=1).reshape(streams, -1, H, HD)
    values_all = jnp.concatenate([compressed[:, 1], memory[:, 1], values_now], axis=1).reshape(streams, -1, H, HD)

    def one_stream(pieces):
        return attend_stream(pieces, slope_rates)
    head_mixture = lax.map(jax.checkpoint(one_stream), (queries, keys_all, values_all, lengths))
    head_mixture = lowered_input(lowered_input_backward(head_mixture.reshape(streams, L, D)))
    attention_result = lowered_input_backward(jnp.einsum('ngw,wt->ngt', head_mixture, output_weight, precision=highest_exactness))
    middle_state = inputs + attention_result * row_validity
    second_normalized = lowered_input(layer_norm(middle_state, gain_two))
    hidden_state = lowered_input_backward(jnp.einsum('yvh,hn->yvn', second_normalized, up_weight, precision=highest_exactness))
    active_rows_mask = lowered_input(jax.nn.gelu(hidden_state, approximate=True))
    layer_output = middle_state + jnp.einsum('ngw,wt->ngt', active_rows_mask, down_weight, precision=highest_exactness) * row_validity
    return (layer_output, (queries, keys_now, values_now))

def compress(conv, memory):
    streams = memory.shape[0]
    head_count = conv.shape[0]
    head_dim = conv.shape[-1]
    made = memory.shape[2] // 3
    window = memory[:, :, :3 * made].reshape(streams, 2, made, 3, head_count, head_dim)
    squeezed = jnp.einsum('scjthe,hctef->scjhf', window, conv, precision=highest_exactness)
    return squeezed.reshape(streams, 2, made, head_count * head_dim)

def reconstruction(packed, queries, memory, valid_grid):
    streams, query_count, head_count, head_dim = queries.shape
    evicted = 3 * packed.shape[2]
    head_scale = 1.0 / math.sqrt(head_dim)

    def attend_plain(keys, values):
        keys = keys.reshape(streams, -1, head_count, head_dim)
        values = values.reshape(streams, -1, head_count, head_dim)
        scores = jnp.einsum('sqhe,skhe->shqk', queries, keys, precision=highest_exactness) * head_scale
        weights = jax.nn.softmax(scores, axis=-1)
        return jnp.einsum('shqk,skhe->sqhe', weights, values, precision=highest_exactness)
    target = attend_plain(memory[:, 0, :evicted], memory[:, 1, :evicted])
    approach = attend_plain(packed[:, 0], packed[:, 1])
    gap_values = (target - approach) * valid_grid[:, :, None, None]
    return jnp.sum(gap_values * gap_values) / query_count

def reference(inputs, cotangent, lengths, memory, compressed, query_key_value_weight, output_weight, up_weight, down_weight, gain_one, gain_two, slope_rates, conv_weight):
    params = (query_key_value_weight.astype(jnp.float32), output_weight.astype(jnp.float32), up_weight.astype(jnp.float32), down_weight.astype(jnp.float32), gain_one.astype(jnp.float32), gain_two.astype(jnp.float32), slope_rates.astype(jnp.float32))
    conv_float = conv_weight.astype(jnp.float32)
    group_size = math.gcd(STREAMS, max(1, 4096 // L))
    group_count = STREAMS // group_size

    def regroup(array):
        return array.reshape((group_count, group_size) + array.shape[1:])

    def group_step(totals, pieces):
        inputs_group, cot_group, length_group, memory_group, compressed_group = pieces
        inputs_float = inputs_group.astype(jnp.float32)
        memory_float = memory_group.astype(jnp.float32)
        compressed_float = compressed_group.astype(jnp.float32)

        def layer_fn(weights, values):
            return forward(weights, values, length_group, memory_float, compressed_float)
        layer_output, pullback, kept = jax.vjp(layer_fn, params, inputs_float, has_aux=True)
        grad_params, grad_in = pullback(cot_group.astype(jnp.float32))
        queries, keys_now, values_now = kept
        valid_grid = (lax.broadcasted_iota(jnp.int32, (group_size, L), 1) < length_group[:, None]).astype(jnp.float32)
        squeezed = compress(conv_float, memory_float)

        def loss_fn(conv):
            return reconstruction(lowered_input(compress(conv, memory_float)), queries, memory_float, valid_grid)
        loss_value, loss_back = jax.vjp(loss_fn, conv_float)
        grad_conv, = loss_back(jnp.ones_like(loss_value))
        current = jnp.stack([keys_now, values_now], axis=1) * valid_grid[:, None, :, None]
        memory_next = jnp.concatenate([memory_float, current], axis=2)[:, :, L:]
        compressed_next = jnp.concatenate([compressed_float[:, :, CE:], squeezed], axis=2)
        totals = jax.tree.map(jnp.add, totals, tuple(grad_params) + (grad_conv,))
        return (totals, (layer_output.astype(jnp.float32), grad_in.astype(jnp.float32), memory_next.astype(jnp.bfloat16), compressed_next.astype(jnp.bfloat16)))
    zero_totals = tuple((jnp.zeros(piece.shape, jnp.float32) for piece in params)) + (jnp.zeros(conv_float.shape, jnp.float32),)
    totals, stacked = lax.scan(group_step, zero_totals, (regroup(inputs), regroup(cotangent), regroup(lengths), regroup(memory), regroup(compressed)))
    outputs, grad_inputs, memory_next, compressed_next = [piece.reshape((STREAMS,) + piece.shape[2:]) for piece in stacked]
    return (outputs, grad_inputs, memory_next, compressed_next, totals[0], totals[1], totals[2], totals[3], totals[4], totals[5], totals[6], totals[7])
```

```python
import functools
import math

import jax
import jax.numpy as jnp
from jax import lax
from jax.experimental import pallas as pl
from jax.experimental.pallas import tpu as pltpu
from jax.sharding import PartitionSpec as P

HD = 128
CE = 170
EPS = 1e-05
LOG2E = 1.0 / math.log(2.0)
HEAD_SCALE = 1.0 / math.sqrt(HD)
BASE2 = HEAD_SCALE * LOG2E
F32 = jnp.float32
BF16 = jnp.bfloat16
KEEP = BF16


def bits_of(count):
    return count.bit_length() - 1


def flip_pairs(count, bit):
    return [(i, i ^ (1 << bit)) for i in range(count)]


def call(body, grid, in_specs, out_specs, out_shape, scratch=(), prefetch=0, flops=0, moved=0, name=None, aliases=None):
    return pl.pallas_call(
        body,
        grid_spec=pltpu.PrefetchScalarGridSpec(
            num_scalar_prefetch=prefetch,
            grid=grid,
            in_specs=in_specs,
            out_specs=out_specs,
            scratch_shapes=list(scratch),
        ),
        out_shape=out_shape,
        input_output_aliases=aliases or {},
        compiler_params=pltpu.CompilerParams(dimension_semantics=("arbitrary",) * len(grid)),
        cost_estimate=pl.CostEstimate(flops=int(flops), bytes_accessed=int(moved), transcendentals=0),
        name=name,
    )


def whole(shape):
    zeros = (0,) * len(shape)
    return pl.BlockSpec(shape, lambda *_: zeros, pipeline_mode=pl.Buffered(1))


def per_stream(rows, n):
    return pl.BlockSpec((1, rows, n), lambda s, *_: (s, 0, 0))


def turned(rows, n):
    return pl.BlockSpec((n, rows), lambda s, *_: (0, s))


def like(streams, rows, n, kind):
    return jax.ShapeDtypeStruct((streams, rows, n), kind)


def dot(a, b):
    return jnp.dot(a, b, preferred_element_type=F32)


def dot_nt(a, b):
    return lax.dot_general(a, b, (((1,), (1,)), ((), ())), preferred_element_type=F32)


def dot_tn(a, b):
    return lax.dot_general(a, b, (((0,), (0,)), ((), ())), preferred_element_type=F32)


def statistics(v):
    centred = v - jnp.mean(v, axis=-1, keepdims=True)
    spread = jnp.mean(centred * centred, axis=-1, keepdims=True)
    return centred, lax.rsqrt(spread + EPS)


def by_rows(rows, step, body, together=8):
    def one(i, carry):
        for j in range(together):
            body(pl.multiple_of((i * together + j) * step, step))
        return carry

    lax.fori_loop(0, rows // (step * together), one, 0)


def row_ids(start, step):
    return start + lax.broadcasted_iota(jnp.int32, (step, 1), 0)


def project_body(len_ref, x_ref, gain_ref, w_ref, normed_t_ref, q_ref, kv_ref, normed_ref):
    rows, width = q_ref.shape[1], q_ref.shape[2]
    length = len_ref[pl.program_id(0)]

    def norm(r):
        centred, scale = statistics(x_ref[0, pl.ds(r, 16), :].astype(F32))
        normed_ref[pl.ds(r, 16), :] = (centred * scale * gain_ref[...]).astype(BF16)

    by_rows(rows, 16, norm)
    normed_t_ref[...] = normed_ref[...].T
    valid = row_ids(0, rows) < length
    normed = normed_ref[...]
    q_ref[0] = dot(normed, w_ref[:, :width]).astype(BF16)
    for c in range(2):
        now = dot(normed, w_ref[:, (c + 1) * width : (c + 2) * width])
        kv_ref[0, c] = jnp.where(valid, now, 0.0).astype(BF16)


def project(lengths, x, gain, w):
    streams, rows, model = x.shape
    width = w.shape[1] // 3
    per = lambda *tail: pl.BlockSpec((1,) + tail, lambda s, *_: (s,) + (0,) * len(tail))
    return call(
        project_body,
        (streams,),
        [per(rows, model), whole((1, model)), whole(w.shape)],
        [pl.BlockSpec((model, rows), lambda s, *_: (0, s)), per(rows, width), per(2, rows, width)],
        [
            jax.ShapeDtypeStruct((model, streams * rows), BF16),
            jax.ShapeDtypeStruct((streams, rows, width), BF16),
            jax.ShapeDtypeStruct((streams, 2, rows, width), BF16),
        ],
        scratch=[pltpu.VMEM((rows, model), BF16)],
        prefetch=1,
        flops=2 * streams * rows * model * 3 * width,
        moved=2 * (streams * rows * (3 * model + 3 * width) + w.size),
        name="project",
    )(lengths, x, gain, w)


def position_columns(keys):
    centre = keys // 2
    lane = lax.broadcasted_iota(jnp.int32, (keys, HD), 1)
    place = lax.broadcasted_iota(jnp.int32, (keys, HD), 0) - centre
    fine = place & 7
    coarse = place - fine
    value = jnp.where(lane < 6, jnp.where((lane & 1) == 0, coarse, fine), jnp.where(lane == 6, 1, 0))
    return value.astype(F32).astype(BF16)


def slope_columns(slope, rows):
    exact = jnp.full((8, HD), slope, F32) * (1.0 / HEAD_SCALE)
    first = exact.astype(BF16).astype(F32)
    second = (exact - first).astype(BF16).astype(F32)
    third = exact - first - second
    lane = lax.broadcasted_iota(jnp.int32, (8, HD), 1)
    value = jnp.where(lane < 2, first, jnp.where(lane < 4, second, jnp.where(lane < 6, third, 0.0)))
    return jnp.broadcast_to(value[:1], (rows, HD)).astype(BF16)


def one_column(keys):
    lane = lax.broadcasted_iota(jnp.int32, (keys, HD), 1)
    return jnp.where(lane == 0, 1.0, 0.0).astype(BF16)


def diagonal_mask(block, start, length):
    row = lax.broadcasted_iota(jnp.int32, (block, block), 0)
    col = lax.broadcasted_iota(jnp.int32, (block, block), 1)
    return col <= jnp.minimum(row, length - 1 - start)


def pipelined(chains, front, rest):
    following = front(*chains[0])
    for n, chain in enumerate(chains):
        current = following
        if n + 1 < len(chains):
            following = front(*chains[n + 1])
        rest(*chain, *current)


def lanes_of(a):
    return slice(a * HD, (a + 1) * HD)


def attend_body(len_ref, slope_ref, q_ref, old_ref, mem_ref, now_ref, wo_ref, mix_ref, exact_ref, lse_ref, part_ref, kbuf, vbuf):
    s = pl.program_id(0)
    rows, heads = q_ref.shape[1], q_ref.shape[2] // HD
    old, mem = old_ref.shape[2], mem_ref.shape[2]
    past = old + mem
    keys = past + rows
    block = rows // 2
    length = len_ref[s]

    @pl.when(s == 0)
    def _():
        for a in range(heads):
            kbuf[a, :, HD:] = position_columns(keys)
            vbuf[a, :, HD:] = one_column(keys)

    for a in range(heads):
        for buf, c in ((kbuf, 0), (vbuf, 1)):
            buf[a, :old, :HD] = old_ref[0, c, :, lanes_of(a)]
            buf[a, old:past, :HD] = mem_ref[0, c, :, lanes_of(a)]
            buf[a, past:, :HD] = now_ref[0, c, :, lanes_of(a)]

    def front(a, high):
        side = slope_columns(slope_ref[a], high)
        wide = jnp.concatenate([q_ref[0, :high, lanes_of(a)], side], axis=1)
        return (dot_nt(wide, kbuf[a, : past + high]),)

    def rest(a, high, scores):
        allowed = diagonal_mask(high, 0, length)
        last = jnp.where(allowed, scores[:, past:], -1e30)
        scores = jnp.concatenate([scores[:, :past], last], axis=1)
        top = jnp.max(scores, axis=1, keepdims=True)
        weights = jnp.exp2((scores - top) * BASE2).astype(BF16)
        both = dot(weights, vbuf[a, : past + high])
        total = both[:, HD : HD + 1]
        mixed = both[:, :HD] / total
        exact_ref[0, :high, lanes_of(a)] = mixed
        mix_ref[0, :high, lanes_of(a)] = mixed.astype(BF16)
        lse_ref[0, :high, lanes_of(a)] = jnp.broadcast_to(top * BASE2 + jnp.log2(total), (high, HD))

    @pl.when(length > block)
    def _():
        pipelined([(a, rows) for a in range(heads)], front, rest)

    @pl.when(length <= block)
    def _():
        pipelined([(a, block) for a in range(heads)], front, rest)
        exact_ref[0, block:, :] = jnp.zeros((rows - block, heads * HD), F32)
        mix_ref[0, block:, :] = jnp.zeros((rows - block, heads * HD), BF16)
        lse_ref[0, block:, :] = jnp.zeros((rows - block, heads * HD), F32)

    part_ref[0] = dot(mix_ref[0], wo_ref[...]).astype(BF16)


def attend(lengths, slopes, q, compressed, memory, now, wo):
    streams, rows, width = q.shape
    heads = width // HD
    model = wo.shape[1]
    keys = compressed.shape[2] + memory.shape[2] + rows
    cache = lambda a: pl.BlockSpec((1, 2, a.shape[2], width), lambda s, *_: (s, 0, 0, 0))
    return call(
        attend_body,
        (streams,),
        [per_stream(rows, width), cache(compressed), cache(memory), cache(now), whole(wo.shape)],
        [per_stream(rows, width), per_stream(rows, width), per_stream(rows, width), per_stream(rows, model)],
        [
            jax.ShapeDtypeStruct((streams, rows, width), BF16),
            jax.ShapeDtypeStruct((streams, rows, width), F32),
            jax.ShapeDtypeStruct((streams, rows, width), F32),
            jax.ShapeDtypeStruct((streams, rows, model), BF16),
        ],
        scratch=[pltpu.VMEM((heads, keys, 2 * HD), BF16), pltpu.VMEM((heads, keys, 2 * HD), BF16)],
        prefetch=2,
        flops=2 * streams * rows * (4 * keys * width + width * model),
        moved=2 * (q.size + compressed.size + memory.size + now.size) + 12 * q.size,
        name="attend",
    )(lengths, slopes, q, compressed, memory, now, wo)


def attend_back_body(first, len_ref, slope_ref, q_ref, old_ref, mem_ref, now_ref, exact_ref, lse_ref, grad_ref, out_ref, slope_out_ref, kbuf, vbuf):
    s = pl.program_id(0)
    rows, heads = q_ref.shape[1], q_ref.shape[2] // HD
    old, mem = old_ref.shape[2], mem_ref.shape[2]
    past = old + mem
    keys = past + rows
    block = rows // 2
    length = len_ref[s]

    @pl.when(s == 0)
    def _():
        for a in range(heads):
            kbuf[a, :, HD:] = position_columns(keys)
        slope_out_ref[...] = jnp.zeros_like(slope_out_ref)

    for a in range(heads):
        kbuf[a, :old, :HD] = old_ref[0, 0, :, lanes_of(a)]
        kbuf[a, old:past, :HD] = mem_ref[0, 0, :, lanes_of(a)]
        kbuf[a, past:, :HD] = now_ref[0, 0, :, lanes_of(a)]
        vbuf[a, :old] = old_ref[0, 1, :, lanes_of(a)]
        vbuf[a, old:past] = mem_ref[0, 1, :, lanes_of(a)]
        vbuf[a, past:] = now_ref[0, 1, :, lanes_of(a)]

    def here(i):
        return slice(i * block, (i + 1) * block)

    def front(a, i):
        side = slope_columns(slope_ref[first + a], block)
        wide = jnp.concatenate([q_ref[0, here(i), lanes_of(a)], side], axis=1)
        reach = past + (i + 1) * block
        return dot_nt(wide, kbuf[a, :reach]), dot_nt(grad_ref[0, here(i), lanes_of(a)], vbuf[a, :reach])

    def run(blocks):
        sums = {}

        def rest(a, i, scores, grad_probs):
            reach = past + (i + 1) * block
            q, grad = q_ref[0, here(i), lanes_of(a)], grad_ref[0, here(i), lanes_of(a)]
            exact = jnp.exp2(scores * BASE2 - lse_ref[0, here(i), a * HD : a * HD + 1])
            allowed = diagonal_mask(block, i * block, length)
            last = jnp.where(allowed, exact[:, reach - block :], 0.0)
            exact = jnp.concatenate([exact[:, : reach - block], last], axis=1)
            inner = jnp.sum(grad.astype(F32) * exact_ref[0, here(i), lanes_of(a)], axis=1, keepdims=True)
            grad_scores = (exact * (grad_probs - inner)).astype(BF16)
            wide = dot(grad_scores, kbuf[a, :reach])
            out_ref[0, 0, here(i), lanes_of(a)] = (wide[:, :HD] * HEAD_SCALE).astype(BF16)
            coarse, fine, total = (wide[:, HD + n : HD + n + 1] for n in (0, 1, 6))
            distance = (past + i * block - keys // 2 + lax.broadcasted_iota(jnp.int32, (block, 1), 0)).astype(F32)
            moment = jnp.sum(coarse + fine - distance * total, axis=0, keepdims=True)
            grad_keys = dot_tn(grad_scores[:, past:], q)
            grad_values = dot_tn(exact[:, past:].astype(BF16), grad)
            if i > 0:
                moment = moment + sums[a][0]
                done = sums[a][1].shape[0]
                join = lambda before, now: jnp.concatenate([before + now[:done], now[done:]], axis=0)
                grad_keys, grad_values = join(sums[a][1], grad_keys), join(sums[a][2], grad_values)
            sums[a] = moment, grad_keys, grad_values
            if i == blocks - 1:
                high = blocks * block
                out_ref[1, 0, :high, lanes_of(a)] = (grad_keys * HEAD_SCALE).astype(BF16)
                out_ref[2, 0, :high, lanes_of(a)] = grad_values.astype(BF16)
                slope_out_ref[first + a : first + a + 1, :] += jnp.broadcast_to(moment, (1, HD))

        pipelined([(a, i) for a in range(heads) for i in range(blocks)], front, rest)

    @pl.when(length > block)
    def _():
        run(2)

    @pl.when(length <= block)
    def _():
        run(1)
        for c in range(3):
            out_ref[c, 0, block:, :] = jnp.zeros((rows - block, heads * HD), BF16)


def attend_back(first, heads, lengths, slopes, q, compressed, memory, now, exact, lse, grad):
    streams, rows, width = q.shape
    keys = compressed.shape[2] + memory.shape[2] + rows
    group = first // heads
    cache = lambda a: pl.BlockSpec((1, 2, a.shape[2], heads * HD), lambda s, *_: (s, 0, 0, group))
    some = pl.BlockSpec((1, rows, heads * HD), lambda s, *_: (s, 0, group))
    return call(
        functools.partial(attend_back_body, first),
        (streams,),
        [some, cache(compressed), cache(memory), cache(now), some, some, some],
        [pl.BlockSpec((3, 1, rows, heads * HD), lambda s, *_: (0, s, 0, 0)), pl.BlockSpec((8, HD), lambda *_: (0, 0))],
        [jax.ShapeDtypeStruct((3, streams, rows, heads * HD), BF16), jax.ShapeDtypeStruct((8, HD), F32)],
        scratch=[pltpu.VMEM((heads, keys, 2 * HD), BF16), pltpu.VMEM((heads, keys, HD), BF16)],
        prefetch=2,
        flops=2 * streams * rows * heads * HD * 8 * keys,
        moved=heads * HD * streams * rows * 40,
        name="attend_back",
    )(lengths, slopes, q, compressed, memory, now, exact, lse, grad)


GELU_K = math.sqrt(2.0 / math.pi)
GELU_C = 0.044715


def gate_of(v):
    square = v * v
    rate = -2.0 * GELU_K * LOG2E
    return 1.0 / (1.0 + jnp.exp2(v * (rate + (rate * GELU_C) * square))), square


def gelu_slope(v):
    gate, square = gate_of(v)
    lean = v * (2.0 * GELU_K + (6.0 * GELU_K * GELU_C) * square)
    return gate * (1.0 + lean * (1.0 - gate))


def rise_body(len_ref, x_ref, own_ref, other_ref, cot_ref, gain_ref, up_ref, mid_ref, normed_t_ref, branch_t_ref, active_ref, before_ref, normed, branch):
    rows = x_ref.shape[1]
    hidden_width = up_ref.shape[1]
    length = len_ref[pl.program_id(0)]

    def norm(r):
        here = pl.ds(r, 16)
        valid = (row_ids(r, 16) < length).astype(F32)
        attended = own_ref[0, here, :].astype(F32) + other_ref[0, here, :].astype(F32)
        middle = x_ref[0, here, :].astype(F32) + attended * valid
        mid_ref[0, here, :] = middle
        centred, scale = statistics(middle)
        normed[here, :] = (centred * scale * gain_ref[...]).astype(BF16)
        branch[here, :] = (cot_ref[0, here, :].astype(F32) * valid).astype(BF16)

    by_rows(rows, 16, norm)
    normed_t_ref[...] = normed[...].T
    branch_t_ref[...] = branch[...].T
    chunk = min(512, hidden_width)
    columns = [slice(f, f + chunk) for f in range(0, hidden_width, chunk)]

    def front(cols):
        return (dot(normed[...], up_ref[:, cols]),)

    def rest(cols, v):
        active_ref[0, :, cols] = (v * gate_of(v)[0]).astype(BF16)
        before_ref[0, :, cols] = v.astype(BF16)

    pipelined([(cols,) for cols in columns], front, rest)


def rise(lengths, x, own, other, cot, gain, up):
    streams, rows, model = x.shape
    hidden = up.shape[1]
    tokens = streams * rows
    return call(
        rise_body,
        (streams,),
        [per_stream(rows, model)] * 4 + [whole((1, model)), whole(up.shape)],
        [per_stream(rows, model), turned(rows, model), turned(rows, model), per_stream(rows, hidden), per_stream(rows, hidden)],
        [
            like(streams, rows, model, F32),
            jax.ShapeDtypeStruct((model, tokens), BF16),
            jax.ShapeDtypeStruct((model, tokens), BF16),
            like(streams, rows, hidden, BF16),
            like(streams, rows, hidden, BF16),
        ],
        scratch=[pltpu.VMEM((rows, model), BF16), pltpu.VMEM((rows, model), BF16)],
        prefetch=1,
        flops=2 * tokens * model * hidden,
        moved=tokens * (16 * model + 4 * hidden) + 2 * model * hidden,
        name="rise",
    )(lengths, x, own, other, cot, gain, up)


def fall_body(len_ref, cot_ref, before_ref, up_ref, down_ref, hidden_ref, *back_refs):
    rows = cot_ref.shape[1]
    hidden_width = up_ref.shape[1]
    valid = row_ids(0, rows) < len_ref[pl.program_id(0)]
    branch = jnp.where(valid, cot_ref[0].astype(F32), 0.0).astype(BF16)
    chunk = min(512, hidden_width)
    back = []

    def front(cols):
        return (dot_nt(branch, down_ref[cols, :]),)

    def rest(cols, grad_active):
        grad_hidden = (grad_active * gelu_slope(before_ref[0, :, cols].astype(F32))).astype(BF16)
        hidden_ref[0, :, cols] = grad_hidden
        back.append(dot_nt(grad_hidden, up_ref[:, cols]))

    pipelined([(slice(f, f + chunk),) for f in range(0, hidden_width, chunk)], front, rest)
    total = sum(back[1:], back[0]).astype(BF16)
    part = total.shape[1] // len(back_refs)
    for n, back_ref in enumerate(back_refs):
        back_ref[0] = total[:, n * part : (n + 1) * part]


PIECES = 4


def fall(lengths, cot, slope, up, down):
    streams, rows, model = cot.shape
    hidden = up.shape[1]
    tokens = streams * rows
    return call(
        fall_body,
        (streams,),
        [per_stream(rows, model), per_stream(rows, hidden), whole(up.shape), whole(down.shape)],
        [per_stream(rows, hidden)] + [per_stream(rows, model // PIECES)] * PIECES,
        [like(streams, rows, hidden, BF16)] + [like(streams, rows, model // PIECES, BF16)] * PIECES,
        prefetch=1,
        flops=4 * tokens * model * hidden,
        moved=tokens * (4 * model + 4 * hidden) + 4 * model * hidden,
        name="fall",
    )(lengths, cot, slope, up, down)


def leave_body(_, active_ref, down_ref, part_ref):
    part_ref[0] = dot(active_ref[0], down_ref[...]).astype(BF16)


def leave(lengths, active, down):
    streams, rows, hidden = active.shape
    model = down.shape[1]
    return call(
        leave_body,
        (streams,),
        [per_stream(rows, hidden), whole(down.shape)],
        per_stream(rows, model),
        like(streams, rows, model, BF16),
        prefetch=1,
        flops=2 * streams * rows * model * hidden,
        moved=2 * (active.size + down.size + streams * rows * model),
        name="leave",
    )(lengths, active, down)


def outputs_body(start, len_ref, mid_ref, own_ref, other_ref, out_ref):
    rows = mid_ref.shape[1]
    length = len_ref[start + pl.program_id(0)]

    def one(r):
        here = pl.ds(r, 16)
        valid = (row_ids(r, 16) < length).astype(F32)
        branch = own_ref[0, here, :].astype(F32) + other_ref[0, here, :].astype(F32)
        out_ref[0, here, :] = mid_ref[0, here, :] + valid * branch

    by_rows(rows, 16, one, 4)


def in_part(body, first, count, into, lengths, args, gain, like_this, name):
    rows, model = like_this.shape[1:]
    per = pl.BlockSpec((1, rows, model), lambda s, *_: (s + first, 0, 0))
    extra = [] if gain is None else [whole(gain.shape)]
    held = [] if into is None else [into]

    def inner(len_ref, *refs):
        body(first, len_ref, *refs[: len(args) + len(extra)], refs[-1])

    return call(
        inner,
        (count,),
        [per] * len(args) + extra + [pl.BlockSpec(memory_space=pl.ANY)] * len(held),
        per,
        jax.ShapeDtypeStruct(like_this.shape, F32),
        prefetch=1,
        aliases={1 + len(args) + len(extra): 0} if held else {},
        moved=count * rows * model * 14,
        name=name,
    )(lengths, *args, *([] if gain is None else [gain]), *held)


def chunk_at(place, order, me):
    apart = 0
    for i, bit in enumerate(order):
        apart |= ((place >> (len(order) - 1 - i)) & 1) << bit
    return apart ^ me


def send_order(source, order, me, first, count):
    deep = source.shape[0] // (1 << len(order))
    lines = []
    for p in range(first, first + count):
        lines.append(source[pl.ds(pl.multiple_of(chunk_at(p, order, me) * deep, deep), deep), :])
    return jnp.concatenate(lines, axis=0)


def weight_body(orders, spans, extra, me_ref, *refs):
    sources = [span[3] for span in spans]
    xts = list(refs[: sum(sources)])
    ys = refs[sum(sources) : sum(sources) + len(spans)]
    sides = refs[sum(sources) + len(spans) : -2]
    outs = refs[-2:]
    me = me_ref[0]
    j = pl.program_id(0)
    places = 1 << len(orders[0])
    for y, (start, stop, order, product) in zip(ys, spans):
        xt = xts.pop(0) if product else None

        @pl.when((j >= start) & (j < stop))
        def _(xt=xt, y=y, order=order):
            for out, first in ((outs[0], 0), (outs[1], places // 2)):
                if xt is None:
                    block = send_order(y, order, me, first, places // 2)
                else:
                    block = dot(send_order(xt, order, me, first, places // 2), y[...] if len(y.shape) == 2 else y[0])
                out[: block.shape[0], :] = block.astype(out.dtype)

    if extra:
        total = sum(side[...] for side in sides)
        first = total.astype(BF16).astype(F32)
        both = jnp.concatenate([first, total - first], axis=0).astype(BF16)
        outs[1][outs[1].shape[0] - extra :, :] = jnp.concatenate([both] * (outs[1].shape[1] // HD), axis=1)


def weight_gradient(me, sources, step, name, sides=()):
    places = 1 << len(sources[0][2])
    model = next(xt.shape[0] for xt, _, _ in sources if xt is not None)
    spans, specs, at = [], [], 0
    for xt, y, order in sources:
        n = y.shape[-1] // step
        blocks = n * (y.shape[0] if y.ndim == 3 else 1)
        spans.append((at, at + blocks, order, xt is not None))
        if y.ndim == 3:
            pick = lambda j, *_, at=at, n=n, blocks=blocks: (jnp.clip(j - at, 0, blocks - 1) // n, 0, jnp.clip(j - at, 0, blocks - 1) % n)
            specs.append(pl.BlockSpec((1, y.shape[1], step), pick))
        else:
            specs.append(pl.BlockSpec((y.shape[0], step), lambda j, *_, at=at, blocks=blocks: (0, jnp.clip(j - at, 0, blocks - 1))))
        at += blocks
    columns = at * step
    extra = 16 if sides else 0
    turned_sources = [xt for xt, _, _ in sources if xt is not None]
    return call(
        functools.partial(weight_body, [s[2] for s in sources], spans, extra),
        (at,),
        [whole(xt.shape) for xt in turned_sources] + specs + [whole(side.shape) for side in sides],
        [pl.BlockSpec((model // 2, step), lambda j, *_: (0, j)), pl.BlockSpec((model // 2 + extra, step), lambda j, *_: (0, j))],
        [jax.ShapeDtypeStruct((model // 2, columns), KEEP), jax.ShapeDtypeStruct((model // 2 + extra, columns), BF16)],
        prefetch=1,
        flops=2 * model * turned_sources[0].shape[1] * columns,
        moved=2 * (sum(xt.size for xt in turned_sources) + turned_sources[0].shape[1] * columns + model * columns),
        name=name,
    )(me, *turned_sources, *[s[1] for s in sources], *sides)


class Halving:
    def __init__(self, keep, send, order, count, side=None):
        self.order, self.count, self.stage, self.total = order, count, 0, None
        self.keep, self.side = keep, side
        self.send(send)

    def send(self, what):
        self.sent = what
        self.came = lax.ppermute(what, "dp", flip_pairs(self.count, self.order[self.stage]))

    def step(self, token):
        if self.total is not None:
            return token
        came = after(self.came, token).astype(F32)
        high = self.keep.shape[0]
        total = self.keep.astype(F32) + came[:high]
        if self.side is not None:
            self.side = self.side + (came[high : high + 8] + came[high + 8 :])
        self.stage += 1
        if self.stage == len(self.order):
            self.total = total
            return total
        half = high // 2
        self.keep = total[:half].astype(KEEP)
        send = total[half:].astype(BF16)
        if self.side is not None:
            first = lax.reduce_precision(self.side, 8, 7)
            send = jnp.concatenate([send, first.astype(BF16), (self.side - first).astype(BF16)], axis=0)
        self.send(send)
        return self.sent


def after(value, token):
    return lax.optimization_barrier((value, token))[0]


def conv_rows(grad, ranks, model, columns):
    share = grad.shape[3] // ranks
    pieces = math.prod(grad.shape[:3])
    groups = -(-pieces * HD // model)
    grad = grad.astype(BF16).reshape(pieces, ranks, share, HD)
    grad = jnp.pad(grad, ((0, groups * (model // HD) - pieces), (0, 0), (0, 0), (0, 0)))
    grad = grad.reshape(groups, model // HD, ranks, share, HD).transpose(2, 1, 3, 0, 4).reshape(model, groups * HD)
    return jnp.pad(grad, ((0, 0), (0, columns - groups * HD)))


def conv_share(total, like, ranks, model):
    share = like.shape[3] // ranks
    pieces = math.prod(like.shape[:3])
    groups = -(-pieces * HD // model)
    total = total[:, : groups * HD].reshape(model // HD, share, groups, HD).transpose(2, 0, 1, 3)
    return total.reshape(groups * (model // HD), share, HD)[:pieces].reshape(like.shape[:3] + (share, HD))


def pair_over_head(part):
    count = lax.axis_size("head")
    for bit in range(bits_of(count)):
        came = lax.ppermute(part, "head", flip_pairs(count, bit))
        if bit == bits_of(count) - 1:
            return part, came
        part = (part.astype(F32) + came.astype(F32)).astype(part.dtype)
    return part, jnp.zeros_like(part)


def middle_body(len_ref, *refs):
    owns, others = refs[:PIECES], refs[PIECES : 2 * PIECES]
    mid_ref, cot_ref, gain_ref, wo_ref, grad_ref, turned_ref, mixed_ref, attended = refs[2 * PIECES :]
    rows = mid_ref.shape[1]
    s = pl.program_id(0)
    length = len_ref[s]

    def one(r):
        here = pl.ds(r, 16)
        valid = (row_ids(r, 16) < length).astype(F32)
        middle = mid_ref[0, here, :]
        sums = [own[0, here, :].astype(F32) + other[0, here, :].astype(F32) for own, other in zip(owns, others)]
        grad = jnp.concatenate(sums, axis=1)
        centred, scale = statistics(middle)
        hat = centred * scale
        e = grad * gain_ref[...]
        lean = jnp.mean(e * hat, axis=-1, keepdims=True)
        total = cot_ref[0, here, :].astype(F32) + scale * (e - jnp.mean(e, axis=-1, keepdims=True) - hat * lean)
        grad_ref[0, here, :] = total
        attended[here, :] = (total * valid).astype(BF16)

    by_rows(rows, 16, one)
    turned_ref[...] = attended[...].T
    mixed_ref[0] = dot_nt(attended[...], wo_ref[...]).astype(BF16)


def middle_back(lengths, owns, others, mid, cot, gain, wo):
    streams, rows, model = mid.shape
    width = wo.shape[0]
    return call(
        middle_body,
        (streams,),
        [per_stream(rows, model // PIECES)] * (2 * PIECES) + [per_stream(rows, model)] * 2 + [whole((1, model)), whole(wo.shape)],
        [per_stream(rows, model), turned(rows, model), per_stream(rows, width)],
        [
            jax.ShapeDtypeStruct(mid.shape, F32),
            jax.ShapeDtypeStruct((model, streams * rows), BF16),
            like(streams, rows, width, BF16),
        ],
        scratch=[pltpu.VMEM((rows, model), BF16)],
        prefetch=1,
        flops=2 * streams * rows * model * width,
        moved=mid.size * 16,
        name="middle_back",
    )(lengths, *owns, *others, mid, cot, gain, wo)


def lower_body(_, *refs):
    pieces, (w_ref, part_ref) = refs[:-2], refs[-2:]
    joint = jnp.concatenate([piece[c, 0] for c in range(3) for piece in pieces], axis=1)
    part_ref[0] = dot_nt(joint, w_ref[...]).astype(BF16)


def lower(lengths, pieces, w):
    model = w.shape[0]
    _, streams, rows, _ = pieces[0].shape
    joint = lambda a: pl.BlockSpec((3, 1, rows, a.shape[3]), lambda s, *_: (0, s, 0, 0))
    return call(
        lower_body,
        (streams,),
        [joint(a) for a in pieces] + [whole(w.shape)],
        per_stream(rows, model),
        like(streams, rows, model, BF16),
        prefetch=1,
        flops=2 * streams * rows * model * w.shape[1],
        moved=streams * rows * model * 6,
        name="lower",
    )(lengths, *pieces, w)


def inputs_body(_, __, x_ref, own_ref, other_ref, grad_ref, gain_ref, out_ref):
    rows = x_ref.shape[1]

    def one(r):
        here = pl.ds(r, 16)
        centred, scale = statistics(x_ref[0, here, :].astype(F32))
        hat = centred * scale
        e = (own_ref[0, here, :].astype(F32) + other_ref[0, here, :].astype(F32)) * gain_ref[...]
        lean = jnp.mean(e * hat, axis=-1, keepdims=True)
        out_ref[0, here, :] = grad_ref[0, here, :] + scale * (e - jnp.mean(e, axis=-1, keepdims=True) - hat * lean)

    by_rows(rows, 16, one)


SLOTS = 256


def rebuild_body(len_ref, q_ref, mem_ref, old_ref, conv_ref, next_ref, grad_ref, wide):
    s = pl.program_id(0)
    rows, heads = q_ref.shape[1], q_ref.shape[2] // HD
    slots = mem_ref.shape[2]
    made = slots // 3
    valid = row_ids(0, rows) < len_ref[s]
    row = lax.broadcasted_iota(jnp.int32, (slots, HD), 0)

    @pl.when(s == 0)
    def _():
        grad_ref[...] = jnp.zeros_like(grad_ref)
        wide[...] = jnp.zeros_like(wide)

    def front(a):
        windows, packed = [], []
        for c in range(2):
            wide[a, c, :slots] = mem_ref[0, c, :, lanes_of(a)].astype(F32)
            taps = [wide[a, c, pl.ds(t, SLOTS, stride=3), :].astype(BF16) for t in range(3)]
            windows.append(jnp.concatenate(taps, axis=1))
            squeezed = dot(windows[c], conv_ref[a, c].reshape(3 * HD, HD))
            packed.append(squeezed.astype(BF16))
            tail = jnp.concatenate([squeezed, jnp.zeros((slots - SLOTS, HD), F32)], axis=0)
            kept = pltpu.roll(old_ref[0, c, :, lanes_of(a)].astype(F32), slots - made, 0)
            tail = pltpu.roll(tail, slots - made, 0)
            next_ref[0, c, :, lanes_of(a)] = jnp.where(row < slots - made, kept, tail).astype(BF16)
        q = q_ref[0, :, lanes_of(a)]
        return windows, packed, dot_nt(q, mem_ref[0, 0, :, lanes_of(a)]), dot_nt(q, packed[0])

    def soft(scores, count):
        start = scores.shape[1] - HD
        lane = start + lax.broadcasted_iota(jnp.int32, (rows, HD), 1)
        last = jnp.where(lane < count, scores[:, start:], -1e30)
        scores = jnp.concatenate([scores[:, :start], last], axis=1)
        weights = jnp.exp2((scores - jnp.max(scores, axis=1, keepdims=True)) * BASE2)
        return weights, 1.0 / jnp.sum(weights, axis=1, keepdims=True)

    def rest(a, windows, packed, scores, few_scores):
        q = q_ref[0, :, lanes_of(a)]
        weights, share = soft(few_scores, made)
        probs = weights * share
        low = probs.astype(BF16)
        approach = dot(low, packed[1])
        weights, share = soft(scores, 3 * made)
        target = dot(weights.astype(BF16), mem_ref[0, 1, :, lanes_of(a)]) * share
        grad = jnp.where(valid, (approach - target) * (2.0 / rows), 0.0).astype(BF16)
        grad_probs = dot_nt(grad, packed[1])
        inner = jnp.sum(probs * grad_probs, axis=1, keepdims=True)
        grad_scores = (probs * (grad_probs - inner) * HEAD_SCALE).astype(BF16)
        back = [dot_tn(grad_scores, q), dot_tn(low, grad)]
        for c in range(2):
            grad_ref[a, c] += dot_tn(windows[c], back[c].astype(BF16)).reshape(3, HD, HD)

    pipelined([(a,) for a in range(heads)], front, rest)


def rebuild(lengths, q, memory, compressed, conv):
    streams, rows, width = q.shape
    heads = width // HD
    slots = memory.shape[2]
    cache = pl.BlockSpec((1, 2, slots, width), lambda s, *_: (s, 0, 0, 0))
    return call(
        rebuild_body,
        (streams,),
        [per_stream(rows, width), cache, cache, whole(conv.shape)],
        [cache, pl.BlockSpec(conv.shape, lambda *_: (0,) * conv.ndim)],
        [jax.ShapeDtypeStruct(compressed.shape, BF16), jax.ShapeDtypeStruct(conv.shape, F32)],
        scratch=[pltpu.VMEM((heads, 2, 3 * SLOTS, HD), F32)],
        prefetch=1,
        flops=2 * streams * rows * heads * 256 * (2 * slots + 5 * SLOTS),
        moved=2 * (q.size + memory.size + 2 * compressed.size) + 6 * conv.size,
        name="rebuild",
    )(lengths, q, memory, compressed, conv)


def per_device(
    inputs,
    cotangent,
    lengths,
    memory,
    compressed,
    query_key_value_weight,
    output_weight,
    up_weight,
    down_weight,
    gain_one,
    gain_two,
    slope_rates,
    conv_weight,
):
    streams, rows, model = inputs.shape
    tokens = streams * rows
    heads = slope_rates.shape[0]
    width = heads * HD
    ranks = lax.axis_size("dp")
    rank_bits = bits_of(ranks)
    me = lax.axis_index("dp").astype(jnp.int32)
    me_array = me.reshape(1)
    later = tuple(range(2, rank_bits))
    x_first, y_first, x_then_z = (0, 1) + later, (1, 0) + later, (0,) + later + (1,)
    gain_1, gain_2 = gain_one.reshape(1, model), gain_two.reshape(1, model)
    qkv = query_key_value_weight.reshape(model, 3 * width)

    normed_t, q, memory_next = project(lengths, inputs, gain_1, qkv)
    mixed, exact, lse, part = attend(lengths, slope_rates, q, compressed, memory, memory_next, output_weight)
    own, other = pair_over_head(part)
    compressed_next, grad_conv = rebuild(after(lengths, part), q, memory, compressed, conv_weight)
    step = min(512, up_weight.shape[1])
    conv = conv_rows(grad_conv, ranks, model, step)
    mid, normed_two_t, branch_t, active, before = rise(
        after(lengths, conv), inputs, own, other, cotangent, gain_2, up_weight
    )
    keep, send = weight_gradient(me_array, [(branch_t, active.reshape(tokens, -1), x_then_z)], step, "grad_down")
    down = Halving(keep, send, x_then_z, ranks)
    grad_hidden, *backs = fall(after(lengths, send), cotangent, before, up_weight, down_weight)
    owns, others = zip(*[pair_over_head(back) for back in backs])
    sources = [(normed_two_t, grad_hidden.reshape(tokens, -1), y_first), (None, conv, y_first)]
    keep, send = weight_gradient(me_array, sources, step, "grad_up")
    up = Halving(keep, send, y_first, ranks)
    token = down.step(send)
    grad_middle, attended_t, grad_mixed = middle_back(
        after(lengths, token), owns, others, mid, cotangent, gain_2, output_weight
    )
    token = grad_mixed

    groups = 2 if heads % 2 == 0 else 1
    each = heads // groups
    pieces, sides, rounds = [], [], []
    for g in range(groups):
        piece, slopes = attend_back(
            g * each, each, after(lengths, token), slope_rates, q, compressed, memory, memory_next, exact, lse, grad_mixed
        )
        pieces.append(piece)
        sides.append(slopes)
        order = x_first if g else y_first
        sources = [(normed_t, piece.reshape(3, tokens, each * HD), order)]
        if g == 0:
            sources.append((attended_t, mixed.reshape(tokens, width), order))
        final = g == groups - 1
        token = piece
        if final:
            part = lower(after(lengths, token), pieces, qkv)
            own, other = pair_over_head(part)
            token = part
        keep, send = weight_gradient(after(me_array, token), sources, each * HD, "grad_joint", sides if final else ())
        side = jnp.broadcast_to(sum(sides)[:, :1], (8, keep.shape[1])) if final else None
        rounds.append(Halving(keep, send, order, ranks, side))
        token = send
        if g == 0:
            token = up.step(token)
            token = down.step(token)
    early, late = rounds[0], rounds[-1]

    for r in (early, up):
        token = r.step(token)
    branch = leave(after(lengths, token), active, down_weight)
    branch, branch_other = pair_over_head(branch)
    token = down.step(late.step(branch))
    grad_inputs, outputs = None, None
    parts = 2 if streams % 2 == 0 else 1
    count = streams // parts
    for p in range(parts):
        grad_inputs = in_part(
            inputs_body, p * count, count, grad_inputs, after(lengths, token), [inputs, own, other, grad_middle], gain_1, mid, "inputs_back"
        )
        token = grad_inputs
        for r in (late, early, down) if p else (early, up):
            token = r.step(token)
    for p in range(parts):
        outputs = in_part(
            outputs_body, p * count, count, outputs, after(lengths, token), [mid, branch, branch_other], None, mid, "outputs"
        )
        token = outputs
        for r in (late, early):
            token = r.step(token)
    for r in (down, up, early, late):
        while r.total is None:
            token = r.step(token)

    share = each * HD
    columns = lambda r, c: r.total[:, c * share : (c + 1) * share]
    total_qkv = jnp.stack([jnp.concatenate([columns(r, c) for r in rounds], axis=1) for c in range(3)], axis=1)
    total_out = rounds[0].total[:, 3 * share :]
    total_up = up.total[:, : up_weight.shape[1]]
    total_conv = conv_share(up.total[:, up_weight.shape[1] :], conv_weight, ranks, model)

    portion = model // ranks
    mine = lambda a: lax.dynamic_slice_in_dim(a, me * portion, portion, 0).astype(F32)
    flat = total_qkv.reshape(portion, 3 * width)
    gains = jnp.stack([jnp.sum(flat * mine(qkv), axis=1), jnp.sum(total_up * mine(up_weight), axis=1)])
    head_count = lax.axis_size("head")
    for bit in range(bits_of(head_count)):
        gains = gains + lax.ppermute(gains, "head", flip_pairs(head_count, bit))
    gains = gains / jnp.stack([mine(gain_one), mine(gain_two)])

    return (
        outputs,
        grad_inputs,
        memory_next,
        compressed_next,
        total_qkv,
        total_out.T,
        total_up,
        down.total.T,
        gains[0],
        gains[1],
        rounds[-1].side[:heads, 0],
        total_conv,
    )


def solution(mesh):
    placed = (
        P("dp", None, None),
        P("dp", None, None),
        P("dp"),
        P("dp", None, None, "head"),
        P("dp", None, None, "head"),
        P(None, None, "head"),
        P("head", None),
        P(None, "head"),
        P("head", None),
        P(),
        P(),
        P("head"),
        P("head", None, None, None, None),
    )
    return jax.shard_map(
        per_device,
        mesh=mesh,
        in_specs=placed,
        out_specs=(
            P("dp", None, None),
            P("dp", None, None),
            P("dp", None, None, "head"),
            P("dp", None, None, "head"),
            P("dp", None, "head"),
            P("head", "dp"),
            P("dp", "head"),
            P("head", "dp"),
            P("dp"),
            P("dp"),
            P("head"),
            P("head", None, None, "dp", None),
        ),
        check_vma=False,
    )
```

```python
import functools
import math

import jax
import jax.numpy as jnp
from jax import lax
from jax.experimental import pallas as pl
from jax.experimental.pallas import tpu as pltpu
from jax.sharding import PartitionSpec as P

HD = 128
CE = 170
EPS = 1e-05
LOG2E = 1.0 / math.log(2.0)
HEAD_SCALE = 1.0 / math.sqrt(HD)
BASE2 = HEAD_SCALE * LOG2E
F32 = jnp.float32
BF16 = jnp.bfloat16
KEEP = BF16


def bits_of(count):
    return count.bit_length() - 1


def flip_pairs(count, bit):
    return [(i, i ^ (1 << bit)) for i in range(count)]


def call(body, grid, in_specs, out_specs, out_shape, scratch=(), prefetch=0, cover=False, name=None, aliases=None):
    return pl.pallas_call(
        body,
        grid_spec=pltpu.PrefetchScalarGridSpec(
            num_scalar_prefetch=prefetch,
            grid=grid,
            in_specs=in_specs,
            out_specs=out_specs,
            scratch_shapes=list(scratch),
        ),
        out_shape=out_shape,
        input_output_aliases=aliases or {},
        compiler_params=pltpu.CompilerParams(dimension_semantics=("arbitrary",) * len(grid)),
        cost_estimate=pl.CostEstimate(flops=10**13 if cover else 0, bytes_accessed=0, transcendentals=0),
        name=name,
    )


def whole(shape):
    zeros = (0,) * len(shape)
    return pl.BlockSpec(shape, lambda *_: zeros, pipeline_mode=pl.Buffered(1))


def per_stream(rows, n):
    return pl.BlockSpec((1, rows, n), lambda s, *_: (s, 0, 0))


def turned(rows, n):
    return pl.BlockSpec((n, rows), lambda s, *_: (0, s))


def like(streams, rows, n, kind):
    return jax.ShapeDtypeStruct((streams, rows, n), kind)


def dot(a, b):
    return jnp.dot(a, b, preferred_element_type=F32)


def dot_nt(a, b):
    return lax.dot_general(a, b, (((1,), (1,)), ((), ())), preferred_element_type=F32)


def dot_tn(a, b):
    return lax.dot_general(a, b, (((0,), (0,)), ((), ())), preferred_element_type=F32)


def statistics(v):
    centred = v - jnp.mean(v, axis=-1, keepdims=True)
    spread = jnp.mean(centred * centred, axis=-1, keepdims=True)
    return centred, lax.rsqrt(spread + EPS)


def by_rows(rows, step, body, together=8):
    def one(i, carry):
        for j in range(together):
            body(pl.multiple_of((i * together + j) * step, step))
        return carry

    lax.fori_loop(0, rows // (step * together), one, 0)


def row_ids(start, step):
    return start + lax.broadcasted_iota(jnp.int32, (step, 1), 0)


def project_body(len_ref, x_ref, gain_ref, w_ref, normed_t_ref, q_ref, kv_ref, normed_ref):
    rows = q_ref.shape[1]
    length = len_ref[pl.program_id(0)]

    def norm(r):
        centred, scale = statistics(x_ref[0, pl.ds(r, 16), :].astype(F32))
        normed_ref[pl.ds(r, 16), :] = (centred * scale * gain_ref[...]).astype(BF16)

    by_rows(rows, 16, norm)
    normed_t_ref[...] = normed_ref[...].T
    valid = row_ids(0, rows) < length
    normed = normed_ref[...]
    q_ref[0] = dot(normed, w_ref[0]).astype(BF16)
    for c in range(2):
        now = dot(normed, w_ref[c + 1])
        kv_ref[0, c] = jnp.where(valid, now, 0.0).astype(BF16)


def project(lengths, x, gain, w):
    streams, rows, model = x.shape
    width = w.shape[2]
    per = lambda *tail: pl.BlockSpec((1,) + tail, lambda s, *_: (s,) + (0,) * len(tail))
    return call(
        project_body,
        (streams,),
        [per(rows, model), whole((1, model)), whole(w.shape)],
        [pl.BlockSpec((model, rows), lambda s, *_: (0, s)), per(rows, width), per(2, rows, width)],
        [
            jax.ShapeDtypeStruct((model, streams * rows), BF16),
            jax.ShapeDtypeStruct((streams, rows, width), BF16),
            jax.ShapeDtypeStruct((streams, 2, rows, width), BF16),
        ],
        scratch=[pltpu.VMEM((rows, model), BF16)],
        prefetch=1,
        name="project",
    )(lengths, x, gain, w)


def position_columns(keys):
    centre = keys // 2
    lane = lax.broadcasted_iota(jnp.int32, (keys, HD), 1)
    place = lax.broadcasted_iota(jnp.int32, (keys, HD), 0) - centre
    fine = place & 7
    coarse = place - fine
    value = jnp.where(lane < 6, jnp.where((lane & 1) == 0, coarse, fine), jnp.where(lane == 6, 1, 0))
    return value.astype(F32).astype(BF16)


def slope_columns(slope, rows):
    exact = jnp.full((8, HD), slope, F32) * (1.0 / HEAD_SCALE)
    first = exact.astype(BF16).astype(F32)
    second = (exact - first).astype(BF16).astype(F32)
    third = exact - first - second
    lane = lax.broadcasted_iota(jnp.int32, (8, HD), 1)
    value = jnp.where(lane < 2, first, jnp.where(lane < 4, second, jnp.where(lane < 6, third, 0.0)))
    return jnp.broadcast_to(value[:1], (rows, HD)).astype(BF16)


def one_column(keys):
    lane = lax.broadcasted_iota(jnp.int32, (keys, HD), 1)
    return jnp.where(lane == 0, 1.0, 0.0).astype(BF16)


def diagonal_mask(block, start, length):
    row = lax.broadcasted_iota(jnp.int32, (block, block), 0)
    col = lax.broadcasted_iota(jnp.int32, (block, block), 1)
    return col <= jnp.minimum(row, length - 1 - start)


def pipelined(chains, front, rest):
    following = front(*chains[0])
    for n, chain in enumerate(chains):
        current = following
        if n + 1 < len(chains):
            following = front(*chains[n + 1])
        rest(*chain, *current)


def lanes_of(a):
    return slice(a * HD, (a + 1) * HD)


def attend_body(len_ref, slope_ref, q_ref, old_ref, mem_ref, now_ref, wo_ref, mix_ref, exact_ref, lse_ref, part_ref, kbuf, vbuf):
    s = pl.program_id(0)
    rows, heads = q_ref.shape[1], q_ref.shape[2] // HD
    old, mem = old_ref.shape[2], mem_ref.shape[2]
    past = old + mem
    keys = past + rows
    block = rows // 2
    length = len_ref[s]

    @pl.when(s == 0)
    def _():
        for a in range(heads):
            kbuf[a, :, HD:] = position_columns(keys)
            vbuf[a, :, HD:] = one_column(keys)

    for a in range(heads):
        for buf, c in ((kbuf, 0), (vbuf, 1)):
            buf[a, :old, :HD] = old_ref[0, c, :, lanes_of(a)]
            buf[a, old:past, :HD] = mem_ref[0, c, :, lanes_of(a)]
            buf[a, past:, :HD] = now_ref[0, c, :, lanes_of(a)]

    def front(a, i):
        side = slope_columns(slope_ref[a], block)
        wide = jnp.concatenate([q_ref[0, i * block : (i + 1) * block, lanes_of(a)], side], axis=1)
        return (dot_nt(wide, kbuf[a, : past + (i + 1) * block]),)

    def rest(a, i, scores):
        high = (i + 1) * block
        here = slice(i * block, high)
        allowed = diagonal_mask(block, i * block, length)
        last = jnp.where(allowed, scores[:, past + i * block :], -1e30)
        scores = jnp.concatenate([scores[:, : past + i * block], last], axis=1)
        top = jnp.max(scores, axis=1, keepdims=True)
        weights = jnp.exp2((scores - top) * BASE2).astype(BF16)
        both = dot(weights, vbuf[a, : past + high])
        total = both[:, HD : HD + 1]
        mixed = both[:, :HD] / total
        exact_ref[0, here, lanes_of(a)] = mixed
        mix_ref[0, here, lanes_of(a)] = mixed.astype(BF16)
        lse_ref[0, here, lanes_of(a)] = jnp.broadcast_to(top * BASE2 + jnp.log2(total), (block, HD))

    @pl.when(length > block)
    def _():
        pipelined([(a, i) for a in range(heads) for i in range(2)], front, rest)

    @pl.when(length <= block)
    def _():
        pipelined([(a, 0) for a in range(heads)], front, rest)
        exact_ref[0, block:, :] = jnp.zeros((rows - block, heads * HD), F32)
        mix_ref[0, block:, :] = jnp.zeros((rows - block, heads * HD), BF16)
        lse_ref[0, block:, :] = jnp.zeros((rows - block, heads * HD), F32)

    part_ref[0] = dot(mix_ref[0], wo_ref[...]).astype(BF16)


def attend(lengths, slopes, q, compressed, memory, now, wo):
    streams, rows, width = q.shape
    heads = width // HD
    model = wo.shape[1]
    keys = compressed.shape[2] + memory.shape[2] + rows
    cache = lambda a: pl.BlockSpec((1, 2, a.shape[2], width), lambda s, *_: (s, 0, 0, 0))
    return call(
        attend_body,
        (streams,),
        [per_stream(rows, width), cache(compressed), cache(memory), cache(now), whole(wo.shape)],
        [per_stream(rows, width), per_stream(rows, width), per_stream(rows, width), per_stream(rows, model)],
        [
            jax.ShapeDtypeStruct((streams, rows, width), BF16),
            jax.ShapeDtypeStruct((streams, rows, width), F32),
            jax.ShapeDtypeStruct((streams, rows, width), F32),
            jax.ShapeDtypeStruct((streams, rows, model), BF16),
        ],
        scratch=[pltpu.VMEM((heads, keys, 2 * HD), BF16), pltpu.VMEM((heads, keys, 2 * HD), BF16)],
        prefetch=2,
        name="attend",
    )(lengths, slopes, q, compressed, memory, now, wo)


def attend_back_body(first, len_ref, slope_ref, q_ref, old_ref, mem_ref, now_ref, exact_ref, lse_ref, grad_ref, out_ref, slope_out_ref, kbuf, vbuf):
    s = pl.program_id(0)
    rows, heads = q_ref.shape[1], q_ref.shape[2] // HD
    old, mem = old_ref.shape[2], mem_ref.shape[2]
    past = old + mem
    keys = past + rows
    block = rows // 2
    length = len_ref[s]

    @pl.when(s == 0)
    def _():
        for a in range(heads):
            kbuf[a, :, HD:] = position_columns(keys)
        slope_out_ref[...] = jnp.zeros_like(slope_out_ref)

    for a in range(heads):
        kbuf[a, :old, :HD] = old_ref[0, 0, :, lanes_of(a)]
        kbuf[a, old:past, :HD] = mem_ref[0, 0, :, lanes_of(a)]
        kbuf[a, past:, :HD] = now_ref[0, 0, :, lanes_of(a)]
        vbuf[a, :old] = old_ref[0, 1, :, lanes_of(a)]
        vbuf[a, old:past] = mem_ref[0, 1, :, lanes_of(a)]
        vbuf[a, past:] = now_ref[0, 1, :, lanes_of(a)]

    def here(i):
        return slice(i * block, (i + 1) * block)

    def front(a, i):
        side = slope_columns(slope_ref[first + a], block)
        wide = jnp.concatenate([q_ref[0, here(i), lanes_of(a)], side], axis=1)
        reach = past + (i + 1) * block
        return dot_nt(wide, kbuf[a, :reach]), dot_nt(grad_ref[0, here(i), lanes_of(a)], vbuf[a, :reach])

    def run(blocks):
        sums = {}

        def rest(a, i, scores, grad_probs):
            reach = past + (i + 1) * block
            q, grad = q_ref[0, here(i), lanes_of(a)], grad_ref[0, here(i), lanes_of(a)]
            exact = jnp.exp2(scores * BASE2 - lse_ref[0, here(i), a * HD : a * HD + 1])
            allowed = diagonal_mask(block, i * block, length)
            last = jnp.where(allowed, exact[:, reach - block :], 0.0)
            exact = jnp.concatenate([exact[:, : reach - block], last], axis=1)
            inner = jnp.sum(grad.astype(F32) * exact_ref[0, here(i), lanes_of(a)], axis=1, keepdims=True)
            grad_scores = (exact * (grad_probs - inner)).astype(BF16)
            wide = dot(grad_scores, kbuf[a, :reach])
            out_ref[0, 0, here(i), lanes_of(a)] = (wide[:, :HD] * HEAD_SCALE).astype(BF16)
            coarse, fine, total = (wide[:, HD + n : HD + n + 1] for n in (0, 1, 6))
            distance = (past + i * block - keys // 2 + lax.broadcasted_iota(jnp.int32, (block, 1), 0)).astype(F32)
            moment = jnp.sum(coarse + fine - distance * total, axis=0, keepdims=True)
            grad_keys = dot_tn(grad_scores[:, past:], q)
            grad_values = dot_tn(exact[:, past:].astype(BF16), grad)
            if i > 0:
                moment = moment + sums[a][0]
                done = sums[a][1].shape[0]
                join = lambda before, now: jnp.concatenate([before + now[:done], now[done:]], axis=0)
                grad_keys, grad_values = join(sums[a][1], grad_keys), join(sums[a][2], grad_values)
            sums[a] = moment, grad_keys, grad_values
            if i == blocks - 1:
                high = blocks * block
                out_ref[1, 0, :high, lanes_of(a)] = (grad_keys * HEAD_SCALE).astype(BF16)
                out_ref[2, 0, :high, lanes_of(a)] = grad_values.astype(BF16)
                slope_out_ref[first + a : first + a + 1, :] += jnp.broadcast_to(moment, (1, HD))

        pipelined([(a, i) for a in range(heads) for i in range(blocks)], front, rest)

    @pl.when(length > block)
    def _():
        run(2)

    @pl.when(length <= block)
    def _():
        run(1)
        for c in range(3):
            out_ref[c, 0, block:, :] = jnp.zeros((rows - block, heads * HD), BF16)


def attend_back(first, heads, lengths, slopes, q, compressed, memory, now, exact, lse, grad):
    streams, rows, width = q.shape
    keys = compressed.shape[2] + memory.shape[2] + rows
    group = first // heads
    cache = lambda a: pl.BlockSpec((1, 2, a.shape[2], heads * HD), lambda s, *_: (s, 0, 0, group))
    some = pl.BlockSpec((1, rows, heads * HD), lambda s, *_: (s, 0, group))
    return call(
        functools.partial(attend_back_body, first),
        (streams,),
        [some, cache(compressed), cache(memory), cache(now), some, some, some],
        [pl.BlockSpec((3, 1, rows, heads * HD), lambda s, *_: (0, s, 0, 0)), pl.BlockSpec((8, HD), lambda *_: (0, 0))],
        [jax.ShapeDtypeStruct((3, streams, rows, heads * HD), BF16), jax.ShapeDtypeStruct((8, HD), F32)],
        scratch=[pltpu.VMEM((heads, keys, 2 * HD), BF16), pltpu.VMEM((heads, keys, HD), BF16)],
        prefetch=2,
        cover=True,
        name="attend_back",
    )(lengths, slopes, q, compressed, memory, now, exact, lse, grad)


GELU_K = math.sqrt(2.0 / math.pi)
GELU_C = 0.044715


def gate_of(v):
    square = v * v
    rate = -2.0 * GELU_K * LOG2E
    return 1.0 / (1.0 + jnp.exp2(v * (rate + (rate * GELU_C) * square))), square


def gelu_slope(v):
    gate, square = gate_of(v)
    lean = v * (2.0 * GELU_K + (6.0 * GELU_K * GELU_C) * square)
    return gate * (1.0 + lean * (1.0 - gate))


def rise_body(len_ref, x_ref, own_ref, other_ref, gain_ref, up_ref, mid_ref, normed_t_ref, active_ref, before_ref, normed):
    rows = x_ref.shape[1]
    hidden_width = up_ref.shape[1]
    length = len_ref[pl.program_id(0)]

    def norm(r):
        here = pl.ds(r, 16)
        valid = (row_ids(r, 16) < length).astype(F32)
        attended = own_ref[0, here, :].astype(F32) + other_ref[0, here, :].astype(F32)
        middle = x_ref[0, here, :].astype(F32) + attended * valid
        mid_ref[0, here, :] = middle.astype(BF16)
        centred, scale = statistics(middle)
        normed[here, :] = (centred * scale * gain_ref[...]).astype(BF16)

    by_rows(rows, 16, norm)
    normed_t_ref[...] = normed[...].T
    chunk = min(512, hidden_width)
    columns = [slice(f, f + chunk) for f in range(0, hidden_width, chunk)]

    def front(cols):
        return (dot(normed[...], up_ref[:, cols]),)

    def rest(cols, v):
        active_ref[0, :, cols] = (v * gate_of(v)[0]).astype(BF16)
        before_ref[0, :, cols] = v.astype(BF16)

    pipelined([(cols,) for cols in columns], front, rest)


def rise(lengths, x, own, other, gain, up):
    streams, rows, model = x.shape
    hidden = up.shape[1]
    tokens = streams * rows
    return call(
        rise_body,
        (streams,),
        [per_stream(rows, model)] * 3 + [whole((1, model)), whole(up.shape)],
        [per_stream(rows, model), turned(rows, model), per_stream(rows, hidden), per_stream(rows, hidden)],
        [
            like(streams, rows, model, BF16),
            jax.ShapeDtypeStruct((model, tokens), BF16),
            like(streams, rows, hidden, BF16),
            like(streams, rows, hidden, BF16),
        ],
        scratch=[pltpu.VMEM((rows, model), BF16)],
        prefetch=1,
        name="rise",
    )(lengths, x, own, other, gain, up)


def fall_body(len_ref, cot_ref, before_ref, up_ref, down_ref, hidden_ref, *back_refs):
    rows = cot_ref.shape[1]
    hidden_width = up_ref.shape[1]
    valid = row_ids(0, rows) < len_ref[pl.program_id(0)]
    branch = jnp.where(valid, cot_ref[0].astype(F32), 0.0).astype(BF16)
    chunk = min(512, hidden_width)
    back = []

    def front(cols):
        return (dot_nt(branch, down_ref[cols, :]),)

    def rest(cols, grad_active):
        grad_hidden = (grad_active * gelu_slope(before_ref[0, :, cols].astype(F32))).astype(BF16)
        hidden_ref[0, :, cols] = grad_hidden
        back.append(dot_nt(grad_hidden, up_ref[:, cols]))

    pipelined([(slice(f, f + chunk),) for f in range(0, hidden_width, chunk)], front, rest)
    total = sum(back[1:], back[0]).astype(BF16)
    part = total.shape[1] // len(back_refs)
    for n, back_ref in enumerate(back_refs):
        back_ref[0] = total[:, n * part : (n + 1) * part]


PIECES = 4


def fall(lengths, cot, slope, up, down):
    streams, rows, model = cot.shape
    hidden = up.shape[1]
    tokens = streams * rows
    return call(
        fall_body,
        (streams,),
        [per_stream(rows, model), per_stream(rows, hidden), whole(up.shape), whole(down.shape)],
        [per_stream(rows, hidden)] + [per_stream(rows, model // PIECES)] * PIECES,
        [like(streams, rows, hidden, BF16)] + [like(streams, rows, model // PIECES, BF16)] * PIECES,
        prefetch=1,
        name="fall",
    )(lengths, cot, slope, up, down)


def leave_body(_, active_ref, down_ref, part_ref):
    part_ref[0] = dot(active_ref[0], down_ref[...]).astype(BF16)


def leave(lengths, active, down):
    streams, rows, hidden = active.shape
    model = down.shape[1]
    return call(
        leave_body,
        (streams,),
        [per_stream(rows, hidden), whole(down.shape)],
        per_stream(rows, model),
        like(streams, rows, model, BF16),
        prefetch=1,
        cover=True,
        name="leave",
    )(lengths, active, down)


def outputs_body(start, len_ref, mid_ref, own_ref, other_ref, out_ref):
    rows = mid_ref.shape[1]
    length = len_ref[start + pl.program_id(0)]

    def one(r):
        here = pl.ds(r, 16)
        valid = (row_ids(r, 16) < length).astype(F32)
        branch = own_ref[0, here, :].astype(F32) + other_ref[0, here, :].astype(F32)
        out_ref[0, here, :] = mid_ref[0, here, :].astype(F32) + valid * branch

    by_rows(rows, 16, one, 4)


def in_part(body, first, count, into, lengths, args, gain, like_this, name):
    rows, model = like_this.shape[1:]
    per = pl.BlockSpec((1, rows, model), lambda s, *_: (s + first, 0, 0))
    extra = [] if gain is None else [whole(gain.shape)]
    held = [] if into is None else [into]

    def inner(len_ref, *refs):
        body(first, len_ref, *refs[: len(args) + len(extra)], refs[-1])

    return call(
        inner,
        (count,),
        [per] * len(args) + extra + [pl.BlockSpec(memory_space=pl.ANY)] * len(held),
        per,
        jax.ShapeDtypeStruct(like_this.shape, F32),
        prefetch=1,
        cover=first > 0 or gain is None,
        aliases={1 + len(args) + len(extra): 0} if held else {},
        name=name,
    )(lengths, *args, *([] if gain is None else [gain]), *held)


def chunk_at(place, order, me):
    apart = 0
    for i, bit in enumerate(order):
        apart |= ((place >> (len(order) - 1 - i)) & 1) << bit
    return apart ^ me


def send_order(source, order, me, first, count):
    deep = source.shape[0] // (1 << len(order))
    lines = []
    for p in range(first, first + count):
        lines.append(source[pl.ds(pl.multiple_of(chunk_at(p, order, me) * deep, deep), deep), :])
    return jnp.concatenate(lines, axis=0)


def weight_body(spans, extra, order, me_ref, *refs):
    products = sum(span[2] for span in spans)
    xts, ys = list(refs[:products]), refs[products : products + len(spans)]
    sides, (keep_ref, send_ref) = refs[products + len(spans) : -2], refs[-2:]
    me = me_ref[0]
    j = pl.program_id(0)
    places = 1 << len(order)
    half = keep_ref.shape[0]
    for y, (start, stop, product) in zip(ys, spans):
        xt = xts.pop(0) if product else None

        @pl.when((j >= start) & (j < stop))
        def _(xt=xt, y=y):
            for n, out in enumerate((keep_ref, send_ref)):
                rows = send_order(y if xt is None else xt, order, me, n * places // 2, places // 2)
                if xt is not None:
                    rows = dot(rows, y[...] if len(y.shape) == 2 else y[0])
                out[:half, :] = rows.astype(out.dtype)

    if extra:
        total = sum(side[...] for side in sides)
        first = total.astype(BF16).astype(F32)
        both = jnp.concatenate([first, total - first], axis=0).astype(BF16)
        send_ref[half:, :] = jnp.concatenate([both] * (send_ref.shape[1] // HD), axis=1)


def weight_gradient(me, order, sources, step, name, sides=()):
    xts = [xt for xt, _ in sources if xt is not None]
    model, tokens = xts[0].shape
    spans, specs, at = [], [], 0
    for xt, y in sources:
        n = y.shape[-1] // step
        blocks = n * (y.shape[0] if y.ndim == 3 else 1)
        spans.append((at, at + blocks, xt is not None))
        if y.ndim == 3:
            pick = lambda j, *_, at=at, n=n, blocks=blocks: (jnp.clip(j - at, 0, blocks - 1) // n, 0, jnp.clip(j - at, 0, blocks - 1) % n)
            specs.append(pl.BlockSpec((1, y.shape[1], step), pick))
        else:
            specs.append(pl.BlockSpec((y.shape[0], step), lambda j, *_, at=at, blocks=blocks: (0, jnp.clip(j - at, 0, blocks - 1))))
        at += blocks
    columns = at * step
    extra = 16 if sides else 0
    return call(
        functools.partial(weight_body, spans, extra, order),
        (at,),
        [whole(xt.shape) for xt in xts] + specs + [whole(side.shape) for side in sides],
        [pl.BlockSpec((model // 2, step), lambda j, *_: (0, j)), pl.BlockSpec((model // 2 + extra, step), lambda j, *_: (0, j))],
        [jax.ShapeDtypeStruct((model // 2, columns), KEEP), jax.ShapeDtypeStruct((model // 2 + extra, columns), BF16)],
        prefetch=1,
        name=name,
    )(me, *xts, *[y for _, y in sources], *sides)


class Halving:
    def __init__(self, keep, send, order, count, side=None):
        self.order, self.count, self.stage, self.total = order, count, 0, None
        self.keep, self.side = keep, side
        self.send(send)

    def send(self, what):
        self.sent = what
        self.came = lax.ppermute(what, "dp", flip_pairs(self.count, self.order[self.stage]))


def advance_body(items, *refs):
    refs = list(refs)
    ins = [[refs.pop(0) for _ in range(3 if side else 2)] for _, side in items]
    for (final, side), (keep, came, *before) in zip(items, ins):
        high = keep.shape[0]
        half = high // 2
        if final:
            refs.pop(0)[...] = keep[...].astype(F32) + came[:high, :].astype(F32)
        else:
            stay, go = refs.pop(0), refs.pop(0)
            stay[...] = (keep[:half, :].astype(F32) + came[:half, :].astype(F32)).astype(stay.dtype)
            go[:half, :] = (keep[half:, :].astype(F32) + came[half:high, :].astype(F32)).astype(BF16)
        if side:
            both = came[high:, :].astype(F32)
            total = before[0][...] + (both[:8] + both[8:])
            refs.pop(0)[...] = total
            if not final:
                first = total.astype(BF16).astype(F32)
                go[half:, :] = jnp.concatenate([first, total - first], axis=0).astype(BF16)


def advance(rounds, token):
    rounds = [r for r in rounds if r.total is None]
    if not rounds:
        return token
    blocks = lambda a: pl.BlockSpec((a.shape[0], a.shape[1] // 2), lambda j: (0, j))
    items, args, outs = [], [], []
    for r in rounds:
        final, side = r.stage + 1 == len(r.order), r.side is not None
        items.append((final, side))
        args += [r.keep, after(r.came, token)] + ([r.side] if side else [])
        high, columns = r.keep.shape
        if final:
            outs.append(jax.ShapeDtypeStruct((high, columns), F32))
        else:
            outs.append(jax.ShapeDtypeStruct((high // 2, columns), KEEP))
            outs.append(jax.ShapeDtypeStruct((high // 2 + (16 if side else 0), columns), BF16))
        if side:
            outs.append(jax.ShapeDtypeStruct(r.side.shape, F32))
    got = list(
        call(
            functools.partial(advance_body, items),
            (2,),
            [blocks(a) for a in args],
            [blocks(a) for a in outs],
            outs,
            name="advance",
        )(*args)
    )
    token = got[0]
    for r, (final, side) in zip(rounds, items):
        r.stage += 1
        if final:
            r.total = got.pop(0)
        else:
            r.keep = got.pop(0)
            send = got.pop(0)
        if side:
            r.side = got.pop(0)
        if not final:
            r.send(send)
    return token


def after(value, token):
    return lax.optimization_barrier((value, token))[0]


def conv_share(total, like, ranks, model):
    share = like.shape[3] // ranks
    pieces = math.prod(like.shape[:3])
    groups = -(-pieces * HD // model)
    total = total[:, : groups * HD].reshape(model // HD, share, groups, HD).transpose(2, 0, 1, 3)
    return total.reshape(groups * (model // HD), share, HD)[:pieces].reshape(like.shape[:3] + (share, HD))


def pair_over_head(part):
    count = lax.axis_size("head")
    for bit in range(bits_of(count)):
        came = lax.ppermute(part, "head", flip_pairs(count, bit))
        if bit == bits_of(count) - 1:
            return part, came
        part = (part.astype(F32) + came.astype(F32)).astype(part.dtype)
    return part, jnp.zeros_like(part)


def middle_body(len_ref, *refs):
    owns, others = refs[:PIECES], refs[PIECES : 2 * PIECES]
    mid_ref, cot_ref, gain_ref, wo_ref, grad_ref, turned_ref, mixed_ref, attended = refs[2 * PIECES :]
    rows = mid_ref.shape[1]
    s = pl.program_id(0)
    length = len_ref[s]

    def one(r):
        here = pl.ds(r, 16)
        valid = (row_ids(r, 16) < length).astype(F32)
        middle = mid_ref[0, here, :].astype(F32)
        sums = [own[0, here, :].astype(F32) + other[0, here, :].astype(F32) for own, other in zip(owns, others)]
        grad = jnp.concatenate(sums, axis=1)
        centred, scale = statistics(middle)
        hat = centred * scale
        e = grad * gain_ref[...]
        lean = jnp.mean(e * hat, axis=-1, keepdims=True)
        total = cot_ref[0, here, :].astype(F32) + scale * (e - jnp.mean(e, axis=-1, keepdims=True) - hat * lean)
        grad_ref[0, here, :] = total.astype(BF16)
        attended[here, :] = (total * valid).astype(BF16)

    by_rows(rows, 16, one)
    turned_ref[...] = attended[...].T
    mixed_ref[0] = dot_nt(attended[...], wo_ref[...]).astype(BF16)


def middle_back(lengths, owns, others, mid, cot, gain, wo):
    streams, rows, model = mid.shape
    width = wo.shape[0]
    return call(
        middle_body,
        (streams,),
        [per_stream(rows, model // PIECES)] * (2 * PIECES) + [per_stream(rows, model)] * 2 + [whole((1, model)), whole(wo.shape)],
        [per_stream(rows, model), turned(rows, model), per_stream(rows, width)],
        [
            jax.ShapeDtypeStruct(mid.shape, BF16),
            jax.ShapeDtypeStruct((model, streams * rows), BF16),
            like(streams, rows, width, BF16),
        ],
        scratch=[pltpu.VMEM((rows, model), BF16)],
        prefetch=1,
        name="middle_back",
    )(lengths, *owns, *others, mid, cot, gain, wo)


def lower_body(_, *refs):
    pieces, (w_ref, part_ref) = refs[:-2], refs[-2:]
    total = None
    for c in range(3):
        more = dot_nt(jnp.concatenate([piece[c, 0] for piece in pieces], axis=1), w_ref[c])
        total = more if total is None else total + more
    part_ref[0] = total.astype(BF16)


def lower(lengths, pieces, w):
    model = w.shape[1]
    _, streams, rows, _ = pieces[0].shape
    joint = lambda a: pl.BlockSpec((3, 1, rows, a.shape[3]), lambda s, *_: (0, s, 0, 0))
    return call(
        lower_body,
        (streams,),
        [joint(a) for a in pieces] + [whole(w.shape)],
        per_stream(rows, model),
        like(streams, rows, model, BF16),
        prefetch=1,
        name="lower",
    )(lengths, *pieces, w)


def inputs_body(_, __, x_ref, own_ref, other_ref, grad_ref, gain_ref, out_ref):
    rows = x_ref.shape[1]

    def one(r):
        here = pl.ds(r, 16)
        centred, scale = statistics(x_ref[0, here, :].astype(F32))
        hat = centred * scale
        e = (own_ref[0, here, :].astype(F32) + other_ref[0, here, :].astype(F32)) * gain_ref[...]
        lean = jnp.mean(e * hat, axis=-1, keepdims=True)
        out_ref[0, here, :] = grad_ref[0, here, :].astype(F32) + scale * (e - jnp.mean(e, axis=-1, keepdims=True) - hat * lean)

    by_rows(rows, 16, one)


SLOTS = 256


def rebuild_body(len_ref, q_ref, mem_ref, old_ref, conv_ref, cot_ref, next_ref, rows_ref, branch_t_ref, wide, grad_ref):
    s = pl.program_id(0)
    rows, heads = q_ref.shape[1], q_ref.shape[2] // HD
    slots = mem_ref.shape[2]
    made = slots // 3
    valid = row_ids(0, rows) < len_ref[s]
    row = lax.broadcasted_iota(jnp.int32, (slots, HD), 0)

    @pl.when(s == 0)
    def _():
        grad_ref[...] = jnp.zeros_like(grad_ref)
        wide[...] = jnp.zeros_like(wide)

    def front(a):
        windows, packed = [], []
        for c in range(2):
            wide[a, c, :slots] = mem_ref[0, c, :, lanes_of(a)].astype(F32)
            taps = [wide[a, c, pl.ds(t, SLOTS, stride=3), :].astype(BF16) for t in range(3)]
            windows.append(jnp.concatenate(taps, axis=1))
            squeezed = dot(windows[c], conv_ref[a, c].reshape(3 * HD, HD))
            packed.append(squeezed.astype(BF16))
            tail = jnp.concatenate([squeezed, jnp.zeros((slots - SLOTS, HD), F32)], axis=0)
            kept = pltpu.roll(old_ref[0, c, :, lanes_of(a)].astype(F32), slots - made, 0)
            tail = pltpu.roll(tail, slots - made, 0)
            next_ref[0, c, :, lanes_of(a)] = jnp.where(row < slots - made, kept, tail).astype(BF16)
        q = q_ref[0, :, lanes_of(a)]
        return windows, packed, dot_nt(q, mem_ref[0, 0, :, lanes_of(a)]), dot_nt(q, packed[0])

    def soft(scores, count):
        start = scores.shape[1] - HD
        lane = start + lax.broadcasted_iota(jnp.int32, (rows, HD), 1)
        last = jnp.where(lane < count, scores[:, start:], -1e30)
        scores = jnp.concatenate([scores[:, :start], last], axis=1)
        weights = jnp.exp2((scores - jnp.max(scores, axis=1, keepdims=True)) * BASE2)
        return weights, 1.0 / jnp.sum(weights, axis=1, keepdims=True)

    def rest(a, windows, packed, scores, few_scores):
        q = q_ref[0, :, lanes_of(a)]
        weights, share = soft(few_scores, made)
        probs = weights * share
        low = probs.astype(BF16)
        approach = dot(low, packed[1])
        weights, share = soft(scores, 3 * made)
        target = dot(weights.astype(BF16), mem_ref[0, 1, :, lanes_of(a)]) * share
        grad = jnp.where(valid, (approach - target) * (2.0 / rows), 0.0).astype(BF16)
        grad_probs = dot_nt(grad, packed[1])
        inner = jnp.sum(probs * grad_probs, axis=1, keepdims=True)
        grad_scores = (probs * (grad_probs - inner) * HEAD_SCALE).astype(BF16)
        back = [dot_tn(grad_scores, q), dot_tn(low, grad)]
        for c in range(2):
            grad_ref[a, c] += dot_tn(windows[c], back[c].astype(BF16)).reshape(3, HD, HD)

    pipelined([(a,) for a in range(heads)], front, rest)
    branch_t_ref[...] = jnp.where(valid, cot_ref[0], jnp.zeros_like(cot_ref[0])).T

    @pl.when(s == pl.num_programs(0) - 1)
    def _():
        ranks, deep, _ = rows_ref.shape
        share = HD // ranks
        rows_ref[...] = jnp.zeros_like(rows_ref)
        for a in range(heads):
            for n in range(6):
                piece = 6 * a + n
                at, group = piece % (deep // share) * share, piece // (deep // share)
                rows_ref[:, at : at + share, group * HD : (group + 1) * HD] = grad_ref[a, n // 3, n % 3].reshape(ranks, share, HD)


def rebuild(lengths, q, memory, compressed, conv, cot, ranks, columns):
    model = cot.shape[2]
    streams, rows, width = q.shape
    heads = width // HD
    slots = memory.shape[2]
    cache = pl.BlockSpec((1, 2, slots, width), lambda s, *_: (s, 0, 0, 0))
    return call(
        rebuild_body,
        (streams,),
        [per_stream(rows, width), cache, cache, whole(conv.shape), per_stream(rows, model)],
        [cache, pl.BlockSpec((ranks, model // ranks, columns), lambda *_: (0, 0, 0)), turned(rows, model)],
        [
            jax.ShapeDtypeStruct(compressed.shape, BF16),
            jax.ShapeDtypeStruct((ranks, model // ranks, columns), F32),
            jax.ShapeDtypeStruct((model, streams * rows), BF16),
        ],
        scratch=[pltpu.VMEM((heads, 2, 3 * SLOTS, HD), F32), pltpu.VMEM(conv.shape, F32)],
        prefetch=1,
        cover=True,
        name="rebuild",
    )(lengths, q, memory, compressed, conv, cot)


def per_device(
    inputs,
    cotangent,
    lengths,
    memory,
    compressed,
    query_key_value_weight,
    output_weight,
    up_weight,
    down_weight,
    gain_one,
    gain_two,
    slope_rates,
    conv_weight,
):
    streams, rows, model = inputs.shape
    tokens = streams * rows
    heads = slope_rates.shape[0]
    width = heads * HD
    ranks = lax.axis_size("dp")
    rank_bits = bits_of(ranks)
    me = lax.axis_index("dp").astype(jnp.int32)
    me_array = me.reshape(1)
    later = tuple(range(2, rank_bits))
    x_first, x_then_z, y_then_z = (0, 1) + later, (0,) + later + (1,), (1,) + later + (0,)
    y_then_mixed = (1, 2, 0) + later[1:]
    gain_1, gain_2 = gain_one.reshape(1, model), gain_two.reshape(1, model)
    qkv = query_key_value_weight.transpose(1, 0, 2)

    normed_t, q, memory_next = project(lengths, inputs, gain_1, qkv)
    mixed, exact, lse, part = attend(lengths, slope_rates, q, compressed, memory, memory_next, output_weight)
    own, other = pair_over_head(part)
    step = min(512, up_weight.shape[1])
    compressed_next, conv, branch_t = rebuild(after(lengths, part), q, memory, compressed, conv_weight, cotangent, ranks, step)
    conv = conv.reshape(model, step)
    mid, normed_two_t, active, before = rise(after(lengths, conv), inputs, own, other, gain_2, up_weight)
    sources = [(branch_t, active.reshape(tokens, -1)), (None, conv)]
    keep, send = weight_gradient(me_array, x_then_z, sources, step, "grad_down")
    down = Halving(keep, send, x_then_z, ranks)
    grad_hidden, *backs = fall(after(lengths, send), cotangent, before, up_weight, down_weight)
    owns, others = zip(*[pair_over_head(back) for back in backs])
    keep, send = weight_gradient(me_array, y_then_z, [(normed_two_t, grad_hidden.reshape(tokens, -1))], step, "grad_up")
    up = Halving(keep, send, y_then_z, ranks)
    grad_middle, attended_t, grad_mixed = middle_back(
        after(lengths, send), owns, others, mid, cotangent, gain_2, output_weight
    )
    token = advance([down], grad_mixed)

    groups = 2 if heads % 2 == 0 else 1
    each = heads // groups
    pieces, sides, rounds = [], [], []
    for g in range(groups):
        piece, slopes = attend_back(
            g * each, each, after(lengths, token), slope_rates, q, compressed, memory, memory_next, exact, lse, grad_mixed
        )
        pieces.append(piece)
        sides.append(slopes)
        order = x_first if g else y_then_mixed
        sources = [(normed_t, piece.reshape(3, tokens, each * HD))]
        if g == 0:
            sources.append((attended_t, mixed.reshape(tokens, width)))
        final = g == groups - 1
        token = piece
        if final:
            part = lower(after(lengths, token), pieces, qkv)
            own, other = pair_over_head(part)
            token = part
        keep, send = weight_gradient(after(me_array, token), order, sources, each * HD, "grad_joint", sides if final else ())
        side = jnp.broadcast_to(sum(sides)[:, :1], (8, keep.shape[1])) if final else None
        rounds.append(Halving(keep, send, order, ranks, side))
        token = advance([up, down], send) if g == 0 else send
    early, late = rounds[0], rounds[-1]
    both = rounds[::-1]

    token = advance([early, up, down] if groups > 1 else [up, down], token)
    branch = leave(after(lengths, token), active, down_weight)
    token = advance([late, down], branch)
    branch, branch_other = pair_over_head(after(branch, token))
    grad_inputs, outputs = None, None
    parts = 2 if streams % 2 == 0 else 1
    count = streams // parts
    for p in range(parts):
        grad_inputs = in_part(
            inputs_body, p * count, count, grad_inputs, after(lengths, token), [inputs, own, other, grad_middle], gain_1, mid, "inputs_back"
        )
        token = advance(both + [down if p else up], grad_inputs)
    for p in range(parts):
        if p == parts - 1:
            while any(r.total is None for r in rounds + [up, down]):
                token = advance(both + [up, down], token)
        outputs = in_part(
            outputs_body, p * count, count, outputs, after(lengths, token), [mid, branch, branch_other], None, mid, "outputs"
        )
        token = outputs

    share = each * HD
    columns = lambda r, c: r.total[:, c * share : (c + 1) * share]
    total_qkv = jnp.stack([jnp.concatenate([columns(r, c) for r in rounds], axis=1) for c in range(3)], axis=1)
    total_out = rounds[0].total[:, 3 * share :]
    down_last = after(down.total, late.total)
    total_down = down_last[:, : up_weight.shape[1]]
    total_conv = conv_share(down_last[:, up_weight.shape[1] :], conv_weight, ranks, model)

    portion = model // ranks
    mine = lambda a: lax.dynamic_slice_in_dim(a, me * portion, portion, 0).astype(F32)
    ahead = jnp.sum(total_qkv * mine(query_key_value_weight), axis=(1, 2))
    gains = jnp.stack([ahead, jnp.sum(up.total * mine(up_weight), axis=1)])
    head_count = lax.axis_size("head")
    for bit in range(bits_of(head_count)):
        gains = gains + lax.ppermute(gains, "head", flip_pairs(head_count, bit))
    gains = gains / jnp.stack([mine(gain_one), mine(gain_two)])

    return (
        outputs,
        grad_inputs,
        memory_next,
        compressed_next,
        total_qkv,
        total_out.T,
        up.total,
        total_down.T,
        gains[0],
        gains[1],
        rounds[-1].side[:heads, 0],
        total_conv,
    )


def solution(mesh):
    placed = (
        P("dp", None, None),
        P("dp", None, None),
        P("dp"),
        P("dp", None, None, "head"),
        P("dp", None, None, "head"),
        P(None, None, "head"),
        P("head", None),
        P(None, "head"),
        P("head", None),
        P(),
        P(),
        P("head"),
        P("head", None, None, None, None),
    )
    return jax.shard_map(
        per_device,
        mesh=mesh,
        in_specs=placed,
        out_specs=(
            P("dp", None, None),
            P("dp", None, None),
            P("dp", None, None, "head"),
            P("dp", None, None, "head"),
            P("dp", None, "head"),
            P("head", "dp"),
            P("dp", "head"),
            P("head", "dp"),
            P("dp"),
            P("dp"),
            P("head"),
            P("head", None, None, "dp", None),
        ),
        check_vma=False,
    )
```

```python
import functools
import math

import jax
import jax.numpy as jnp
from jax import lax
from jax.experimental import pallas as pl
from jax.experimental.pallas import tpu as pltpu
from jax.sharding import PartitionSpec as P

HD = 128
CE = 170
EPS = 1e-05
LOG2E = 1.0 / math.log(2.0)
HEAD_SCALE = 1.0 / math.sqrt(HD)
BASE2 = HEAD_SCALE * LOG2E
F32 = jnp.float32
BF16 = jnp.bfloat16
KEEP = BF16
VMEM_LIMIT = 67043328


def bits_of(count):
    return count.bit_length() - 1


def flip_pairs(count, bit):
    return [(i, i ^ (1 << bit)) for i in range(count)]


def call(body, grid, in_specs, out_specs, out_shape, scratch=(), prefetch=0, cover=False, name=None, aliases=None):
    return pl.pallas_call(
        body,
        grid_spec=pltpu.PrefetchScalarGridSpec(
            num_scalar_prefetch=prefetch,
            grid=grid,
            in_specs=in_specs,
            out_specs=out_specs,
            scratch_shapes=list(scratch),
        ),
        out_shape=out_shape,
        input_output_aliases=aliases or {},
        compiler_params=pltpu.CompilerParams(dimension_semantics=("arbitrary",) * len(grid), vmem_limit_bytes=VMEM_LIMIT),
        cost_estimate=pl.CostEstimate(flops=10**13 if cover else 0, bytes_accessed=0, transcendentals=0),
        name=name,
    )


def whole(shape):
    zeros = (0,) * len(shape)
    return pl.BlockSpec(shape, lambda *_: zeros, pipeline_mode=pl.Buffered(1))


def per_stream(rows, n):
    return pl.BlockSpec((1, rows, n), lambda s, *_: (s, 0, 0))


def turned(rows, n):
    return pl.BlockSpec((n, rows), lambda s, *_: (0, s))


def like(streams, rows, n, kind):
    return jax.ShapeDtypeStruct((streams, rows, n), kind)


def dot(a, b):
    return jnp.dot(a, b, preferred_element_type=F32)


def dot_nt(a, b):
    return lax.dot_general(a, b, (((1,), (1,)), ((), ())), preferred_element_type=F32)


def dot_tn(a, b):
    return lax.dot_general(a, b, (((0,), (0,)), ((), ())), preferred_element_type=F32)


def statistics(v):
    centred = v - jnp.mean(v, axis=-1, keepdims=True)
    spread = jnp.mean(centred * centred, axis=-1, keepdims=True)
    return centred, lax.rsqrt(spread + EPS)


def by_rows(rows, step, body, together=8):
    def one(i, carry):
        for j in range(together):
            body(pl.multiple_of((i * together + j) * step, step))
        return carry

    lax.fori_loop(0, rows // (step * together), one, 0)


def row_ids(start, step):
    return start + lax.broadcasted_iota(jnp.int32, (step, 1), 0)


def project_body(len_ref, x_ref, gain_ref, w_ref, normed_t_ref, q_ref, kv_ref, normed_ref):
    rows = q_ref.shape[1]
    length = len_ref[pl.program_id(0)]

    def norm(r):
        centred, scale = statistics(x_ref[0, pl.ds(r, 16), :].astype(F32))
        normed_ref[pl.ds(r, 16), :] = (centred * scale * gain_ref[...]).astype(BF16)

    by_rows(rows, 16, norm)
    normed_t_ref[...] = normed_ref[...].T
    valid = row_ids(0, rows) < length
    normed = normed_ref[...]
    q_ref[0] = dot(normed, w_ref[0]).astype(BF16)
    for c in range(2):
        now = dot(normed, w_ref[c + 1])
        kv_ref[0, c] = jnp.where(valid, now, 0.0).astype(BF16)


def project(lengths, x, gain, w):
    streams, rows, model = x.shape
    width = w.shape[2]
    per = lambda *tail: pl.BlockSpec((1,) + tail, lambda s, *_: (s,) + (0,) * len(tail))
    return call(
        project_body,
        (streams,),
        [per(rows, model), whole((1, model)), whole(w.shape)],
        [pl.BlockSpec((model, rows), lambda s, *_: (0, s)), per(rows, width), per(2, rows, width)],
        [
            jax.ShapeDtypeStruct((model, streams * rows), BF16),
            jax.ShapeDtypeStruct((streams, rows, width), BF16),
            jax.ShapeDtypeStruct((streams, 2, rows, width), BF16),
        ],
        scratch=[pltpu.VMEM((rows, model), BF16)],
        prefetch=1,
        name="project",
    )(lengths, x, gain, w)


def position_columns(keys):
    centre = keys // 2
    lane = lax.broadcasted_iota(jnp.int32, (keys, HD), 1)
    place = lax.broadcasted_iota(jnp.int32, (keys, HD), 0) - centre
    fine = place & 7
    coarse = place - fine
    value = jnp.where(lane < 6, jnp.where((lane & 1) == 0, coarse, fine), jnp.where(lane == 6, 1, 0))
    return value.astype(F32).astype(BF16)


def slope_columns(slope, rows):
    exact = jnp.full((8, HD), slope, F32) * (1.0 / HEAD_SCALE)
    first = exact.astype(BF16).astype(F32)
    second = (exact - first).astype(BF16).astype(F32)
    third = exact - first - second
    lane = lax.broadcasted_iota(jnp.int32, (8, HD), 1)
    value = jnp.where(lane < 2, first, jnp.where(lane < 4, second, jnp.where(lane < 6, third, 0.0)))
    return jnp.broadcast_to(value[:1], (rows, HD)).astype(BF16)


def one_column(keys):
    lane = lax.broadcasted_iota(jnp.int32, (keys, HD), 1)
    return jnp.where(lane == 0, 1.0, 0.0).astype(BF16)


def diagonal_mask(block, start, length):
    row = lax.broadcasted_iota(jnp.int32, (block, block), 0)
    col = lax.broadcasted_iota(jnp.int32, (block, block), 1)
    return col <= jnp.minimum(row, length - 1 - start)


def pipelined(chains, front, rest):
    following = front(*chains[0])
    for n, chain in enumerate(chains):
        current = following
        if n + 1 < len(chains):
            following = front(*chains[n + 1])
        rest(*chain, *current)


def lanes_of(a):
    return slice(a * HD, (a + 1) * HD)


def attend_body(len_ref, slope_ref, q_ref, old_ref, mem_ref, now_ref, wo_ref, mix_ref, exact_ref, lse_ref, part_ref, kbuf, vbuf):
    s = pl.program_id(0)
    rows, heads = q_ref.shape[1], q_ref.shape[2] // HD
    old, mem = old_ref.shape[2], mem_ref.shape[2]
    past = old + mem
    keys = past + rows
    block = rows // 2
    length = len_ref[s]

    @pl.when(s == 0)
    def _():
        for a in range(heads):
            kbuf[a, :, HD:] = position_columns(keys)
            vbuf[a, :, HD:] = one_column(keys)

    for a in range(heads):
        for buf, c in ((kbuf, 0), (vbuf, 1)):
            buf[a, :old, :HD] = old_ref[0, c, :, lanes_of(a)]
            buf[a, old:past, :HD] = mem_ref[0, c, :, lanes_of(a)]
            buf[a, past:, :HD] = now_ref[0, c, :, lanes_of(a)]

    def front(a, i):
        side = slope_columns(slope_ref[a], block)
        wide = jnp.concatenate([q_ref[0, i * block : (i + 1) * block, lanes_of(a)], side], axis=1)
        return (dot_nt(wide, kbuf[a, : past + (i + 1) * block]),)

    def rest(a, i, scores):
        high = (i + 1) * block
        here = slice(i * block, high)
        allowed = diagonal_mask(block, i * block, length)
        last = jnp.where(allowed, scores[:, past + i * block :], -1e30)
        scores = jnp.concatenate([scores[:, : past + i * block], last], axis=1)
        top = jnp.max(scores, axis=1, keepdims=True)
        weights = jnp.exp2((scores - top) * BASE2).astype(BF16)
        both = dot(weights, vbuf[a, : past + high])
        total = both[:, HD : HD + 1]
        mixed = both[:, :HD] / total
        exact_ref[0, here, lanes_of(a)] = mixed
        mix_ref[0, here, lanes_of(a)] = mixed.astype(BF16)
        lse_ref[0, here, lanes_of(a)] = jnp.broadcast_to(top * BASE2 + jnp.log2(total), (block, HD))

    @pl.when(length > block)
    def _():
        pipelined([(a, i) for a in range(heads) for i in range(2)], front, rest)

    @pl.when(length <= block)
    def _():
        pipelined([(a, 0) for a in range(heads)], front, rest)
        exact_ref[0, block:, :] = jnp.zeros((rows - block, heads * HD), F32)
        mix_ref[0, block:, :] = jnp.zeros((rows - block, heads * HD), BF16)
        lse_ref[0, block:, :] = jnp.zeros((rows - block, heads * HD), F32)

    part_ref[0] = dot(mix_ref[0], wo_ref[...]).astype(BF16)


def attend(lengths, slopes, q, compressed, memory, now, wo):
    streams, rows, width = q.shape
    heads = width // HD
    model = wo.shape[1]
    keys = compressed.shape[2] + memory.shape[2] + rows
    cache = lambda a: pl.BlockSpec((1, 2, a.shape[2], width), lambda s, *_: (s, 0, 0, 0))
    return call(
        attend_body,
        (streams,),
        [per_stream(rows, width), cache(compressed), cache(memory), cache(now), whole(wo.shape)],
        [per_stream(rows, width), per_stream(rows, width), per_stream(rows, width), per_stream(rows, model)],
        [
            jax.ShapeDtypeStruct((streams, rows, width), BF16),
            jax.ShapeDtypeStruct((streams, rows, width), F32),
            jax.ShapeDtypeStruct((streams, rows, width), F32),
            jax.ShapeDtypeStruct((streams, rows, model), BF16),
        ],
        scratch=[pltpu.VMEM((heads, keys, 2 * HD), BF16), pltpu.VMEM((heads, keys, 2 * HD), BF16)],
        prefetch=2,
        name="attend",
    )(lengths, slopes, q, compressed, memory, now, wo)


def attend_back_body(first, len_ref, slope_ref, q_ref, old_ref, mem_ref, now_ref, exact_ref, lse_ref, grad_ref, out_ref, slope_out_ref, kbuf, vbuf):
    s = pl.program_id(0)
    rows, heads = q_ref.shape[1], q_ref.shape[2] // HD
    old, mem = old_ref.shape[2], mem_ref.shape[2]
    past = old + mem
    keys = past + rows
    block = rows // 2
    length = len_ref[s]

    @pl.when(s == 0)
    def _():
        for a in range(heads):
            kbuf[a, :, HD:] = position_columns(keys)
        slope_out_ref[...] = jnp.zeros_like(slope_out_ref)

    for a in range(heads):
        kbuf[a, :old, :HD] = old_ref[0, 0, :, lanes_of(a)]
        kbuf[a, old:past, :HD] = mem_ref[0, 0, :, lanes_of(a)]
        kbuf[a, past:, :HD] = now_ref[0, 0, :, lanes_of(a)]
        vbuf[a, :old] = old_ref[0, 1, :, lanes_of(a)]
        vbuf[a, old:past] = mem_ref[0, 1, :, lanes_of(a)]
        vbuf[a, past:] = now_ref[0, 1, :, lanes_of(a)]

    def here(i):
        return slice(i * block, (i + 1) * block)

    def front(a, i):
        side = slope_columns(slope_ref[first + a], block)
        wide = jnp.concatenate([q_ref[0, here(i), lanes_of(a)], side], axis=1)
        reach = past + (i + 1) * block
        return dot_nt(wide, kbuf[a, :reach]), dot_nt(grad_ref[0, here(i), lanes_of(a)], vbuf[a, :reach])

    def run(blocks):
        sums = {}

        def rest(a, i, scores, grad_probs):
            reach = past + (i + 1) * block
            q, grad = q_ref[0, here(i), lanes_of(a)], grad_ref[0, here(i), lanes_of(a)]
            exact = jnp.exp2(scores * BASE2 - lse_ref[0, here(i), a * HD : a * HD + 1])
            allowed = diagonal_mask(block, i * block, length)
            last = jnp.where(allowed, exact[:, reach - block :], 0.0)
            exact = jnp.concatenate([exact[:, : reach - block], last], axis=1)
            inner = jnp.sum(grad.astype(F32) * exact_ref[0, here(i), lanes_of(a)], axis=1, keepdims=True)
            grad_scores = (exact * (grad_probs - inner)).astype(BF16)
            wide = dot(grad_scores, kbuf[a, :reach])
            out_ref[0, 0, here(i), lanes_of(a)] = (wide[:, :HD] * HEAD_SCALE).astype(BF16)
            coarse, fine, total = (wide[:, HD + n : HD + n + 1] for n in (0, 1, 6))
            distance = (past + i * block - keys // 2 + lax.broadcasted_iota(jnp.int32, (block, 1), 0)).astype(F32)
            moment = jnp.sum(coarse + fine - distance * total, axis=0, keepdims=True)
            grad_keys = dot_tn(grad_scores[:, past:], q)
            grad_values = dot_tn(exact[:, past:].astype(BF16), grad)
            if i > 0:
                moment = moment + sums[a][0]
                done = sums[a][1].shape[0]
                join = lambda before, now: jnp.concatenate([before + now[:done], now[done:]], axis=0)
                grad_keys, grad_values = join(sums[a][1], grad_keys), join(sums[a][2], grad_values)
            sums[a] = moment, grad_keys, grad_values
            if i == blocks - 1:
                high = blocks * block
                out_ref[1, 0, :high, lanes_of(a)] = (grad_keys * HEAD_SCALE).astype(BF16)
                out_ref[2, 0, :high, lanes_of(a)] = grad_values.astype(BF16)
                slope_out_ref[first + a : first + a + 1, :] += jnp.broadcast_to(moment, (1, HD))

        pipelined([(a, i) for a in range(heads) for i in range(blocks)], front, rest)

    @pl.when(length > block)
    def _():
        run(2)

    @pl.when(length <= block)
    def _():
        run(1)
        for c in range(3):
            out_ref[c, 0, block:, :] = jnp.zeros((rows - block, heads * HD), BF16)


def attend_back(first, heads, lengths, slopes, q, compressed, memory, now, exact, lse, grad):
    streams, rows, width = q.shape
    keys = compressed.shape[2] + memory.shape[2] + rows
    group = first // heads
    cache = lambda a: pl.BlockSpec((1, 2, a.shape[2], heads * HD), lambda s, *_: (s, 0, 0, group))
    some = pl.BlockSpec((1, rows, heads * HD), lambda s, *_: (s, 0, group))
    return call(
        functools.partial(attend_back_body, first),
        (streams,),
        [some, cache(compressed), cache(memory), cache(now), some, some, some],
        [pl.BlockSpec((3, 1, rows, heads * HD), lambda s, *_: (0, s, 0, 0)), pl.BlockSpec((8, HD), lambda *_: (0, 0))],
        [jax.ShapeDtypeStruct((3, streams, rows, heads * HD), BF16), jax.ShapeDtypeStruct((8, HD), F32)],
        scratch=[pltpu.VMEM((heads, keys, 2 * HD), BF16), pltpu.VMEM((heads, keys, HD), BF16)],
        prefetch=2,
        cover=True,
        name="attend_back",
    )(lengths, slopes, q, compressed, memory, now, exact, lse, grad)


GELU_K = math.sqrt(2.0 / math.pi)
GELU_C = 0.044715


def gate_of(v):
    square = v * v
    rate = -2.0 * GELU_K * LOG2E
    return 1.0 / (1.0 + jnp.exp2(v * (rate + (rate * GELU_C) * square))), square


def gelu_slope(v):
    gate, square = gate_of(v)
    lean = v * (2.0 * GELU_K + (6.0 * GELU_K * GELU_C) * square)
    return gate * (1.0 + lean * (1.0 - gate))


def rise_body(len_ref, x_ref, own_ref, other_ref, gain_ref, up_ref, mid_ref, normed_t_ref, active_ref, before_ref, normed):
    rows = x_ref.shape[1]
    hidden_width = up_ref.shape[1]
    length = len_ref[pl.program_id(0)]

    def norm(r):
        here = pl.ds(r, 16)
        valid = (row_ids(r, 16) < length).astype(F32)
        attended = own_ref[0, here, :].astype(F32) + other_ref[0, here, :].astype(F32)
        middle = x_ref[0, here, :].astype(F32) + attended * valid
        mid_ref[0, here, :] = middle.astype(BF16)
        centred, scale = statistics(middle)
        normed[here, :] = (centred * scale * gain_ref[...]).astype(BF16)

    by_rows(rows, 16, norm)
    normed_t_ref[...] = normed[...].T
    chunk = min(512, hidden_width)
    columns = [slice(f, f + chunk) for f in range(0, hidden_width, chunk)]

    def front(cols):
        return (dot(normed[...], up_ref[:, cols]),)

    def rest(cols, v):
        active_ref[0, :, cols] = (v * gate_of(v)[0]).astype(BF16)
        before_ref[0, :, cols] = v.astype(BF16)

    pipelined([(cols,) for cols in columns], front, rest)


def rise(lengths, x, own, other, gain, up):
    streams, rows, model = x.shape
    hidden = up.shape[1]
    tokens = streams * rows
    return call(
        rise_body,
        (streams,),
        [per_stream(rows, model)] * 3 + [whole((1, model)), whole(up.shape)],
        [per_stream(rows, model), turned(rows, model), per_stream(rows, hidden), per_stream(rows, hidden)],
        [
            like(streams, rows, model, BF16),
            jax.ShapeDtypeStruct((model, tokens), BF16),
            like(streams, rows, hidden, BF16),
            like(streams, rows, hidden, BF16),
        ],
        scratch=[pltpu.VMEM((rows, model), BF16)],
        prefetch=1,
        name="rise",
    )(lengths, x, own, other, gain, up)


def fall_body(len_ref, cot_ref, before_ref, up_ref, down_ref, hidden_ref, *back_refs):
    rows = cot_ref.shape[1]
    hidden_width = up_ref.shape[1]
    valid = row_ids(0, rows) < len_ref[pl.program_id(0)]
    branch = jnp.where(valid, cot_ref[0].astype(F32), 0.0).astype(BF16)
    chunk = min(512, hidden_width)
    back = []

    def front(cols):
        return (dot_nt(branch, down_ref[cols, :]),)

    def rest(cols, grad_active):
        grad_hidden = (grad_active * gelu_slope(before_ref[0, :, cols].astype(F32))).astype(BF16)
        hidden_ref[0, :, cols] = grad_hidden
        back.append(dot_nt(grad_hidden, up_ref[:, cols]))

    pipelined([(slice(f, f + chunk),) for f in range(0, hidden_width, chunk)], front, rest)
    total = sum(back[1:], back[0]).astype(BF16)
    part = total.shape[1] // len(back_refs)
    for n, back_ref in enumerate(back_refs):
        back_ref[0] = total[:, n * part : (n + 1) * part]


PIECES = 4


def fall(lengths, cot, slope, up, down):
    streams, rows, model = cot.shape
    hidden = up.shape[1]
    tokens = streams * rows
    return call(
        fall_body,
        (streams,),
        [per_stream(rows, model), per_stream(rows, hidden), whole(up.shape), whole(down.shape)],
        [per_stream(rows, hidden)] + [per_stream(rows, model // PIECES)] * PIECES,
        [like(streams, rows, hidden, BF16)] + [like(streams, rows, model // PIECES, BF16)] * PIECES,
        prefetch=1,
        name="fall",
    )(lengths, cot, slope, up, down)


def leave_body(_, active_ref, down_ref, part_ref):
    part_ref[0] = dot(active_ref[0], down_ref[...]).astype(BF16)


def leave(lengths, active, down):
    streams, rows, hidden = active.shape
    model = down.shape[1]
    return call(
        leave_body,
        (streams,),
        [per_stream(rows, hidden), whole(down.shape)],
        per_stream(rows, model),
        like(streams, rows, model, BF16),
        prefetch=1,
        cover=True,
        name="leave",
    )(lengths, active, down)


def outputs_body(start, len_ref, mid_ref, own_ref, other_ref, out_ref):
    rows = mid_ref.shape[1]
    length = len_ref[start + pl.program_id(0)]

    def one(r):
        here = pl.ds(r, 16)
        valid = (row_ids(r, 16) < length).astype(F32)
        branch = own_ref[0, here, :].astype(F32) + other_ref[0, here, :].astype(F32)
        out_ref[0, here, :] = mid_ref[0, here, :].astype(F32) + valid * branch

    by_rows(rows, 16, one, 4)


def in_part(body, first, count, into, lengths, args, gain, like_this, name):
    rows, model = like_this.shape[1:]
    per = pl.BlockSpec((1, rows, model), lambda s, *_: (s + first, 0, 0))
    extra = [] if gain is None else [whole(gain.shape)]
    held = [] if into is None else [into]

    def inner(len_ref, *refs):
        body(first, len_ref, *refs[: len(args) + len(extra)], refs[-1])

    return call(
        inner,
        (count,),
        [per] * len(args) + extra + [pl.BlockSpec(memory_space=pl.ANY)] * len(held),
        per,
        jax.ShapeDtypeStruct(like_this.shape, F32),
        prefetch=1,
        cover=first > 0 or gain is None,
        aliases={1 + len(args) + len(extra): 0} if held else {},
        name=name,
    )(lengths, *args, *([] if gain is None else [gain]), *held)


def chunk_at(place, order, me):
    apart = 0
    for i, bit in enumerate(order):
        apart |= ((place >> (len(order) - 1 - i)) & 1) << bit
    return apart ^ me


def send_order(source, order, me, first, count):
    deep = source.shape[0] // (1 << len(order))
    lines = []
    for p in range(first, first + count):
        lines.append(source[pl.ds(pl.multiple_of(chunk_at(p, order, me) * deep, deep), deep), :])
    return jnp.concatenate(lines, axis=0)


def weight_body(spans, extra, order, me_ref, *refs):
    products = sum(span[2] for span in spans)
    xts, ys = list(refs[:products]), refs[products : products + len(spans)]
    sides, (keep_ref, send_ref) = refs[products + len(spans) : -2], refs[-2:]
    me = me_ref[0]
    j = pl.program_id(0)
    places = 1 << len(order)
    half = keep_ref.shape[0]
    for y, (start, stop, product) in zip(ys, spans):
        xt = xts.pop(0) if product else None

        @pl.when((j >= start) & (j < stop))
        def _(xt=xt, y=y):
            for n, out in enumerate((keep_ref, send_ref)):
                rows = send_order(y if xt is None else xt, order, me, n * places // 2, places // 2)
                if xt is not None:
                    rows = dot(rows, y[...] if len(y.shape) == 2 else y[0])
                out[:half, :] = rows.astype(out.dtype)

    if extra:
        total = sum(side[...] for side in sides)
        first = total.astype(BF16).astype(F32)
        both = jnp.concatenate([first, total - first], axis=0).astype(BF16)
        send_ref[half:, :] = jnp.concatenate([both] * (send_ref.shape[1] // HD), axis=1)


def weight_gradient(me, order, sources, step, name, sides=()):
    xts = [xt for xt, _ in sources if xt is not None]
    model, tokens = xts[0].shape
    spans, specs, at = [], [], 0
    for xt, y in sources:
        n = y.shape[-1] // step
        blocks = n * (y.shape[0] if y.ndim == 3 else 1)
        spans.append((at, at + blocks, xt is not None))
        if y.ndim == 3:
            pick = lambda j, *_, at=at, n=n, blocks=blocks: (jnp.clip(j - at, 0, blocks - 1) // n, 0, jnp.clip(j - at, 0, blocks - 1) % n)
            specs.append(pl.BlockSpec((1, y.shape[1], step), pick))
        else:
            specs.append(pl.BlockSpec((y.shape[0], step), lambda j, *_, at=at, blocks=blocks: (0, jnp.clip(j - at, 0, blocks - 1))))
        at += blocks
    columns = at * step
    extra = 16 if sides else 0
    return call(
        functools.partial(weight_body, spans, extra, order),
        (at,),
        [whole(xt.shape) for xt in xts] + specs + [whole(side.shape) for side in sides],
        [pl.BlockSpec((model // 2, step), lambda j, *_: (0, j)), pl.BlockSpec((model // 2 + extra, step), lambda j, *_: (0, j))],
        [jax.ShapeDtypeStruct((model // 2, columns), KEEP), jax.ShapeDtypeStruct((model // 2 + extra, columns), BF16)],
        prefetch=1,
        name=name,
    )(me, *xts, *[y for _, y in sources], *sides)


class Halving:
    def __init__(self, keep, send, order, count, side=None, cut=None):
        self.order, self.count, self.stage, self.total = order, count, 0, None
        self.cuts = (0, cut or keep.shape[1], keep.shape[1])
        self.keep, self.side = keep, side
        self.send(send)

    def send(self, what):
        self.sent = what
        self.came = lax.ppermute(what, "dp", flip_pairs(self.count, self.order[self.stage]))


def sum_of(keep, came, rows, columns=slice(None)):
    return keep[rows, columns].astype(F32) + came[rows, columns].astype(F32)


def side_sum(before, came, high):
    both = came[high:, :].astype(F32)
    return before[...] + (both[:8] + both[8:])


def advance_body(items, *refs):
    refs = list(refs)
    ins = [[refs.pop(0) for _ in range(3 if side else 2)] for _, side in items]
    for (cuts, side), (keep, came, *before) in zip(items, ins):
        high = keep.shape[0]
        half = high // 2
        if cuts:
            parts = [(refs.pop(0), slice(a, b)) for a, b in zip(cuts, cuts[1:]) if a < b]

            @pl.when(pl.program_id(0) == 0)
            def _(keep=keep, came=came, parts=parts, high=high):
                for out, columns in parts:
                    out[...] = sum_of(keep, came, slice(0, high), columns)

        else:
            stay, go = refs.pop(0), refs.pop(0)
            stay[...] = sum_of(keep, came, slice(0, half)).astype(stay.dtype)
            go[:half, :] = sum_of(keep, came, slice(half, high)).astype(BF16)
            if side:
                total = side_sum(before[0], came, high)
                refs.pop(0)[...] = total
                first = total.astype(BF16).astype(F32)
                go[half:, :] = jnp.concatenate([first, total - first], axis=0).astype(BF16)


def advance(rounds, token):
    rounds = [r for r in rounds if r.total is None]
    if not rounds:
        return token
    blocks = lambda a: pl.BlockSpec((a.shape[0], a.shape[1] // 2), lambda j: (0, j))
    items, args, outs, in_specs, out_specs = [], [], [], [], []
    for r in rounds:
        final, side = r.stage + 1 == len(r.order), r.side is not None
        high, columns = r.keep.shape
        items.append((r.cuts if final else None, side))
        mine = [r.keep, after(r.came, token)] + ([r.side] if side else [])
        if final:
            made = [jax.ShapeDtypeStruct((high, b - a), F32) for a, b in zip(r.cuts, r.cuts[1:]) if a < b]
        else:
            made = [
                jax.ShapeDtypeStruct((high // 2, columns), KEEP),
                jax.ShapeDtypeStruct((high // 2 + (16 if side else 0), columns), BF16),
            ] + ([jax.ShapeDtypeStruct(r.side.shape, F32)] if side else [])
        args += mine
        outs += made
        in_specs += [whole(a.shape) if final else blocks(a) for a in mine]
        out_specs += [pl.BlockSpec(a.shape, lambda j: (0, 0)) if final else blocks(a) for a in made]
    got = list(call(functools.partial(advance_body, items), (2,), in_specs, out_specs, outs, name="advance")(*args))
    token = got[0]
    for r, (cuts, side) in zip(rounds, items):
        r.stage += 1
        if cuts:
            r.total = [got.pop(0) for a, b in zip(cuts, cuts[1:]) if a < b]
            continue
        r.keep, send = got.pop(0), got.pop(0)
        if side:
            r.side = got.pop(0)
        r.send(send)
    return token


def finish_body(share, *refs):
    *ins, before, qkv_ref, out_ref, side_ref = refs
    high = ins[0].shape[0]
    for g in range(len(ins) // 2):
        keep, came = ins[2 * g], ins[2 * g + 1]
        for c in range(3):
            qkv_ref[c, :, g * share : (g + 1) * share] = sum_of(keep, came, slice(0, high), slice(c * share, (c + 1) * share))
        if g == 0:
            out_ref[...] = sum_of(keep, came, slice(0, high), slice(3 * share, keep.shape[1]))
    side_ref[...] = side_sum(before, ins[-1], high)[:, :HD]


def finish(rounds, token, share):
    high = rounds[0].keep.shape[0]
    width = share * len(rounds)
    args = [a for r in rounds for a in (r.keep, after(r.came, token))] + [rounds[-1].side]
    return call(
        functools.partial(finish_body, share),
        (1,),
        [whole(a.shape) for a in args],
        [whole((3, high, width)), whole((high, width)), whole((8, HD))],
        [
            jax.ShapeDtypeStruct((3, high, width), F32),
            jax.ShapeDtypeStruct((high, width), F32),
            jax.ShapeDtypeStruct((8, HD), F32),
        ],
        name="finish",
    )(*args)


def after(value, token):
    return lax.optimization_barrier((value, token))[0]


def conv_share(total, like, ranks, model):
    share = like.shape[3] // ranks
    pieces = math.prod(like.shape[:3])
    groups = -(-pieces * HD // model)
    total = total[:, : groups * HD].reshape(model // HD, share, groups, HD).transpose(2, 0, 1, 3)
    return total.reshape(groups * (model // HD), share, HD)[:pieces].reshape(like.shape[:3] + (share, HD))


def pair_over_head(part):
    count = lax.axis_size("head")
    for bit in range(bits_of(count)):
        came = lax.ppermute(part, "head", flip_pairs(count, bit))
        if bit == bits_of(count) - 1:
            return part, came
        part = (part.astype(F32) + came.astype(F32)).astype(part.dtype)
    return part, jnp.zeros_like(part)


def middle_body(len_ref, *refs):
    owns, others = refs[:PIECES], refs[PIECES : 2 * PIECES]
    mid_ref, cot_ref, gain_ref, wo_ref, grad_ref, turned_ref, mixed_ref, attended = refs[2 * PIECES :]
    rows = mid_ref.shape[1]
    s = pl.program_id(0)
    length = len_ref[s]

    def one(r):
        here = pl.ds(r, 16)
        valid = (row_ids(r, 16) < length).astype(F32)
        middle = mid_ref[0, here, :].astype(F32)
        sums = [own[0, here, :].astype(F32) + other[0, here, :].astype(F32) for own, other in zip(owns, others)]
        grad = jnp.concatenate(sums, axis=1)
        centred, scale = statistics(middle)
        hat = centred * scale
        e = grad * gain_ref[...]
        lean = jnp.mean(e * hat, axis=-1, keepdims=True)
        total = cot_ref[0, here, :].astype(F32) + scale * (e - jnp.mean(e, axis=-1, keepdims=True) - hat * lean)
        grad_ref[0, here, :] = total.astype(BF16)
        attended[here, :] = (total * valid).astype(BF16)

    by_rows(rows, 16, one)
    turned_ref[...] = attended[...].T
    mixed_ref[0] = dot_nt(attended[...], wo_ref[...]).astype(BF16)


def middle_back(lengths, owns, others, mid, cot, gain, wo):
    streams, rows, model = mid.shape
    width = wo.shape[0]
    return call(
        middle_body,
        (streams,),
        [per_stream(rows, model // PIECES)] * (2 * PIECES) + [per_stream(rows, model)] * 2 + [whole((1, model)), whole(wo.shape)],
        [per_stream(rows, model), turned(rows, model), per_stream(rows, width)],
        [
            jax.ShapeDtypeStruct(mid.shape, BF16),
            jax.ShapeDtypeStruct((model, streams * rows), BF16),
            like(streams, rows, width, BF16),
        ],
        scratch=[pltpu.VMEM((rows, model), BF16)],
        prefetch=1,
        name="middle_back",
    )(lengths, *owns, *others, mid, cot, gain, wo)


def lower_body(_, *refs):
    pieces, (w_ref, part_ref) = refs[:-2], refs[-2:]
    total = None
    for c in range(3):
        more = dot_nt(jnp.concatenate([piece[c, 0] for piece in pieces], axis=1), w_ref[c])
        total = more if total is None else total + more
    part_ref[0] = total.astype(BF16)


def lower(lengths, pieces, w):
    model = w.shape[1]
    _, streams, rows, _ = pieces[0].shape
    joint = lambda a: pl.BlockSpec((3, 1, rows, a.shape[3]), lambda s, *_: (0, s, 0, 0))
    return call(
        lower_body,
        (streams,),
        [joint(a) for a in pieces] + [whole(w.shape)],
        per_stream(rows, model),
        like(streams, rows, model, BF16),
        prefetch=1,
        name="lower",
    )(lengths, *pieces, w)


def inputs_body(_, __, x_ref, own_ref, other_ref, grad_ref, gain_ref, out_ref):
    rows = x_ref.shape[1]

    def one(r):
        here = pl.ds(r, 16)
        centred, scale = statistics(x_ref[0, here, :].astype(F32))
        hat = centred * scale
        e = (own_ref[0, here, :].astype(F32) + other_ref[0, here, :].astype(F32)) * gain_ref[...]
        lean = jnp.mean(e * hat, axis=-1, keepdims=True)
        out_ref[0, here, :] = grad_ref[0, here, :].astype(F32) + scale * (e - jnp.mean(e, axis=-1, keepdims=True) - hat * lean)

    by_rows(rows, 16, one)


SLOTS = 256


def rebuild_body(len_ref, q_ref, mem_ref, old_ref, conv_ref, cot_ref, next_ref, rows_ref, branch_t_ref, wide, grad_ref):
    s = pl.program_id(0)
    rows, heads = q_ref.shape[1], q_ref.shape[2] // HD
    slots = mem_ref.shape[2]
    made = slots // 3
    valid = row_ids(0, rows) < len_ref[s]
    valid_lane = lax.broadcasted_iota(jnp.int32, (1, rows), 1) < len_ref[s]
    row = lax.broadcasted_iota(jnp.int32, (slots, HD), 0)

    @pl.when(s == 0)
    def _():
        grad_ref[...] = jnp.zeros_like(grad_ref)
        wide[...] = jnp.zeros_like(wide)

    def front(a):
        windows, packed = [], []
        for c in range(2):
            wide[a, c, :slots] = mem_ref[0, c, :, lanes_of(a)].astype(F32)
            taps = [wide[a, c, pl.ds(t, SLOTS, stride=3), :].astype(BF16) for t in range(3)]
            windows.append(jnp.concatenate(taps, axis=1))
            squeezed = dot(windows[c], conv_ref[a, c].reshape(3 * HD, HD))
            packed.append(squeezed.astype(BF16))
            tail = jnp.concatenate([squeezed, jnp.zeros((slots - SLOTS, HD), F32)], axis=0)
            kept = pltpu.roll(old_ref[0, c, :, lanes_of(a)].astype(F32), slots - made, 0)
            tail = pltpu.roll(tail, slots - made, 0)
            next_ref[0, c, :, lanes_of(a)] = jnp.where(row < slots - made, kept, tail).astype(BF16)
        q = q_ref[0, :, lanes_of(a)]
        return windows, packed, dot_nt(mem_ref[0, 0, :, lanes_of(a)], q), dot_nt(packed[0], q)

    def soft(scores, count):
        start = count // 8 * 8
        key = start + lax.broadcasted_iota(jnp.int32, (scores.shape[0] - start, rows), 0)
        last = jnp.where(key < count, scores[start:], -1e30)
        scores = jnp.concatenate([scores[:start], last], axis=0)
        weights = jnp.exp2((scores - jnp.max(scores, axis=0, keepdims=True)) * BASE2)
        return weights, 1.0 / jnp.sum(weights, axis=0, keepdims=True)

    def rest(a, windows, packed, scores, few_scores):
        weights, share = soft(few_scores, made)
        probs = weights * share
        low = probs.astype(BF16)
        approach = dot(packed[1].T, low)
        weights, share = soft(scores, 3 * made)
        target = dot(mem_ref[0, 1, :, lanes_of(a)].T, weights.astype(BF16)) * share
        grad = jnp.where(valid_lane, (approach - target) * (2.0 / rows), 0.0).astype(BF16)
        grad_probs = dot(packed[1], grad)
        inner = jnp.sum(probs * grad_probs, axis=0, keepdims=True)
        grad_scores = (probs * (grad_probs - inner) * HEAD_SCALE).astype(BF16)
        back = [dot(grad_scores, q_ref[0, :, lanes_of(a)]), dot_nt(low, grad)]
        for c in range(2):
            grad_ref[a, c] += dot_tn(windows[c], back[c].astype(BF16)).reshape(3, HD, HD)

    pipelined([(a,) for a in range(heads)], front, rest)
    branch_t_ref[...] = jnp.where(valid, cot_ref[0], jnp.zeros_like(cot_ref[0])).T

    @pl.when(s == pl.num_programs(0) - 1)
    def _():
        ranks, deep, _ = rows_ref.shape
        share = HD // ranks
        rows_ref[...] = jnp.zeros_like(rows_ref)
        for a in range(heads):
            for n in range(6):
                piece = 6 * a + n
                at, group = piece % (deep // share) * share, piece // (deep // share)
                rows_ref[:, at : at + share, group * HD : (group + 1) * HD] = grad_ref[a, n // 3, n % 3].reshape(ranks, share, HD)


def rebuild(lengths, q, memory, compressed, conv, cot, ranks, columns):
    model = cot.shape[2]
    streams, rows, width = q.shape
    heads = width // HD
    slots = memory.shape[2]
    cache = pl.BlockSpec((1, 2, slots, width), lambda s, *_: (s, 0, 0, 0))
    return call(
        rebuild_body,
        (streams,),
        [per_stream(rows, width), cache, cache, whole(conv.shape), per_stream(rows, model)],
        [cache, pl.BlockSpec((ranks, model // ranks, columns), lambda *_: (0, 0, 0)), turned(rows, model)],
        [
            jax.ShapeDtypeStruct(compressed.shape, BF16),
            jax.ShapeDtypeStruct((ranks, model // ranks, columns), F32),
            jax.ShapeDtypeStruct((model, streams * rows), BF16),
        ],
        scratch=[pltpu.VMEM((heads, 2, 3 * SLOTS, HD), F32), pltpu.VMEM(conv.shape, F32)],
        prefetch=1,
        cover=True,
        name="rebuild",
    )(lengths, q, memory, compressed, conv, cot)


def per_device(
    inputs,
    cotangent,
    lengths,
    memory,
    compressed,
    query_key_value_weight,
    output_weight,
    up_weight,
    down_weight,
    gain_one,
    gain_two,
    slope_rates,
    conv_weight,
):
    streams, rows, model = inputs.shape
    tokens = streams * rows
    heads = slope_rates.shape[0]
    width = heads * HD
    ranks = lax.axis_size("dp")
    rank_bits = bits_of(ranks)
    me = lax.axis_index("dp").astype(jnp.int32)
    me_array = me.reshape(1)
    later = tuple(range(2, rank_bits))
    x_first, x_then_z, y_then_z = (0, 1) + later, (0,) + later + (1,), (1,) + later + (0,)
    y_then_mixed = (1, 2, 0) + later[1:]
    gain_1, gain_2 = gain_one.reshape(1, model), gain_two.reshape(1, model)
    qkv = query_key_value_weight.transpose(1, 0, 2)

    normed_t, q, memory_next = project(lengths, inputs, gain_1, qkv)
    mixed, exact, lse, part = attend(lengths, slope_rates, q, compressed, memory, memory_next, output_weight)
    own, other = pair_over_head(part)
    step = min(512, up_weight.shape[1])
    compressed_next, conv, branch_t = rebuild(after(lengths, part), q, memory, compressed, conv_weight, cotangent, ranks, step)
    conv = conv.reshape(model, step)
    mid, normed_two_t, active, before = rise(after(lengths, conv), inputs, own, other, gain_2, up_weight)
    sources = [(branch_t, active.reshape(tokens, -1)), (None, conv)]
    keep, send = weight_gradient(me_array, x_then_z, sources, step, "grad_down")
    down = Halving(keep, send, x_then_z, ranks, cut=up_weight.shape[1])
    grad_hidden, *backs = fall(after(lengths, send), cotangent, before, up_weight, down_weight)
    owns, others = zip(*[pair_over_head(back) for back in backs])
    keep, send = weight_gradient(me_array, y_then_z, [(normed_two_t, grad_hidden.reshape(tokens, -1))], step, "grad_up")
    up = Halving(keep, send, y_then_z, ranks)
    grad_middle, attended_t, grad_mixed = middle_back(
        after(lengths, send), owns, others, mid, cotangent, gain_2, output_weight
    )
    token = advance([down], grad_mixed)

    groups = 2 if heads % 2 == 0 else 1
    each = heads // groups
    pieces, sides, rounds = [], [], []
    for g in range(groups):
        piece, slopes = attend_back(
            g * each, each, after(lengths, token), slope_rates, q, compressed, memory, memory_next, exact, lse, grad_mixed
        )
        pieces.append(piece)
        sides.append(slopes)
        order = x_first if g else y_then_mixed
        sources = [(normed_t, piece.reshape(3, tokens, each * HD))]
        if g == 0:
            sources.append((attended_t, mixed.reshape(tokens, width)))
        final = g == groups - 1
        token = piece
        if final:
            part = lower(after(lengths, token), pieces, qkv)
            own, other = pair_over_head(part)
            token = part
        keep, send = weight_gradient(after(me_array, token), order, sources, each * HD, "grad_joint", sides if final else ())
        side = jnp.broadcast_to(sum(sides)[:, :1], (8, keep.shape[1])) if final else None
        rounds.append(Halving(keep, send, order, ranks, side))
        token = advance([up, down], send) if g == 0 else send
    early, late = rounds[0], rounds[-1]
    both = rounds[::-1]

    token = advance([early, up, down] if groups > 1 else [up, down], token)
    branch = leave(after(lengths, token), active, down_weight)
    token = advance([late, down], branch)
    branch, branch_other = pair_over_head(after(branch, token))
    grad_inputs, outputs = None, None
    parts = 2 if streams % 2 == 0 else 1
    count = streams // parts
    for p in range(parts):
        grad_inputs = in_part(
            inputs_body, p * count, count, grad_inputs, after(lengths, token), [inputs, own, other, grad_middle], gain_1, mid, "inputs_back"
        )
        token = advance(both + [up], grad_inputs)
    spans = [(0, streams - 1), (streams - 1, 1)] if streams > 1 else [(0, 1)]
    for first, count in spans:
        if first + count == streams:
            while any(r.total is None for r in [up, down]) or any(r.stage + 1 < len(r.order) for r in rounds):
                token = advance([r for r in both if r.stage + 1 < len(r.order)] + [up, down], token)
            total_qkv, total_out, slopes = finish(rounds, token, each * HD)
            token = total_qkv
        outputs = in_part(
            outputs_body, first, count, outputs, after(lengths, token), [mid, branch, branch_other], None, mid, "outputs"
        )
        token = outputs

    total_down, conv_rows = down.total
    total_conv = conv_share(conv_rows, conv_weight, ranks, model)
    total_up = up.total[0]

    portion = model // ranks
    mine = lambda a: lax.dynamic_slice_in_dim(a, me * portion, portion, 0).astype(F32)
    total_qkv = total_qkv.transpose(1, 0, 2)
    ahead = jnp.sum(total_qkv * mine(query_key_value_weight), axis=(1, 2))
    gains = jnp.stack([ahead, jnp.sum(total_up * mine(up_weight), axis=1)])
    head_count = lax.axis_size("head")
    for bit in range(bits_of(head_count)):
        gains = gains + lax.ppermute(gains, "head", flip_pairs(head_count, bit))
    gains = gains / jnp.stack([mine(gain_one), mine(gain_two)])

    return (
        outputs,
        grad_inputs,
        memory_next,
        compressed_next,
        total_qkv,
        total_out.T,
        total_up,
        total_down.T,
        gains[0],
        gains[1],
        slopes[:heads, 0],
        total_conv,
    )


def solution(mesh):
    placed = (
        P("dp", None, None),
        P("dp", None, None),
        P("dp"),
        P("dp", None, None, "head"),
        P("dp", None, None, "head"),
        P(None, None, "head"),
        P("head", None),
        P(None, "head"),
        P("head", None),
        P(),
        P(),
        P("head"),
        P("head", None, None, None, None),
    )
    return jax.shard_map(
        per_device,
        mesh=mesh,
        in_specs=placed,
        out_specs=(
            P("dp", None, None),
            P("dp", None, None),
            P("dp", None, None, "head"),
            P("dp", None, None, "head"),
            P("dp", None, "head"),
            P("head", "dp"),
            P("dp", "head"),
            P("head", "dp"),
            P("dp"),
            P("dp"),
            P("head"),
            P("head", None, None, "dp", None),
        ),
        check_vma=False,
    )
```

```python
import functools
import math

import jax
import jax.numpy as jnp
from jax import lax
from jax.experimental import pallas as pl
from jax.experimental.pallas import tpu as pltpu
from jax.sharding import PartitionSpec as P

HD = 128
CE = 170
EPS = 1e-05
LOG2E = 1.0 / math.log(2.0)
HEAD_SCALE = 1.0 / math.sqrt(HD)
BASE2 = HEAD_SCALE * LOG2E
F32 = jnp.float32
BF16 = jnp.bfloat16
KEEP = BF16
VMEM_LIMIT = 67043328


def bits_of(count):
    return count.bit_length() - 1


def flip_pairs(count, bit):
    return [(i, i ^ (1 << bit)) for i in range(count)]


def call(body, grid, in_specs, out_specs, out_shape, scratch=(), prefetch=0, cover=False, name=None, aliases=None):
    return pl.pallas_call(
        body,
        grid_spec=pltpu.PrefetchScalarGridSpec(
            num_scalar_prefetch=prefetch,
            grid=grid,
            in_specs=in_specs,
            out_specs=out_specs,
            scratch_shapes=list(scratch),
        ),
        out_shape=out_shape,
        input_output_aliases=aliases or {},
        compiler_params=pltpu.CompilerParams(dimension_semantics=("arbitrary",) * len(grid), vmem_limit_bytes=VMEM_LIMIT),
        cost_estimate=pl.CostEstimate(flops=10**13 if cover else 0, bytes_accessed=0, transcendentals=0),
        name=name,
    )


def whole(shape):
    zeros = (0,) * len(shape)
    return pl.BlockSpec(shape, lambda *_: zeros, pipeline_mode=pl.Buffered(1))


def per_stream(rows, n):
    return pl.BlockSpec((1, rows, n), lambda s, *_: (s, 0, 0))


def turned(rows, n):
    return pl.BlockSpec((n, rows), lambda s, *_: (0, s))


def like(streams, rows, n, kind):
    return jax.ShapeDtypeStruct((streams, rows, n), kind)


def dot(a, b):
    return jnp.dot(a, b, preferred_element_type=F32)


def dot_nt(a, b):
    return lax.dot_general(a, b, (((1,), (1,)), ((), ())), preferred_element_type=F32)


def dot_tn(a, b):
    return lax.dot_general(a, b, (((0,), (0,)), ((), ())), preferred_element_type=F32)


def statistics(v):
    centred = v - jnp.mean(v, axis=-1, keepdims=True)
    spread = jnp.mean(centred * centred, axis=-1, keepdims=True)
    return centred, lax.rsqrt(spread + EPS)


def by_rows(rows, step, body, together=8):
    def one(i, carry):
        for j in range(together):
            body(pl.multiple_of((i * together + j) * step, step))
        return carry

    lax.fori_loop(0, rows // (step * together), one, 0)


def row_ids(start, step):
    return start + lax.broadcasted_iota(jnp.int32, (step, 1), 0)


def project_body(len_ref, x_ref, gain_ref, w_ref, normed_t_ref, q_ref, kv_ref, normed_ref):
    rows = q_ref.shape[1]
    length = len_ref[pl.program_id(0)]

    def norm(r):
        centred, scale = statistics(x_ref[0, pl.ds(r, 16), :].astype(F32))
        normed_ref[pl.ds(r, 16), :] = (centred * scale * gain_ref[...]).astype(BF16)

    by_rows(rows, 16, norm)
    normed_t_ref[...] = normed_ref[...].T
    valid = row_ids(0, rows) < length
    normed = normed_ref[...]
    q_ref[0] = dot(normed, w_ref[0]).astype(BF16)
    for c in range(2):
        now = dot(normed, w_ref[c + 1])
        kv_ref[0, c] = jnp.where(valid, now, 0.0).astype(BF16)


def project(lengths, x, gain, w):
    streams, rows, model = x.shape
    width = w.shape[2]
    per = lambda *tail: pl.BlockSpec((1,) + tail, lambda s, *_: (s,) + (0,) * len(tail))
    return call(
        project_body,
        (streams,),
        [per(rows, model), whole((1, model)), whole(w.shape)],
        [pl.BlockSpec((model, rows), lambda s, *_: (0, s)), per(rows, width), per(2, rows, width)],
        [
            jax.ShapeDtypeStruct((model, streams * rows), BF16),
            jax.ShapeDtypeStruct((streams, rows, width), BF16),
            jax.ShapeDtypeStruct((streams, 2, rows, width), BF16),
        ],
        scratch=[pltpu.VMEM((rows, model), BF16)],
        prefetch=1,
        name="project",
    )(lengths, x, gain, w)


def position_columns(keys):
    centre = keys // 2
    lane = lax.broadcasted_iota(jnp.int32, (keys, HD), 1)
    place = lax.broadcasted_iota(jnp.int32, (keys, HD), 0) - centre
    fine = place & 7
    coarse = place - fine
    value = jnp.where(lane < 6, jnp.where((lane & 1) == 0, coarse, fine), jnp.where(lane == 6, 1, 0))
    return value.astype(F32).astype(BF16)


def slope_columns(slope, rows):
    exact = jnp.full((8, HD), slope, F32) * (1.0 / HEAD_SCALE)
    first = exact.astype(BF16).astype(F32)
    second = (exact - first).astype(BF16).astype(F32)
    third = exact - first - second
    lane = lax.broadcasted_iota(jnp.int32, (8, HD), 1)
    value = jnp.where(lane < 2, first, jnp.where(lane < 4, second, jnp.where(lane < 6, third, 0.0)))
    return jnp.broadcast_to(value[:1], (rows, HD)).astype(BF16)


def one_column(keys):
    lane = lax.broadcasted_iota(jnp.int32, (keys, HD), 1)
    return jnp.where(lane == 0, 1.0, 0.0).astype(BF16)


def diagonal_mask(block, start, length):
    row = lax.broadcasted_iota(jnp.int32, (block, block), 0)
    col = lax.broadcasted_iota(jnp.int32, (block, block), 1)
    return col <= jnp.minimum(row, length - 1 - start)


def pipelined(chains, front, rest):
    following = front(*chains[0])
    for n, chain in enumerate(chains):
        current = following
        if n + 1 < len(chains):
            following = front(*chains[n + 1])
        rest(*chain, *current)


def lanes_of(a):
    return slice(a * HD, (a + 1) * HD)


def attend_body(len_ref, slope_ref, q_ref, old_ref, mem_ref, now_ref, wo_ref, mix_ref, exact_ref, lse_ref, part_ref, kbuf, vbuf):
    s = pl.program_id(0)
    rows, heads = q_ref.shape[1], q_ref.shape[2] // HD
    old, mem = old_ref.shape[2], mem_ref.shape[2]
    past = old + mem
    keys = past + rows
    block = rows // 2
    length = len_ref[s]

    @pl.when(s == 0)
    def _():
        for a in range(heads):
            kbuf[a, :, HD:] = position_columns(keys)
            vbuf[a, :, HD:] = one_column(keys)

    for a in range(heads):
        for buf, c in ((kbuf, 0), (vbuf, 1)):
            buf[a, :old, :HD] = old_ref[0, c, :, lanes_of(a)]
            buf[a, old:past, :HD] = mem_ref[0, c, :, lanes_of(a)]
            buf[a, past:, :HD] = now_ref[0, c, :, lanes_of(a)]

    def front(a, i):
        side = slope_columns(slope_ref[a], block)
        wide = jnp.concatenate([q_ref[0, i * block : (i + 1) * block, lanes_of(a)], side], axis=1)
        return (dot_nt(wide, kbuf[a, : past + (i + 1) * block]),)

    def rest(a, i, scores):
        high = (i + 1) * block
        here = slice(i * block, high)
        allowed = diagonal_mask(block, i * block, length)
        last = jnp.where(allowed, scores[:, past + i * block :], -1e30)
        scores = jnp.concatenate([scores[:, : past + i * block], last], axis=1)
        top = jnp.max(scores, axis=1, keepdims=True)
        weights = jnp.exp2((scores - top) * BASE2).astype(BF16)
        both = dot(weights, vbuf[a, : past + high])
        total = both[:, HD : HD + 1]
        mixed = both[:, :HD] / total
        exact_ref[0, here, lanes_of(a)] = mixed
        mix_ref[0, here, lanes_of(a)] = mixed.astype(BF16)
        lse_ref[0, here, lanes_of(a)] = jnp.broadcast_to(top * BASE2 + jnp.log2(total), (block, HD))

    @pl.when(length > block)
    def _():
        pipelined([(a, i) for a in range(heads) for i in range(2)], front, rest)

    @pl.when(length <= block)
    def _():
        pipelined([(a, 0) for a in range(heads)], front, rest)
        exact_ref[0, block:, :] = jnp.zeros((rows - block, heads * HD), F32)
        mix_ref[0, block:, :] = jnp.zeros((rows - block, heads * HD), BF16)
        lse_ref[0, block:, :] = jnp.zeros((rows - block, heads * HD), F32)

    part_ref[0] = dot(mix_ref[0], wo_ref[...]).astype(BF16)


def attend(lengths, slopes, q, compressed, memory, now, wo):
    streams, rows, width = q.shape
    heads = width // HD
    model = wo.shape[1]
    keys = compressed.shape[2] + memory.shape[2] + rows
    cache = lambda a: pl.BlockSpec((1, 2, a.shape[2], width), lambda s, *_: (s, 0, 0, 0))
    return call(
        attend_body,
        (streams,),
        [per_stream(rows, width), cache(compressed), cache(memory), cache(now), whole(wo.shape)],
        [per_stream(rows, width), per_stream(rows, width), per_stream(rows, width), per_stream(rows, model)],
        [
            jax.ShapeDtypeStruct((streams, rows, width), BF16),
            jax.ShapeDtypeStruct((streams, rows, width), F32),
            jax.ShapeDtypeStruct((streams, rows, width), F32),
            jax.ShapeDtypeStruct((streams, rows, model), BF16),
        ],
        scratch=[pltpu.VMEM((heads, keys, 2 * HD), BF16), pltpu.VMEM((heads, keys, 2 * HD), BF16)],
        prefetch=2,
        name="attend",
    )(lengths, slopes, q, compressed, memory, now, wo)


def attend_back_body(first, len_ref, slope_ref, q_ref, old_ref, mem_ref, now_ref, exact_ref, lse_ref, grad_ref, out_ref, slope_out_ref, kbuf, vbuf):
    s = pl.program_id(0)
    rows, heads = q_ref.shape[1], q_ref.shape[2] // HD
    old, mem = old_ref.shape[2], mem_ref.shape[2]
    past = old + mem
    keys = past + rows
    block = rows // 2
    length = len_ref[s]

    @pl.when(s == 0)
    def _():
        for a in range(heads):
            kbuf[a, :, HD:] = position_columns(keys)
        slope_out_ref[...] = jnp.zeros_like(slope_out_ref)

    for a in range(heads):
        kbuf[a, :old, :HD] = old_ref[0, 0, :, lanes_of(a)]
        kbuf[a, old:past, :HD] = mem_ref[0, 0, :, lanes_of(a)]
        kbuf[a, past:, :HD] = now_ref[0, 0, :, lanes_of(a)]
        vbuf[a, :old] = old_ref[0, 1, :, lanes_of(a)]
        vbuf[a, old:past] = mem_ref[0, 1, :, lanes_of(a)]
        vbuf[a, past:] = now_ref[0, 1, :, lanes_of(a)]

    def here(i):
        return slice(i * block, (i + 1) * block)

    def front(a, i):
        side = slope_columns(slope_ref[first + a], block)
        wide = jnp.concatenate([q_ref[0, here(i), lanes_of(a)], side], axis=1)
        reach = past + (i + 1) * block
        return dot_nt(wide, kbuf[a, :reach]), dot_nt(grad_ref[0, here(i), lanes_of(a)], vbuf[a, :reach])

    def run(blocks):
        sums = {}

        def rest(a, i, scores, grad_probs):
            reach = past + (i + 1) * block
            q, grad = q_ref[0, here(i), lanes_of(a)], grad_ref[0, here(i), lanes_of(a)]
            exact = jnp.exp2(scores * BASE2 - lse_ref[0, here(i), a * HD : a * HD + 1])
            allowed = diagonal_mask(block, i * block, length)
            last = jnp.where(allowed, exact[:, reach - block :], 0.0)
            exact = jnp.concatenate([exact[:, : reach - block], last], axis=1)
            inner = jnp.sum(grad.astype(F32) * exact_ref[0, here(i), lanes_of(a)], axis=1, keepdims=True)
            grad_scores = (exact * (grad_probs - inner)).astype(BF16)
            wide = dot(grad_scores, kbuf[a, :reach])
            out_ref[0, 0, here(i), lanes_of(a)] = (wide[:, :HD] * HEAD_SCALE).astype(BF16)
            coarse, fine, total = (wide[:, HD + n : HD + n + 1] for n in (0, 1, 6))
            distance = (past + i * block - keys // 2 + lax.broadcasted_iota(jnp.int32, (block, 1), 0)).astype(F32)
            moment = jnp.sum(coarse + fine - distance * total, axis=0, keepdims=True)
            grad_keys = dot_tn(grad_scores[:, past:], q)
            grad_values = dot_tn(exact[:, past:].astype(BF16), grad)
            if i > 0:
                moment = moment + sums[a][0]
                done = sums[a][1].shape[0]
                join = lambda before, now: jnp.concatenate([before + now[:done], now[done:]], axis=0)
                grad_keys, grad_values = join(sums[a][1], grad_keys), join(sums[a][2], grad_values)
            sums[a] = moment, grad_keys, grad_values
            if i == blocks - 1:
                high = blocks * block
                out_ref[1, 0, :high, lanes_of(a)] = (grad_keys * HEAD_SCALE).astype(BF16)
                out_ref[2, 0, :high, lanes_of(a)] = grad_values.astype(BF16)
                slope_out_ref[first + a : first + a + 1, :] += jnp.broadcast_to(moment, (1, HD))

        pipelined([(a, i) for a in range(heads) for i in range(blocks)], front, rest)

    @pl.when(length > block)
    def _():
        run(2)

    @pl.when(length <= block)
    def _():
        run(1)
        for c in range(3):
            out_ref[c, 0, block:, :] = jnp.zeros((rows - block, heads * HD), BF16)


def attend_back(first, heads, lengths, slopes, q, compressed, memory, now, exact, lse, grad):
    streams, rows, width = q.shape
    keys = compressed.shape[2] + memory.shape[2] + rows
    group = first // heads
    cache = lambda a: pl.BlockSpec((1, 2, a.shape[2], heads * HD), lambda s, *_: (s, 0, 0, group))
    some = pl.BlockSpec((1, rows, heads * HD), lambda s, *_: (s, 0, group))
    return call(
        functools.partial(attend_back_body, first),
        (streams,),
        [some, cache(compressed), cache(memory), cache(now), some, some, some],
        [pl.BlockSpec((3, 1, rows, heads * HD), lambda s, *_: (0, s, 0, 0)), pl.BlockSpec((8, HD), lambda *_: (0, 0))],
        [jax.ShapeDtypeStruct((3, streams, rows, heads * HD), BF16), jax.ShapeDtypeStruct((8, HD), F32)],
        scratch=[pltpu.VMEM((heads, keys, 2 * HD), BF16), pltpu.VMEM((heads, keys, HD), BF16)],
        prefetch=2,
        cover=True,
        name="attend_back",
    )(lengths, slopes, q, compressed, memory, now, exact, lse, grad)


GELU_K = math.sqrt(2.0 / math.pi)
GELU_C = 0.044715


def gate_of(v):
    square = v * v
    rate = -2.0 * GELU_K * LOG2E
    return 1.0 / (1.0 + jnp.exp2(v * (rate + (rate * GELU_C) * square))), square


def gelu_slope(v):
    gate, square = gate_of(v)
    lean = v * (2.0 * GELU_K + (6.0 * GELU_K * GELU_C) * square)
    return gate * (1.0 + lean * (1.0 - gate))


def rise_body(len_ref, x_ref, own_ref, other_ref, gain_ref, up_ref, mid_ref, normed_t_ref, active_ref, before_ref, normed):
    rows = x_ref.shape[1]
    hidden_width = up_ref.shape[1]
    length = len_ref[pl.program_id(0)]

    def norm(r):
        here = pl.ds(r, 16)
        valid = (row_ids(r, 16) < length).astype(F32)
        attended = own_ref[0, here, :].astype(F32) + other_ref[0, here, :].astype(F32)
        middle = x_ref[0, here, :].astype(F32) + attended * valid
        mid_ref[0, here, :] = middle.astype(BF16)
        centred, scale = statistics(middle)
        normed[here, :] = (centred * scale * gain_ref[...]).astype(BF16)

    by_rows(rows, 16, norm)
    normed_t_ref[...] = normed[...].T
    chunk = min(512, hidden_width)
    columns = [slice(f, f + chunk) for f in range(0, hidden_width, chunk)]

    def front(cols):
        return (dot(normed[...], up_ref[:, cols]),)

    def rest(cols, v):
        active_ref[0, :, cols] = (v * gate_of(v)[0]).astype(BF16)
        before_ref[0, :, cols] = v.astype(BF16)

    pipelined([(cols,) for cols in columns], front, rest)


def rise(lengths, x, own, other, gain, up):
    streams, rows, model = x.shape
    hidden = up.shape[1]
    tokens = streams * rows
    return call(
        rise_body,
        (streams,),
        [per_stream(rows, model)] * 3 + [whole((1, model)), whole(up.shape)],
        [per_stream(rows, model), turned(rows, model), per_stream(rows, hidden), per_stream(rows, hidden)],
        [
            like(streams, rows, model, BF16),
            jax.ShapeDtypeStruct((model, tokens), BF16),
            like(streams, rows, hidden, BF16),
            like(streams, rows, hidden, BF16),
        ],
        scratch=[pltpu.VMEM((rows, model), BF16)],
        prefetch=1,
        name="rise",
    )(lengths, x, own, other, gain, up)


def fall_body(len_ref, cot_ref, before_ref, up_ref, down_ref, hidden_ref, *back_refs):
    rows = cot_ref.shape[1]
    hidden_width = up_ref.shape[1]
    valid = row_ids(0, rows) < len_ref[pl.program_id(0)]
    branch = jnp.where(valid, cot_ref[0].astype(F32), 0.0).astype(BF16)
    chunk = min(512, hidden_width)
    back = []

    def front(cols):
        return (dot_nt(branch, down_ref[cols, :]),)

    def rest(cols, grad_active):
        grad_hidden = (grad_active * gelu_slope(before_ref[0, :, cols].astype(F32))).astype(BF16)
        hidden_ref[0, :, cols] = grad_hidden
        back.append(dot_nt(grad_hidden, up_ref[:, cols]))

    pipelined([(slice(f, f + chunk),) for f in range(0, hidden_width, chunk)], front, rest)
    total = sum(back[1:], back[0]).astype(BF16)
    part = total.shape[1] // len(back_refs)
    for n, back_ref in enumerate(back_refs):
        back_ref[0] = total[:, n * part : (n + 1) * part]


PIECES = 4


def fall(lengths, cot, slope, up, down):
    streams, rows, model = cot.shape
    hidden = up.shape[1]
    tokens = streams * rows
    return call(
        fall_body,
        (streams,),
        [per_stream(rows, model), per_stream(rows, hidden), whole(up.shape), whole(down.shape)],
        [per_stream(rows, hidden)] + [per_stream(rows, model // PIECES)] * PIECES,
        [like(streams, rows, hidden, BF16)] + [like(streams, rows, model // PIECES, BF16)] * PIECES,
        prefetch=1,
        name="fall",
    )(lengths, cot, slope, up, down)


def leave_body(_, active_ref, down_ref, part_ref):
    part_ref[0] = dot(active_ref[0], down_ref[...]).astype(BF16)


def leave(lengths, active, down):
    streams, rows, hidden = active.shape
    model = down.shape[1]
    return call(
        leave_body,
        (streams,),
        [per_stream(rows, hidden), whole(down.shape)],
        per_stream(rows, model),
        like(streams, rows, model, BF16),
        prefetch=1,
        cover=True,
        name="leave",
    )(lengths, active, down)


def outputs_body(start, len_ref, mid_ref, own_ref, other_ref, out_ref):
    rows = mid_ref.shape[1]
    length = len_ref[start + pl.program_id(0)]

    def one(r):
        here = pl.ds(r, 16)
        valid = (row_ids(r, 16) < length).astype(F32)
        branch = own_ref[0, here, :].astype(F32) + other_ref[0, here, :].astype(F32)
        out_ref[0, here, :] = mid_ref[0, here, :].astype(F32) + valid * branch

    by_rows(rows, 16, one, 4)


def in_part(body, first, count, into, lengths, args, gain, like_this, name):
    rows, model = like_this.shape[1:]
    per = pl.BlockSpec((1, rows, model), lambda s, *_: (s + first, 0, 0))
    extra = [] if gain is None else [whole(gain.shape)]
    held = [] if into is None else [into]

    def inner(len_ref, *refs):
        body(first, len_ref, *refs[: len(args) + len(extra)], refs[-1])

    return call(
        inner,
        (count,),
        [per] * len(args) + extra + [pl.BlockSpec(memory_space=pl.ANY)] * len(held),
        per,
        jax.ShapeDtypeStruct(like_this.shape, F32),
        prefetch=1,
        cover=first > 0 or gain is None,
        aliases={1 + len(args) + len(extra): 0} if held else {},
        name=name,
    )(lengths, *args, *([] if gain is None else [gain]), *held)


def chunk_at(place, order, me):
    apart = 0
    for i, bit in enumerate(order):
        apart |= ((place >> (len(order) - 1 - i)) & 1) << bit
    return apart ^ me


def send_order(source, order, me, first, count):
    deep = source.shape[0] // (1 << len(order))
    lines = []
    for p in range(first, first + count):
        lines.append(source[pl.ds(pl.multiple_of(chunk_at(p, order, me) * deep, deep), deep), :])
    return jnp.concatenate(lines, axis=0)


def weight_body(spans, extra, order, me_ref, *refs):
    products = sum(span[2] for span in spans)
    xts, ys = list(refs[:products]), refs[products : products + len(spans)]
    sides, outs = refs[products + len(spans) :], refs[-3 if extra else -2 :]
    sides, keep_ref, send_ref = sides[: -len(outs)], outs[0], outs[1]
    me = me_ref[0]
    j = pl.program_id(0)
    places = 1 << len(order)
    half = keep_ref.shape[0]
    for y, (start, stop, product) in zip(ys, spans):
        xt = xts.pop(0) if product else None

        @pl.when((j >= start) & (j < stop))
        def _(xt=xt, y=y):
            for n, out in enumerate((keep_ref, send_ref)):
                rows = send_order(y if xt is None else xt, order, me, n * places // 2, places // 2)
                if xt is not None:
                    rows = dot(rows, y[...] if len(y.shape) == 2 else y[0])
                out[:half, :] = rows.astype(out.dtype)

    if extra:
        total = sum(side[...] for side in sides)
        first = total.astype(BF16).astype(F32)
        both = jnp.concatenate([first, total - first], axis=0).astype(BF16)
        times = send_ref.shape[1] // HD
        send_ref[half:, :] = jnp.concatenate([both] * times, axis=1)
        outs[2][...] = jnp.concatenate([total] * times, axis=1)


def weight_gradient(me, order, sources, step, name, sides=()):
    xts = [xt for xt, _ in sources if xt is not None]
    model, tokens = xts[0].shape
    spans, specs, at = [], [], 0
    for xt, y in sources:
        n = y.shape[-1] // step
        blocks = n * (y.shape[0] if y.ndim == 3 else 1)
        spans.append((at, at + blocks, xt is not None))
        if y.ndim == 3:
            pick = lambda j, *_, at=at, n=n, blocks=blocks: (jnp.clip(j - at, 0, blocks - 1) // n, 0, jnp.clip(j - at, 0, blocks - 1) % n)
            specs.append(pl.BlockSpec((1, y.shape[1], step), pick))
        else:
            specs.append(pl.BlockSpec((y.shape[0], step), lambda j, *_, at=at, blocks=blocks: (0, jnp.clip(j - at, 0, blocks - 1))))
        at += blocks
    columns = at * step
    extra = 16 if sides else 0
    heights = (model // 2, model // 2 + extra) + ((8,) if sides else ())
    return call(
        functools.partial(weight_body, spans, extra, order),
        (at,),
        [whole(xt.shape) for xt in xts] + specs + [whole(side.shape) for side in sides],
        [pl.BlockSpec((n, step), lambda j, *_: (0, j)) for n in heights],
        [jax.ShapeDtypeStruct((n, columns), kind) for n, kind in zip(heights, (KEEP, BF16, F32))],
        prefetch=1,
        name=name,
    )(me, *xts, *[y for _, y in sources], *sides)


class Halving:
    def __init__(self, keep, send, order, count, side=None, cut=None):
        self.order, self.count, self.stage, self.total = order, count, 0, None
        self.cuts = (0, cut or keep.shape[1], keep.shape[1])
        self.keep, self.side = keep, side
        self.send(send)

    def send(self, what):
        self.sent = what
        self.came = lax.ppermute(what, "dp", flip_pairs(self.count, self.order[self.stage]))


def sum_of(keep, came, rows, columns=slice(None)):
    return keep[rows, columns].astype(F32) + came[rows, columns].astype(F32)


def side_sum(before, came, high):
    both = came[high:, :].astype(F32)
    return before[...] + (both[:8] + both[8:])


def advance_body(items, *refs):
    refs = list(refs)
    ins = [[refs.pop(0) for _ in range(3 if side else 2)] for _, side in items]
    for (cuts, side), (keep, came, *before) in zip(items, ins):
        high = keep.shape[0]
        half = high // 2
        if cuts:
            parts = [(refs.pop(0), slice(a, b)) for a, b in zip(cuts, cuts[1:]) if a < b]

            @pl.when(pl.program_id(0) == 0)
            def _(keep=keep, came=came, parts=parts, high=high):
                for out, columns in parts:
                    out[...] = sum_of(keep, came, slice(0, high), columns)

        else:
            stay, go = refs.pop(0), refs.pop(0)
            stay[...] = sum_of(keep, came, slice(0, half)).astype(stay.dtype)
            go[:half, :] = sum_of(keep, came, slice(half, high)).astype(BF16)
            if side:
                total = side_sum(before[0], came, high)
                refs.pop(0)[...] = total
                first = total.astype(BF16).astype(F32)
                go[half:, :] = jnp.concatenate([first, total - first], axis=0).astype(BF16)


def advance(rounds, token):
    rounds = [r for r in rounds if r.total is None]
    if not rounds:
        return token
    blocks = lambda a: pl.BlockSpec((a.shape[0], a.shape[1] // 2), lambda j: (0, j))
    items, args, outs, in_specs, out_specs = [], [], [], [], []
    for r in rounds:
        final, side = r.stage + 1 == len(r.order), r.side is not None
        high, columns = r.keep.shape
        items.append((r.cuts if final else None, side))
        mine = [r.keep, after(r.came, token)] + ([r.side] if side else [])
        if final:
            made = [jax.ShapeDtypeStruct((high, b - a), F32) for a, b in zip(r.cuts, r.cuts[1:]) if a < b]
        else:
            made = [
                jax.ShapeDtypeStruct((high // 2, columns), KEEP),
                jax.ShapeDtypeStruct((high // 2 + (16 if side else 0), columns), BF16),
            ] + ([jax.ShapeDtypeStruct(r.side.shape, F32)] if side else [])
        args += mine
        outs += made
        in_specs += [whole(a.shape) if final else blocks(a) for a in mine]
        out_specs += [pl.BlockSpec(a.shape, lambda j: (0, 0)) if final else blocks(a) for a in made]
    got = list(call(functools.partial(advance_body, items), (2,), in_specs, out_specs, outs, name="advance")(*args))
    token = got[0]
    for r, (cuts, side) in zip(rounds, items):
        r.stage += 1
        if cuts:
            r.total = [got.pop(0) for a, b in zip(cuts, cuts[1:]) if a < b]
            continue
        r.keep, send = got.pop(0), got.pop(0)
        if side:
            r.side = got.pop(0)
        r.send(send)
    return token


def finish_body(share, _, *refs):
    *ins, before, keep_up, came_up, w_ref, up_w_ref, qkv_ref, out_ref, side_ref, up_ref, gain_ref = refs
    high = keep_up.shape[0]
    rows = slice(0, high)
    for g in range(len(ins) // 2):
        keep, came = ins[2 * g], ins[2 * g + 1]
        for c in range(3):
            qkv_ref[c, :, g * share : (g + 1) * share] = sum_of(keep, came, rows, slice(c * share, (c + 1) * share))
        if g == 0:
            out_ref[...] = sum_of(keep, came, rows, slice(3 * share, keep.shape[1]))
    side_ref[...] = side_sum(before, ins[-1], high)[:, :HD]
    total = sum_of(keep_up, came_up, rows)
    up_ref[...] = total
    ahead = sum(jnp.sum(qkv_ref[c] * w_ref[c].astype(F32), axis=1, keepdims=True) for c in range(3))
    rising = jnp.sum(total * up_w_ref[...].astype(F32), axis=1, keepdims=True)
    lane = lax.broadcasted_iota(jnp.int32, (high, HD), 1)
    both = jnp.where(lane == 0, ahead, rising)
    gain_ref[...] = jnp.concatenate([both, jnp.zeros((HD - high, HD), F32)], axis=0).T[:8]


def finish(me, rounds, up, token, share, w, up_weight):
    high = up.keep.shape[0]
    width = share * len(rounds)
    args = [a for r in rounds for a in (r.keep, after(r.came, token))] + [rounds[-1].side, up.keep, after(up.came, token)]
    hidden = up_weight.shape[1]
    mine = [pl.BlockSpec((3, high, width), lambda j, me: (0, me[0], 0)), pl.BlockSpec((high, hidden), lambda j, me: (me[0], 0))]
    made = [(3, high, width), (high, width), (8, HD), (high, hidden), (8, HD)]
    return call(
        functools.partial(finish_body, share),
        (1,),
        [whole(a.shape) for a in args] + mine,
        [whole(a) for a in made],
        [jax.ShapeDtypeStruct(a, F32) for a in made],
        prefetch=1,
        name="finish",
    )(me, *args, w, up_weight)


def after(value, token):
    return lax.optimization_barrier((value, token))[0]


def conv_share(total, like, ranks, model):
    share = like.shape[3] // ranks
    pieces = math.prod(like.shape[:3])
    groups = -(-pieces * HD // model)
    total = total[:, : groups * HD].reshape(model // HD, share, groups, HD).transpose(2, 0, 1, 3)
    return total.reshape(groups * (model // HD), share, HD)[:pieces].reshape(like.shape[:3] + (share, HD))


def pair_over_head(part):
    count = lax.axis_size("head")
    for bit in range(bits_of(count)):
        came = lax.ppermute(part, "head", flip_pairs(count, bit))
        if bit == bits_of(count) - 1:
            return part, came
        part = (part.astype(F32) + came.astype(F32)).astype(part.dtype)
    return part, jnp.zeros_like(part)


def middle_body(len_ref, *refs):
    owns, others = refs[:PIECES], refs[PIECES : 2 * PIECES]
    mid_ref, cot_ref, gain_ref, wo_ref, grad_ref, turned_ref, mixed_ref, attended = refs[2 * PIECES :]
    rows = mid_ref.shape[1]
    s = pl.program_id(0)
    length = len_ref[s]

    def one(r):
        here = pl.ds(r, 16)
        valid = (row_ids(r, 16) < length).astype(F32)
        middle = mid_ref[0, here, :].astype(F32)
        sums = [own[0, here, :].astype(F32) + other[0, here, :].astype(F32) for own, other in zip(owns, others)]
        grad = jnp.concatenate(sums, axis=1)
        centred, scale = statistics(middle)
        hat = centred * scale
        e = grad * gain_ref[...]
        lean = jnp.mean(e * hat, axis=-1, keepdims=True)
        total = cot_ref[0, here, :].astype(F32) + scale * (e - jnp.mean(e, axis=-1, keepdims=True) - hat * lean)
        grad_ref[0, here, :] = total.astype(BF16)
        attended[here, :] = (total * valid).astype(BF16)

    by_rows(rows, 16, one)
    turned_ref[...] = attended[...].T
    mixed_ref[0] = dot_nt(attended[...], wo_ref[...]).astype(BF16)


def middle_back(lengths, owns, others, mid, cot, gain, wo):
    streams, rows, model = mid.shape
    width = wo.shape[0]
    return call(
        middle_body,
        (streams,),
        [per_stream(rows, model // PIECES)] * (2 * PIECES) + [per_stream(rows, model)] * 2 + [whole((1, model)), whole(wo.shape)],
        [per_stream(rows, model), turned(rows, model), per_stream(rows, width)],
        [
            jax.ShapeDtypeStruct(mid.shape, BF16),
            jax.ShapeDtypeStruct((model, streams * rows), BF16),
            like(streams, rows, width, BF16),
        ],
        scratch=[pltpu.VMEM((rows, model), BF16)],
        prefetch=1,
        name="middle_back",
    )(lengths, *owns, *others, mid, cot, gain, wo)


def lower_body(_, *refs):
    pieces, (w_ref, part_ref) = refs[:-2], refs[-2:]
    total = None
    for c in range(3):
        more = dot_nt(jnp.concatenate([piece[c, 0] for piece in pieces], axis=1), w_ref[c])
        total = more if total is None else total + more
    part_ref[0] = total.astype(BF16)


def lower(lengths, pieces, w):
    model = w.shape[1]
    _, streams, rows, _ = pieces[0].shape
    joint = lambda a: pl.BlockSpec((3, 1, rows, a.shape[3]), lambda s, *_: (0, s, 0, 0))
    return call(
        lower_body,
        (streams,),
        [joint(a) for a in pieces] + [whole(w.shape)],
        per_stream(rows, model),
        like(streams, rows, model, BF16),
        prefetch=1,
        name="lower",
    )(lengths, *pieces, w)


def inputs_body(_, __, x_ref, own_ref, other_ref, grad_ref, gain_ref, out_ref):
    rows = x_ref.shape[1]

    def one(r):
        here = pl.ds(r, 16)
        centred, scale = statistics(x_ref[0, here, :].astype(F32))
        hat = centred * scale
        e = (own_ref[0, here, :].astype(F32) + other_ref[0, here, :].astype(F32)) * gain_ref[...]
        lean = jnp.mean(e * hat, axis=-1, keepdims=True)
        out_ref[0, here, :] = grad_ref[0, here, :].astype(F32) + scale * (e - jnp.mean(e, axis=-1, keepdims=True) - hat * lean)

    by_rows(rows, 16, one)


SLOTS = 256


def rebuild_body(len_ref, q_ref, mem_ref, old_ref, conv_ref, cot_ref, next_ref, rows_ref, branch_t_ref, wide, grad_ref):
    s = pl.program_id(0)
    rows, heads = q_ref.shape[1], q_ref.shape[2] // HD
    slots = mem_ref.shape[2]
    made = slots // 3
    valid = row_ids(0, rows) < len_ref[s]
    valid_lane = lax.broadcasted_iota(jnp.int32, (1, rows), 1) < len_ref[s]
    row = lax.broadcasted_iota(jnp.int32, (slots, HD), 0)

    @pl.when(s == 0)
    def _():
        grad_ref[...] = jnp.zeros_like(grad_ref)
        wide[...] = jnp.zeros_like(wide)

    def front(a):
        windows, packed = [], []
        for c in range(2):
            wide[a, c, :slots] = mem_ref[0, c, :, lanes_of(a)].astype(F32)
            taps = [wide[a, c, pl.ds(t, SLOTS, stride=3), :].astype(BF16) for t in range(3)]
            windows.append(jnp.concatenate(taps, axis=1))
            squeezed = dot(windows[c], conv_ref[a, c].reshape(3 * HD, HD))
            packed.append(squeezed.astype(BF16))
            tail = jnp.concatenate([squeezed, jnp.zeros((slots - SLOTS, HD), F32)], axis=0)
            kept = pltpu.roll(old_ref[0, c, :, lanes_of(a)].astype(F32), slots - made, 0)
            tail = pltpu.roll(tail, slots - made, 0)
            next_ref[0, c, :, lanes_of(a)] = jnp.where(row < slots - made, kept, tail).astype(BF16)
        q = q_ref[0, :, lanes_of(a)]
        return windows, packed, dot_nt(mem_ref[0, 0, :, lanes_of(a)], q), dot_nt(packed[0], q)

    def soft(scores, count):
        start = count // 8 * 8
        key = start + lax.broadcasted_iota(jnp.int32, (scores.shape[0] - start, rows), 0)
        last = jnp.where(key < count, scores[start:], -1e30)
        scores = jnp.concatenate([scores[:start], last], axis=0)
        weights = jnp.exp2((scores - jnp.max(scores, axis=0, keepdims=True)) * BASE2)
        return weights, 1.0 / jnp.sum(weights, axis=0, keepdims=True)

    def rest(a, windows, packed, scores, few_scores):
        weights, share = soft(few_scores, made)
        probs = weights * share
        low = probs.astype(BF16)
        approach = dot(packed[1].T, low)
        weights, share = soft(scores, 3 * made)
        target = dot(mem_ref[0, 1, :, lanes_of(a)].T, weights.astype(BF16)) * share
        grad = jnp.where(valid_lane, (approach - target) * (2.0 / rows), 0.0).astype(BF16)
        grad_probs = dot(packed[1], grad)
        inner = jnp.sum(probs * grad_probs, axis=0, keepdims=True)
        grad_scores = (probs * (grad_probs - inner) * HEAD_SCALE).astype(BF16)
        back = [dot(grad_scores, q_ref[0, :, lanes_of(a)]), dot_nt(low, grad)]
        for c in range(2):
            grad_ref[a, c] += dot_tn(windows[c], back[c].astype(BF16)).reshape(3, HD, HD)

    pipelined([(a,) for a in range(heads)], front, rest)
    branch_t_ref[...] = jnp.where(valid, cot_ref[0], jnp.zeros_like(cot_ref[0])).T

    @pl.when(s == pl.num_programs(0) - 1)
    def _():
        ranks, deep, _ = rows_ref.shape
        share = HD // ranks
        rows_ref[...] = jnp.zeros_like(rows_ref)
        for a in range(heads):
            for n in range(6):
                piece = 6 * a + n
                at, group = piece % (deep // share) * share, piece // (deep // share)
                rows_ref[:, at : at + share, group * HD : (group + 1) * HD] = grad_ref[a, n // 3, n % 3].reshape(ranks, share, HD)


def rebuild(lengths, q, memory, compressed, conv, cot, ranks, columns):
    model = cot.shape[2]
    streams, rows, width = q.shape
    heads = width // HD
    slots = memory.shape[2]
    cache = pl.BlockSpec((1, 2, slots, width), lambda s, *_: (s, 0, 0, 0))
    return call(
        rebuild_body,
        (streams,),
        [per_stream(rows, width), cache, cache, whole(conv.shape), per_stream(rows, model)],
        [cache, pl.BlockSpec((ranks, model // ranks, columns), lambda *_: (0, 0, 0)), turned(rows, model)],
        [
            jax.ShapeDtypeStruct(compressed.shape, BF16),
            jax.ShapeDtypeStruct((ranks, model // ranks, columns), F32),
            jax.ShapeDtypeStruct((model, streams * rows), BF16),
        ],
        scratch=[pltpu.VMEM((heads, 2, 3 * SLOTS, HD), F32), pltpu.VMEM(conv.shape, F32)],
        prefetch=1,
        cover=True,
        name="rebuild",
    )(lengths, q, memory, compressed, conv, cot)


def per_device(
    inputs,
    cotangent,
    lengths,
    memory,
    compressed,
    query_key_value_weight,
    output_weight,
    up_weight,
    down_weight,
    gain_one,
    gain_two,
    slope_rates,
    conv_weight,
):
    streams, rows, model = inputs.shape
    tokens = streams * rows
    heads = slope_rates.shape[0]
    width = heads * HD
    ranks = lax.axis_size("dp")
    rank_bits = bits_of(ranks)
    me = lax.axis_index("dp").astype(jnp.int32)
    me_array = me.reshape(1)
    later = tuple(range(2, rank_bits))
    x_first, x_then_z, y_then_z = (0, 1) + later, (0,) + later + (1,), (1,) + later + (0,)
    y_then_mixed = (1, 2, 0) + later[1:]
    gain_1, gain_2 = gain_one.reshape(1, model), gain_two.reshape(1, model)
    qkv = query_key_value_weight.transpose(1, 0, 2)

    normed_t, q, memory_next = project(lengths, inputs, gain_1, qkv)
    mixed, exact, lse, part = attend(lengths, slope_rates, q, compressed, memory, memory_next, output_weight)
    own, other = pair_over_head(part)
    step = min(512, up_weight.shape[1])
    compressed_next, conv, branch_t = rebuild(after(lengths, part), q, memory, compressed, conv_weight, cotangent, ranks, step)
    conv = conv.reshape(model, step)
    mid, normed_two_t, active, before = rise(after(lengths, conv), inputs, own, other, gain_2, up_weight)
    sources = [(branch_t, active.reshape(tokens, -1)), (None, conv)]
    keep, send = weight_gradient(me_array, x_then_z, sources, step, "grad_down")
    down = Halving(keep, send, x_then_z, ranks, cut=up_weight.shape[1])
    grad_hidden, *backs = fall(after(lengths, send), cotangent, before, up_weight, down_weight)
    owns, others = zip(*[pair_over_head(back) for back in backs])
    keep, send = weight_gradient(me_array, y_then_z, [(normed_two_t, grad_hidden.reshape(tokens, -1))], step, "grad_up")
    up = Halving(keep, send, y_then_z, ranks)
    grad_middle, attended_t, grad_mixed = middle_back(
        after(lengths, send), owns, others, mid, cotangent, gain_2, output_weight
    )
    token = advance([down], grad_mixed)

    groups = 2 if heads % 2 == 0 else 1
    each = heads // groups
    pieces, sides, rounds = [], [], []
    for g in range(groups):
        piece, slopes = attend_back(
            g * each, each, after(lengths, token), slope_rates, q, compressed, memory, memory_next, exact, lse, grad_mixed
        )
        pieces.append(piece)
        sides.append(slopes)
        order = x_first if g else y_then_mixed
        sources = [(normed_t, piece.reshape(3, tokens, each * HD))]
        if g == 0:
            sources.append((attended_t, mixed.reshape(tokens, width)))
        final = g == groups - 1
        token = piece
        if final:
            part = lower(after(lengths, token), pieces, qkv)
            own, other = pair_over_head(part)
            token = part
        made = weight_gradient(after(me_array, token), order, sources, each * HD, "grad_joint", sides if final else ())
        keep, send = made[:2]
        rounds.append(Halving(keep, send, order, ranks, made[2] if final else None))
        token = advance([up, down], send) if g == 0 else send
    early, late = rounds[0], rounds[-1]
    both = rounds[::-1]

    token = advance([early, up, down] if groups > 1 else [up, down], token)
    branch = leave(after(lengths, token), active, down_weight)
    token = advance([late, down], branch)
    branch, branch_other = pair_over_head(after(branch, token))
    grad_inputs, outputs = None, None
    parts = 2 if streams % 2 == 0 else 1
    count = streams // parts
    for p in range(parts):
        grad_inputs = in_part(
            inputs_body, p * count, count, grad_inputs, after(lengths, token), [inputs, own, other, grad_middle], gain_1, mid, "inputs_back"
        )
        token = advance(both + ([] if p else [up]), grad_inputs)
    up.send(after(up.sent, token))
    spans = [(0, streams - 1), (streams - 1, 1)] if streams > 1 else [(0, 1)]
    for first, count in spans:
        if first + count == streams:
            unfinished = lambda: [r for r in both + [up] if r.stage + 1 < len(r.order)] + [r for r in [down] if r.total is None]
            while unfinished():
                token = advance(unfinished(), token)
            total_qkv, total_out, slopes, total_up, gains = finish(me_array, rounds, up, token, each * HD, qkv, up_weight)
            token = total_qkv
        outputs = in_part(
            outputs_body, first, count, outputs, after(lengths, token), [mid, branch, branch_other], None, mid, "outputs"
        )
        token = outputs

    total_down, conv_rows = down.total
    total_conv = conv_share(conv_rows, conv_weight, ranks, model)
    portion = model // ranks
    mine = lambda a: lax.dynamic_slice_in_dim(a, me * portion, portion, 0)
    head_count = lax.axis_size("head")
    for bit in range(bits_of(head_count)):
        gains = gains + lax.ppermute(gains, "head", flip_pairs(head_count, bit))
    total_gain_one = gains[0, :portion] / mine(gain_one)
    total_gain_two = gains[1, :portion] / mine(gain_two)

    return (
        outputs,
        grad_inputs,
        memory_next,
        compressed_next,
        total_qkv.transpose(1, 0, 2),
        total_out.T,
        total_up,
        total_down.T,
        total_gain_one,
        total_gain_two,
        slopes[:heads, 0],
        total_conv,
    )


def solution(mesh):
    placed = (
        P("dp", None, None),
        P("dp", None, None),
        P("dp"),
        P("dp", None, None, "head"),
        P("dp", None, None, "head"),
        P(None, None, "head"),
        P("head", None),
        P(None, "head"),
        P("head", None),
        P(),
        P(),
        P("head"),
        P("head", None, None, None, None),
    )
    return jax.shard_map(
        per_device,
        mesh=mesh,
        in_specs=placed,
        out_specs=(
            P("dp", None, None),
            P("dp", None, None),
            P("dp", None, None, "head"),
            P("dp", None, None, "head"),
            P("dp", None, "head"),
            P("head", "dp"),
            P("dp", "head"),
            P("head", "dp"),
            P("dp"),
            P("dp"),
            P("head"),
            P("head", None, None, "dp", None),
        ),
        check_vma=False,
    )
```

```python
import functools
import math

import jax
import jax.numpy as jnp
from jax import lax
from jax.experimental import pallas as pl
from jax.experimental.pallas import tpu as pltpu
from jax.sharding import PartitionSpec as P

HD = 128
CE = 170
EPS = 1e-05
LOG2E = 1.0 / math.log(2.0)
HEAD_SCALE = 1.0 / math.sqrt(HD)
BASE2 = HEAD_SCALE * LOG2E
F32 = jnp.float32
BF16 = jnp.bfloat16
KEEP = BF16
VMEM_LIMIT = 67043328


def bits_of(count):
    return count.bit_length() - 1


def flip_pairs(count, bit):
    return [(i, i ^ (1 << bit)) for i in range(count)]


def call(body, grid, in_specs, out_specs, out_shape, scratch=(), prefetch=0, cover=False, name=None, aliases=None):
    return pl.pallas_call(
        body,
        grid_spec=pltpu.PrefetchScalarGridSpec(
            num_scalar_prefetch=prefetch,
            grid=grid,
            in_specs=in_specs,
            out_specs=out_specs,
            scratch_shapes=list(scratch),
        ),
        out_shape=out_shape,
        input_output_aliases=aliases or {},
        compiler_params=pltpu.CompilerParams(dimension_semantics=("arbitrary",) * len(grid), vmem_limit_bytes=VMEM_LIMIT),
        cost_estimate=pl.CostEstimate(flops=10**13 if cover else 0, bytes_accessed=0, transcendentals=0),
        name=name,
    )


def whole(shape):
    zeros = (0,) * len(shape)
    return pl.BlockSpec(shape, lambda *_: zeros, pipeline_mode=pl.Buffered(1))


def per_stream(rows, n):
    return pl.BlockSpec((1, rows, n), lambda s, *_: (s, 0, 0))


def turned(rows, n):
    return pl.BlockSpec((n, rows), lambda s, *_: (0, s))


def like(streams, rows, n, kind):
    return jax.ShapeDtypeStruct((streams, rows, n), kind)


def dot(a, b):
    return jnp.dot(a, b, preferred_element_type=F32)


def dot_nt(a, b):
    return lax.dot_general(a, b, (((1,), (1,)), ((), ())), preferred_element_type=F32)


def dot_tn(a, b):
    return lax.dot_general(a, b, (((0,), (0,)), ((), ())), preferred_element_type=F32)


def statistics(v):
    centred = v - jnp.mean(v, axis=-1, keepdims=True)
    spread = jnp.mean(centred * centred, axis=-1, keepdims=True)
    return centred, lax.rsqrt(spread + EPS)


def norm_back(v, e):
    centred = v - jnp.mean(v, axis=-1, keepdims=True)
    spread = jnp.mean(centred * centred, axis=-1, keepdims=True)
    middle = jnp.mean(e, axis=-1, keepdims=True)
    along = jnp.mean(e * centred, axis=-1, keepdims=True)
    scale = lax.rsqrt(spread + EPS)
    return scale * (e - middle - centred * (scale * scale * along))


def by_rows(rows, step, body, together=8):
    def one(i, carry):
        for j in range(together):
            body(pl.multiple_of((i * together + j) * step, step))
        return carry

    if rows == step * together:
        for j in range(together):
            body(j * step)
    else:
        lax.fori_loop(0, rows // (step * together), one, 0)


def row_ids(start, step):
    return start + lax.broadcasted_iota(jnp.int32, (step, 1), 0)


def project_body(len_ref, x_ref, gain_ref, w_ref, normed_t_ref, q_ref, kv_ref, normed_ref):
    rows = q_ref.shape[1]
    length = len_ref[pl.program_id(0)]

    def norm(r):
        centred, scale = statistics(x_ref[0, pl.ds(r, 16), :].astype(F32))
        normed_ref[pl.ds(r, 16), :] = (centred * scale * gain_ref[...]).astype(BF16)

    by_rows(rows, 16, norm, rows // 16)
    normed_t_ref[...] = normed_ref[...].T
    valid = row_ids(0, rows) < length
    normed = normed_ref[...]
    q_ref[0] = dot(normed, w_ref[0]).astype(BF16)
    for c in range(2):
        now = dot(normed, w_ref[c + 1])
        kv_ref[0, c] = jnp.where(valid, now, 0.0).astype(BF16)


def project(lengths, x, gain, w):
    streams, rows, model = x.shape
    width = w.shape[2]
    per = lambda *tail: pl.BlockSpec((1,) + tail, lambda s, *_: (s,) + (0,) * len(tail))
    return call(
        project_body,
        (streams,),
        [per(rows, model), whole((1, model)), whole(w.shape)],
        [pl.BlockSpec((model, rows), lambda s, *_: (0, s)), per(rows, width), per(2, rows, width)],
        [
            jax.ShapeDtypeStruct((model, streams * rows), BF16),
            jax.ShapeDtypeStruct((streams, rows, width), BF16),
            jax.ShapeDtypeStruct((streams, 2, rows, width), BF16),
        ],
        scratch=[pltpu.VMEM((rows, model), BF16)],
        prefetch=1,
        name="project",
    )(lengths, x, gain, w)


def position_columns(keys):
    centre = keys // 2
    lane = lax.broadcasted_iota(jnp.int32, (keys, HD), 1)
    place = lax.broadcasted_iota(jnp.int32, (keys, HD), 0) - centre
    fine = place & 7
    coarse = place - fine
    value = jnp.where(lane < 6, jnp.where((lane & 1) == 0, coarse, fine), jnp.where(lane == 6, 1, 0))
    return value.astype(F32).astype(BF16)


def slope_columns(slope, rows):
    exact = jnp.full((8, HD), slope, F32) * (1.0 / HEAD_SCALE)
    first = exact.astype(BF16).astype(F32)
    second = (exact - first).astype(BF16).astype(F32)
    third = exact - first - second
    lane = lax.broadcasted_iota(jnp.int32, (8, HD), 1)
    value = jnp.where(lane < 2, first, jnp.where(lane < 4, second, jnp.where(lane < 6, third, 0.0)))
    return jnp.broadcast_to(value[:1], (rows, HD)).astype(BF16)


def one_column(keys):
    lane = lax.broadcasted_iota(jnp.int32, (keys, HD), 1)
    return jnp.where(lane == 0, 1.0, 0.0).astype(BF16)


def diagonal_mask(block, start, length):
    row = lax.broadcasted_iota(jnp.int32, (block, block), 0)
    col = lax.broadcasted_iota(jnp.int32, (block, block), 1)
    return col <= jnp.minimum(row, length - 1 - start)


def pipelined(chains, front, rest):
    following = front(*chains[0])
    for n, chain in enumerate(chains):
        current = following
        if n + 1 < len(chains):
            following = front(*chains[n + 1])
        rest(*chain, *current)


def lanes_of(a):
    return slice(a * HD, (a + 1) * HD)


def attend_body(len_ref, slope_ref, q_ref, old_ref, mem_ref, now_ref, wo_ref, mix_ref, exact_ref, lse_ref, part_ref, kbuf, vbuf):
    s = pl.program_id(0)
    rows, heads = q_ref.shape[1], q_ref.shape[2] // HD
    old, mem = old_ref.shape[2], mem_ref.shape[2]
    past = old + mem
    keys = past + rows
    block = rows // 2
    length = len_ref[s]

    @pl.when(s == 0)
    def _():
        for a in range(heads):
            kbuf[a, :, HD:] = position_columns(keys)
            vbuf[a, :, HD:] = one_column(keys)

    for a in range(heads):
        for buf, c in ((kbuf, 0), (vbuf, 1)):
            buf[a, :old, :HD] = old_ref[0, c, :, lanes_of(a)]
            buf[a, old:past, :HD] = mem_ref[0, c, :, lanes_of(a)]
            buf[a, past:, :HD] = now_ref[0, c, :, lanes_of(a)]

    def front(a, i):
        side = slope_columns(slope_ref[a], block)
        wide = jnp.concatenate([q_ref[0, i * block : (i + 1) * block, lanes_of(a)], side], axis=1)
        return (dot_nt(wide, kbuf[a, : past + (i + 1) * block]),)

    def rest(a, i, scores):
        high = (i + 1) * block
        here = slice(i * block, high)
        allowed = diagonal_mask(block, i * block, length)
        last = jnp.where(allowed, scores[:, past + i * block :], -1e30)
        scores = jnp.concatenate([scores[:, : past + i * block], last], axis=1)
        top = jnp.max(scores, axis=1, keepdims=True)
        weights = jnp.exp2((scores - top) * BASE2).astype(BF16)
        both = dot(weights, vbuf[a, : past + high])
        total = both[:, HD : HD + 1]
        mixed = both[:, :HD] / total
        exact_ref[0, here, lanes_of(a)] = mixed
        mix_ref[0, here, lanes_of(a)] = mixed.astype(BF16)
        lse_ref[0, here, lanes_of(a)] = jnp.broadcast_to(top * BASE2 + jnp.log2(total), (block, HD))

    @pl.when(length > block)
    def _():
        pipelined([(a, i) for a in range(heads) for i in range(2)], front, rest)

    @pl.when(length <= block)
    def _():
        pipelined([(a, 0) for a in range(heads)], front, rest)
        exact_ref[0, block:, :] = jnp.zeros((rows - block, heads * HD), F32)
        mix_ref[0, block:, :] = jnp.zeros((rows - block, heads * HD), BF16)
        lse_ref[0, block:, :] = jnp.zeros((rows - block, heads * HD), F32)

    part_ref[0] = dot(mix_ref[0], wo_ref[...]).astype(BF16)


def attend(lengths, slopes, q, compressed, memory, now, wo):
    streams, rows, width = q.shape
    heads = width // HD
    model = wo.shape[1]
    keys = compressed.shape[2] + memory.shape[2] + rows
    cache = lambda a: pl.BlockSpec((1, 2, a.shape[2], width), lambda s, *_: (s, 0, 0, 0))
    return call(
        attend_body,
        (streams,),
        [per_stream(rows, width), cache(compressed), cache(memory), cache(now), whole(wo.shape)],
        [per_stream(rows, width), per_stream(rows, width), per_stream(rows, width), per_stream(rows, model)],
        [
            jax.ShapeDtypeStruct((streams, rows, width), BF16),
            jax.ShapeDtypeStruct((streams, rows, width), F32),
            jax.ShapeDtypeStruct((streams, rows, width), F32),
            jax.ShapeDtypeStruct((streams, rows, model), BF16),
        ],
        scratch=[pltpu.VMEM((heads, keys, 2 * HD), BF16), pltpu.VMEM((heads, keys, 2 * HD), BF16)],
        prefetch=2,
        name="attend",
    )(lengths, slopes, q, compressed, memory, now, wo)


def attend_back_body(first, len_ref, slope_ref, q_ref, old_ref, mem_ref, now_ref, exact_ref, lse_ref, grad_ref, out_ref, slope_out_ref, kbuf, vbuf):
    s = pl.program_id(0)
    rows, heads = q_ref.shape[1], q_ref.shape[2] // HD
    old, mem = old_ref.shape[2], mem_ref.shape[2]
    past = old + mem
    keys = past + rows
    block = rows // 2
    length = len_ref[s]

    @pl.when(s == 0)
    def _():
        for a in range(heads):
            kbuf[a, :, HD:] = position_columns(keys)
        slope_out_ref[...] = jnp.zeros_like(slope_out_ref)

    for a in range(heads):
        kbuf[a, :old, :HD] = old_ref[0, 0, :, lanes_of(a)]
        kbuf[a, old:past, :HD] = mem_ref[0, 0, :, lanes_of(a)]
        kbuf[a, past:, :HD] = now_ref[0, 0, :, lanes_of(a)]
        vbuf[a, :old] = old_ref[0, 1, :, lanes_of(a)]
        vbuf[a, old:past] = mem_ref[0, 1, :, lanes_of(a)]
        vbuf[a, past:] = now_ref[0, 1, :, lanes_of(a)]

    def here(i):
        return slice(i * block, (i + 1) * block)

    def front(a, i):
        side = slope_columns(slope_ref[first + a], block)
        wide = jnp.concatenate([q_ref[0, here(i), lanes_of(a)], side], axis=1)
        reach = past + (i + 1) * block
        return dot_nt(wide, kbuf[a, :reach]), dot_nt(grad_ref[0, here(i), lanes_of(a)], vbuf[a, :reach])

    def run(blocks):
        sums = {}

        def rest(a, i, scores, grad_probs):
            reach = past + (i + 1) * block
            q, grad = q_ref[0, here(i), lanes_of(a)], grad_ref[0, here(i), lanes_of(a)]
            exact = jnp.exp2(scores * BASE2 - lse_ref[0, here(i), a * HD : a * HD + 1])
            allowed = diagonal_mask(block, i * block, length)
            last = jnp.where(allowed, exact[:, reach - block :], 0.0)
            exact = jnp.concatenate([exact[:, : reach - block], last], axis=1)
            inner = jnp.sum(grad.astype(F32) * exact_ref[0, here(i), lanes_of(a)], axis=1, keepdims=True)
            grad_scores = (exact * (grad_probs - inner)).astype(BF16)
            wide = dot(grad_scores, kbuf[a, :reach])
            out_ref[0, 0, here(i), lanes_of(a)] = (wide[:, :HD] * HEAD_SCALE).astype(BF16)
            coarse, fine, total = (wide[:, HD + n : HD + n + 1] for n in (0, 1, 6))
            distance = (past + i * block - keys // 2 + lax.broadcasted_iota(jnp.int32, (block, 1), 0)).astype(F32)
            moment = jnp.sum(coarse + fine - distance * total, axis=0, keepdims=True)
            grad_keys = dot_tn(grad_scores[:, past:], q)
            grad_values = dot_tn(exact[:, past:].astype(BF16), grad)
            if i > 0:
                moment = moment + sums[a][0]
                done = sums[a][1].shape[0]
                join = lambda before, now: jnp.concatenate([before + now[:done], now[done:]], axis=0)
                grad_keys, grad_values = join(sums[a][1], grad_keys), join(sums[a][2], grad_values)
            sums[a] = moment, grad_keys, grad_values
            if i == blocks - 1:
                high = blocks * block
                out_ref[1, 0, :high, lanes_of(a)] = (grad_keys * HEAD_SCALE).astype(BF16)
                out_ref[2, 0, :high, lanes_of(a)] = grad_values.astype(BF16)
                slope_out_ref[first + a : first + a + 1, :] += jnp.broadcast_to(moment, (1, HD))

        pipelined([(a, i) for a in range(heads) for i in range(blocks)], front, rest)

    @pl.when(length > block)
    def _():
        run(2)

    @pl.when(length <= block)
    def _():
        run(1)
        for c in range(3):
            out_ref[c, 0, block:, :] = jnp.zeros((rows - block, heads * HD), BF16)


def attend_back(first, heads, lengths, slopes, q, compressed, memory, now, exact, lse, grad):
    streams, rows, width = q.shape
    keys = compressed.shape[2] + memory.shape[2] + rows
    group = first // heads
    cache = lambda a: pl.BlockSpec((1, 2, a.shape[2], heads * HD), lambda s, *_: (s, 0, 0, group))
    some = pl.BlockSpec((1, rows, heads * HD), lambda s, *_: (s, 0, group))
    return call(
        functools.partial(attend_back_body, first),
        (streams,),
        [some, cache(compressed), cache(memory), cache(now), some, some, some],
        [pl.BlockSpec((3, 1, rows, heads * HD), lambda s, *_: (0, s, 0, 0)), pl.BlockSpec((8, HD), lambda *_: (0, 0))],
        [jax.ShapeDtypeStruct((3, streams, rows, heads * HD), BF16), jax.ShapeDtypeStruct((8, HD), F32)],
        scratch=[pltpu.VMEM((heads, keys, 2 * HD), BF16), pltpu.VMEM((heads, keys, HD), BF16)],
        prefetch=2,
        cover=True,
        name="attend_back",
    )(lengths, slopes, q, compressed, memory, now, exact, lse, grad)


GELU_K = math.sqrt(2.0 / math.pi)
GELU_C = 0.044715


def gate_of(v):
    square = v * v
    rate = -2.0 * GELU_K * LOG2E
    return 1.0 / (1.0 + jnp.exp2(v * (rate + (rate * GELU_C) * square))), square


def gelu_slope(v):
    gate, square = gate_of(v)
    lean = v * (2.0 * GELU_K + (6.0 * GELU_K * GELU_C) * square)
    return gate * (1.0 + lean * (1.0 - gate))


def rise_body(len_ref, x_ref, own_ref, other_ref, gain_ref, up_ref, mid_ref, normed_t_ref, active_ref, before_ref, normed):
    rows = x_ref.shape[1]
    hidden_width = up_ref.shape[1]
    length = len_ref[pl.program_id(0)]

    def norm(r):
        here = pl.ds(r, 16)
        valid = (row_ids(r, 16) < length).astype(F32)
        attended = own_ref[0, here, :].astype(F32) + other_ref[0, here, :].astype(F32)
        middle = x_ref[0, here, :].astype(F32) + attended * valid
        mid_ref[0, here, :] = middle.astype(BF16)
        centred, scale = statistics(middle)
        normed[here, :] = (centred * scale * gain_ref[...]).astype(BF16)

    by_rows(rows, 16, norm, rows // 16)
    normed_t_ref[...] = normed[...].T
    chunk = min(512, hidden_width)
    columns = [slice(f, f + chunk) for f in range(0, hidden_width, chunk)]

    def front(cols):
        return (dot(normed[...], up_ref[:, cols]),)

    def rest(cols, v):
        active_ref[0, :, cols] = (v * gate_of(v)[0]).astype(BF16)
        before_ref[0, :, cols] = v.astype(BF16)

    pipelined([(cols,) for cols in columns], front, rest)


def rise(lengths, x, own, other, gain, up):
    streams, rows, model = x.shape
    hidden = up.shape[1]
    tokens = streams * rows
    return call(
        rise_body,
        (streams,),
        [per_stream(rows, model)] * 3 + [whole((1, model)), whole(up.shape)],
        [per_stream(rows, model), turned(rows, model), per_stream(rows, hidden), per_stream(rows, hidden)],
        [
            like(streams, rows, model, BF16),
            jax.ShapeDtypeStruct((model, tokens), BF16),
            like(streams, rows, hidden, BF16),
            like(streams, rows, hidden, BF16),
        ],
        scratch=[pltpu.VMEM((rows, model), BF16)],
        prefetch=1,
        name="rise",
    )(lengths, x, own, other, gain, up)


def fall_body(len_ref, cot_ref, before_ref, up_ref, down_ref, hidden_ref, *back_refs):
    rows = cot_ref.shape[1]
    hidden_width = up_ref.shape[1]
    valid = row_ids(0, rows) < len_ref[pl.program_id(0)]
    branch = jnp.where(valid, cot_ref[0].astype(F32), 0.0).astype(BF16)
    chunk = min(1024, hidden_width)
    back = []

    def front(cols):
        return (dot_nt(branch, down_ref[cols, :]),)

    def rest(cols, grad_active):
        grad_hidden = (grad_active * gelu_slope(before_ref[0, :, cols].astype(F32))).astype(BF16)
        hidden_ref[0, :, cols] = grad_hidden
        back.append(dot_nt(grad_hidden, up_ref[:, cols]))

    pipelined([(slice(f, f + chunk),) for f in range(0, hidden_width, chunk)], front, rest)
    total = sum(back[1:], back[0]).astype(BF16)
    part = total.shape[1] // len(back_refs)
    for n, back_ref in enumerate(back_refs):
        back_ref[0] = total[:, n * part : (n + 1) * part]


PIECES = 4


def fall(lengths, cot, slope, up, down):
    streams, rows, model = cot.shape
    hidden = up.shape[1]
    tokens = streams * rows
    return call(
        fall_body,
        (streams,),
        [per_stream(rows, model), per_stream(rows, hidden), whole(up.shape), whole(down.shape)],
        [per_stream(rows, hidden)] + [per_stream(rows, model // PIECES)] * PIECES,
        [like(streams, rows, hidden, BF16)] + [like(streams, rows, model // PIECES, BF16)] * PIECES,
        prefetch=1,
        name="fall",
    )(lengths, cot, slope, up, down)


def leave_body(_, active_ref, down_ref, part_ref):
    part_ref[0] = dot(active_ref[0], down_ref[...]).astype(BF16)


def leave(lengths, active, down):
    streams, rows, hidden = active.shape
    model = down.shape[1]
    return call(
        leave_body,
        (streams,),
        [per_stream(rows, hidden), whole(down.shape)],
        per_stream(rows, model),
        like(streams, rows, model, BF16),
        prefetch=1,
        cover=True,
        name="leave",
    )(lengths, active, down)


def outputs_body(start, len_ref, mid_ref, own_ref, other_ref, out_ref):
    rows = mid_ref.shape[1]
    length = len_ref[start + pl.program_id(0)]

    def one(r):
        here = pl.ds(r, 16)
        valid = (row_ids(r, 16) < length).astype(F32)
        branch = own_ref[0, here, :].astype(F32) + other_ref[0, here, :].astype(F32)
        out_ref[0, here, :] = mid_ref[0, here, :].astype(F32) + valid * branch

    by_rows(rows, 16, one, 4)


def in_part(body, first, count, into, lengths, args, gain, like_this, name):
    rows, model = like_this.shape[1:]
    per = pl.BlockSpec((1, rows, model), lambda s, *_: (s + first, 0, 0))
    extra = [] if gain is None else [whole(gain.shape)]
    held = [] if into is None else [into]

    def inner(len_ref, *refs):
        body(first, len_ref, *refs[: len(args) + len(extra)], refs[-1])

    return call(
        inner,
        (count,),
        [per] * len(args) + extra + [pl.BlockSpec(memory_space=pl.ANY)] * len(held),
        per,
        jax.ShapeDtypeStruct(like_this.shape, F32),
        prefetch=1,
        cover=first > 0 or gain is None,
        aliases={1 + len(args) + len(extra): 0} if held else {},
        name=name,
    )(lengths, *args, *([] if gain is None else [gain]), *held)


def chunk_at(place, order, me):
    apart = 0
    for i, bit in enumerate(order):
        apart |= ((place >> (len(order) - 1 - i)) & 1) << bit
    return apart ^ me


def send_order(source, order, me, first, count):
    deep = source.shape[0] // (1 << len(order))
    lines = []
    for p in range(first, first + count):
        lines.append(source[pl.ds(pl.multiple_of(chunk_at(p, order, me) * deep, deep), deep), :])
    return jnp.concatenate(lines, axis=0)


def weight_body(spans, extra, order, me_ref, *refs):
    products = sum(span[2] for span in spans)
    xts, ys = list(refs[:products]), refs[products : products + len(spans)]
    sides, outs = refs[products + len(spans) :], refs[-3 if extra else -2 :]
    sides, keep_ref, send_ref = sides[: -len(outs)], outs[0], outs[1]
    me = me_ref[0]
    j = pl.program_id(0)
    places = 1 << len(order)
    half = keep_ref.shape[0]
    for y, (start, stop, product) in zip(ys, spans):
        xt = xts.pop(0) if product else None

        @pl.when((j >= start) & (j < stop))
        def _(xt=xt, y=y):
            for n, out in enumerate((keep_ref, send_ref)):
                rows = send_order(y if xt is None else xt, order, me, n * places // 2, places // 2)
                if xt is not None:
                    rows = dot(rows, y[...] if len(y.shape) == 2 else y[0])
                out[:half, :] = rows.astype(out.dtype)

    if extra:
        total = sum(side[...] for side in sides)
        first = total.astype(BF16).astype(F32)
        both = jnp.concatenate([first, total - first], axis=0).astype(BF16)
        times = send_ref.shape[1] // HD
        send_ref[half:, :] = jnp.concatenate([both] * times, axis=1)
        outs[2][...] = jnp.concatenate([total] * times, axis=1)


def weight_gradient(me, order, sources, step, name, sides=()):
    xts = [xt for xt, _ in sources if xt is not None]
    model, tokens = xts[0].shape
    spans, specs, at = [], [], 0
    for xt, y in sources:
        n = y.shape[-1] // step
        blocks = n * (y.shape[0] if y.ndim == 3 else 1)
        spans.append((at, at + blocks, xt is not None))
        if y.ndim == 3:
            pick = lambda j, *_, at=at, n=n, blocks=blocks: (jnp.clip(j - at, 0, blocks - 1) // n, 0, jnp.clip(j - at, 0, blocks - 1) % n)
            specs.append(pl.BlockSpec((1, y.shape[1], step), pick))
        else:
            specs.append(pl.BlockSpec((y.shape[0], step), lambda j, *_, at=at, blocks=blocks: (0, jnp.clip(j - at, 0, blocks - 1))))
        at += blocks
    columns = at * step
    extra = 16 if sides else 0
    heights = (model // 2, model // 2 + extra) + ((8,) if sides else ())
    return call(
        functools.partial(weight_body, spans, extra, order),
        (at,),
        [whole(xt.shape) for xt in xts] + specs + [whole(side.shape) for side in sides],
        [pl.BlockSpec((n, step), lambda j, *_: (0, j)) for n in heights],
        [jax.ShapeDtypeStruct((n, columns), kind) for n, kind in zip(heights, (KEEP, BF16, F32))],
        prefetch=1,
        name=name,
    )(me, *xts, *[y for _, y in sources], *sides)


class Halving:
    def __init__(self, keep, send, order, count, side=None, cut=None):
        self.order, self.count, self.stage, self.total = order, count, 0, None
        self.cuts = (0, cut or keep.shape[1], keep.shape[1])
        self.keep, self.side = keep, side
        self.send(send)

    def send(self, what):
        self.sent = what
        self.came = lax.ppermute(what, "dp", flip_pairs(self.count, self.order[self.stage]))


def sum_of(keep, came, rows, columns=slice(None)):
    return keep[rows, columns].astype(F32) + came[rows, columns].astype(F32)


def side_sum(before, came, high):
    both = came[high:, :].astype(F32)
    return before[...] + (both[:8] + both[8:])


def advance_body(items, *refs):
    refs = list(refs)
    ins = [[refs.pop(0) for _ in range(3 if side else 2)] for _, side in items]
    for (cuts, side), (keep, came, *before) in zip(items, ins):
        high = keep.shape[0]
        half = high // 2
        if cuts:
            parts = [(refs.pop(0), slice(a, b)) for a, b in zip(cuts, cuts[1:]) if a < b]

            @pl.when(pl.program_id(0) == 0)
            def _(keep=keep, came=came, parts=parts, high=high):
                for out, columns in parts:
                    out[...] = sum_of(keep, came, slice(0, high), columns)

        else:
            stay, go = refs.pop(0), refs.pop(0)
            stay[...] = sum_of(keep, came, slice(0, half)).astype(stay.dtype)
            go[:half, :] = sum_of(keep, came, slice(half, high)).astype(BF16)
            if side:
                total = side_sum(before[0], came, high)
                refs.pop(0)[...] = total
                first = total.astype(BF16).astype(F32)
                go[half:, :] = jnp.concatenate([first, total - first], axis=0).astype(BF16)


def advance(rounds, token):
    rounds = [r for r in rounds if r.total is None]
    if not rounds:
        return token
    blocks = lambda a: pl.BlockSpec((a.shape[0], a.shape[1] // 2), lambda j: (0, j))
    items, args, outs, in_specs, out_specs = [], [], [], [], []
    for r in rounds:
        final, side = r.stage + 1 == len(r.order), r.side is not None
        high, columns = r.keep.shape
        items.append((r.cuts if final else None, side))
        mine = [r.keep, after(r.came, token)] + ([r.side] if side else [])
        if final:
            made = [jax.ShapeDtypeStruct((high, b - a), F32) for a, b in zip(r.cuts, r.cuts[1:]) if a < b]
        else:
            made = [
                jax.ShapeDtypeStruct((high // 2, columns), KEEP),
                jax.ShapeDtypeStruct((high // 2 + (16 if side else 0), columns), BF16),
            ] + ([jax.ShapeDtypeStruct(r.side.shape, F32)] if side else [])
        args += mine
        outs += made
        in_specs += [whole(a.shape) if final else blocks(a) for a in mine]
        out_specs += [pl.BlockSpec(a.shape, lambda j: (0, 0)) if final else blocks(a) for a in made]
    got = list(call(functools.partial(advance_body, items), (2,), in_specs, out_specs, outs, name="advance")(*args))
    token = got[0]
    for r, (cuts, side) in zip(rounds, items):
        r.stage += 1
        if cuts:
            r.total = [got.pop(0) for a, b in zip(cuts, cuts[1:]) if a < b]
            continue
        r.keep, send = got.pop(0), got.pop(0)
        if side:
            r.side = got.pop(0)
        r.send(send)
    return token


def finish_body(share, _, *refs):
    *ins, before, keep_up, came_up, w_ref, up_w_ref, qkv_ref, out_ref, side_ref, up_ref, gain_ref = refs
    high = keep_up.shape[0]
    rows = slice(0, high)
    for g in range(len(ins) // 2):
        keep, came = ins[2 * g], ins[2 * g + 1]
        for c in range(3):
            qkv_ref[c, :, g * share : (g + 1) * share] = sum_of(keep, came, rows, slice(c * share, (c + 1) * share))
        if g == 0:
            out_ref[...] = sum_of(keep, came, rows, slice(3 * share, keep.shape[1]))
    side_ref[...] = side_sum(before, ins[-1], high)[:, :HD]
    total = sum_of(keep_up, came_up, rows)
    up_ref[...] = total
    ahead = sum(jnp.sum(qkv_ref[c] * w_ref[c].astype(F32), axis=1, keepdims=True) for c in range(3))
    rising = jnp.sum(total * up_w_ref[...].astype(F32), axis=1, keepdims=True)
    lane = lax.broadcasted_iota(jnp.int32, (high, HD), 1)
    both = jnp.where(lane == 0, ahead, rising)
    gain_ref[...] = jnp.concatenate([both, jnp.zeros((HD - high, HD), F32)], axis=0).T[:8]


def finish(me, rounds, up, token, share, w, up_weight):
    high = up.keep.shape[0]
    width = share * len(rounds)
    args = [a for r in rounds for a in (r.keep, after(r.came, token))] + [rounds[-1].side, up.keep, after(up.came, token)]
    hidden = up_weight.shape[1]
    mine = [pl.BlockSpec((3, high, width), lambda j, me: (0, me[0], 0)), pl.BlockSpec((high, hidden), lambda j, me: (me[0], 0))]
    made = [(3, high, width), (high, width), (8, HD), (high, hidden), (8, HD)]
    return call(
        functools.partial(finish_body, share),
        (1,),
        [whole(a.shape) for a in args] + mine,
        [whole(a) for a in made],
        [jax.ShapeDtypeStruct(a, F32) for a in made],
        prefetch=1,
        name="finish",
    )(me, *args, w, up_weight)


def after(value, token):
    return lax.optimization_barrier((value, token))[0]


def conv_share(total, like, ranks, model):
    share = like.shape[3] // ranks
    pieces = math.prod(like.shape[:3])
    groups = -(-pieces * HD // model)
    total = total[:, : groups * HD].reshape(model // HD, share, groups, HD).transpose(2, 0, 1, 3)
    return total.reshape(groups * (model // HD), share, HD)[:pieces].reshape(like.shape[:3] + (share, HD))


def pair_over_head(part):
    count = lax.axis_size("head")
    for bit in range(bits_of(count)):
        came = lax.ppermute(part, "head", flip_pairs(count, bit))
        if bit == bits_of(count) - 1:
            return part, came
        part = (part.astype(F32) + came.astype(F32)).astype(part.dtype)
    return part, jnp.zeros_like(part)


def middle_body(len_ref, *refs):
    owns, others = refs[:PIECES], refs[PIECES : 2 * PIECES]
    mid_ref, cot_ref, gain_ref, wo_ref, grad_ref, turned_ref, mixed_ref, attended = refs[2 * PIECES :]
    rows = mid_ref.shape[1]
    s = pl.program_id(0)
    length = len_ref[s]

    def one(r):
        here = pl.ds(r, 16)
        valid = (row_ids(r, 16) < length).astype(F32)
        middle = mid_ref[0, here, :].astype(F32)
        sums = [own[0, here, :].astype(F32) + other[0, here, :].astype(F32) for own, other in zip(owns, others)]
        grad = jnp.concatenate(sums, axis=1)
        total = cot_ref[0, here, :].astype(F32) + norm_back(middle, grad * gain_ref[...])
        grad_ref[0, here, :] = total.astype(BF16)
        attended[here, :] = (total * valid).astype(BF16)

    by_rows(rows, 16, one)
    turned_ref[...] = attended[...].T
    mixed_ref[0] = dot_nt(attended[...], wo_ref[...]).astype(BF16)


def middle_back(lengths, owns, others, mid, cot, gain, wo):
    streams, rows, model = mid.shape
    width = wo.shape[0]
    return call(
        middle_body,
        (streams,),
        [per_stream(rows, model // PIECES)] * (2 * PIECES) + [per_stream(rows, model)] * 2 + [whole((1, model)), whole(wo.shape)],
        [per_stream(rows, model), turned(rows, model), per_stream(rows, width)],
        [
            jax.ShapeDtypeStruct(mid.shape, BF16),
            jax.ShapeDtypeStruct((model, streams * rows), BF16),
            like(streams, rows, width, BF16),
        ],
        scratch=[pltpu.VMEM((rows, model), BF16)],
        prefetch=1,
        name="middle_back",
    )(lengths, *owns, *others, mid, cot, gain, wo)


def lower_body(_, *refs):
    pieces, (w_ref, part_ref) = refs[:-2], refs[-2:]
    total = None
    for c in range(3):
        more = dot_nt(jnp.concatenate([piece[c, 0] for piece in pieces], axis=1), w_ref[c])
        total = more if total is None else total + more
    part_ref[0] = total.astype(BF16)


def lower(lengths, pieces, w):
    model = w.shape[1]
    _, streams, rows, _ = pieces[0].shape
    joint = lambda a: pl.BlockSpec((3, 1, rows, a.shape[3]), lambda s, *_: (0, s, 0, 0))
    return call(
        lower_body,
        (streams,),
        [joint(a) for a in pieces] + [whole(w.shape)],
        per_stream(rows, model),
        like(streams, rows, model, BF16),
        prefetch=1,
        name="lower",
    )(lengths, *pieces, w)


def inputs_body(_, __, x_ref, own_ref, other_ref, grad_ref, gain_ref, out_ref):
    rows = x_ref.shape[1]

    def one(r):
        here = pl.ds(r, 16)
        e = (own_ref[0, here, :].astype(F32) + other_ref[0, here, :].astype(F32)) * gain_ref[...]
        out_ref[0, here, :] = grad_ref[0, here, :].astype(F32) + norm_back(x_ref[0, here, :].astype(F32), e)

    by_rows(rows, 16, one)


SLOTS = 256


def rebuild_body(len_ref, q_ref, mem_ref, old_ref, conv_ref, cot_ref, next_ref, rows_ref, branch_t_ref, wide, grad_ref):
    s = pl.program_id(0)
    rows, heads = q_ref.shape[1], q_ref.shape[2] // HD
    slots = mem_ref.shape[2]
    made = slots // 3
    valid = row_ids(0, rows) < len_ref[s]
    valid_lane = lax.broadcasted_iota(jnp.int32, (1, rows), 1) < len_ref[s]
    row = lax.broadcasted_iota(jnp.int32, (slots, HD), 0)

    @pl.when(s == 0)
    def _():
        grad_ref[...] = jnp.zeros_like(grad_ref)
        wide[...] = jnp.zeros_like(wide)

    def front(a):
        windows, packed = [], []
        for c in range(2):
            wide[a, c, :slots] = mem_ref[0, c, :, lanes_of(a)].astype(F32)
            taps = [wide[a, c, pl.ds(t, SLOTS, stride=3), :].astype(BF16) for t in range(3)]
            windows.append(jnp.concatenate(taps, axis=1))
            squeezed = dot(windows[c], conv_ref[a, c].reshape(3 * HD, HD))
            packed.append(squeezed.astype(BF16))
            tail = jnp.concatenate([squeezed, jnp.zeros((slots - SLOTS, HD), F32)], axis=0)
            kept = pltpu.roll(old_ref[0, c, :, lanes_of(a)].astype(F32), slots - made, 0)
            tail = pltpu.roll(tail, slots - made, 0)
            next_ref[0, c, :, lanes_of(a)] = jnp.where(row < slots - made, kept, tail).astype(BF16)
        q = q_ref[0, :, lanes_of(a)]
        return windows, packed, dot_nt(mem_ref[0, 0, :, lanes_of(a)], q), dot_nt(packed[0], q)

    def soft(scores, count):
        start = count // 8 * 8
        key = start + lax.broadcasted_iota(jnp.int32, (scores.shape[0] - start, rows), 0)
        last = jnp.where(key < count, scores[start:], -1e30)
        scores = jnp.concatenate([scores[:start], last], axis=0)
        weights = jnp.exp2((scores - jnp.max(scores, axis=0, keepdims=True)) * BASE2)
        return weights, 1.0 / jnp.sum(weights, axis=0, keepdims=True)

    def rest(a, windows, packed, scores, few_scores):
        weights, share = soft(few_scores, made)
        probs = weights * share
        low = probs.astype(BF16)
        approach = dot(packed[1].T, low)
        weights, share = soft(scores, 3 * made)
        target = dot(mem_ref[0, 1, :, lanes_of(a)].T, weights.astype(BF16)) * share
        grad = jnp.where(valid_lane, (approach - target) * (2.0 / rows), 0.0).astype(BF16)
        grad_probs = dot(packed[1], grad)
        inner = jnp.sum(probs * grad_probs, axis=0, keepdims=True)
        grad_scores = (probs * (grad_probs - inner) * HEAD_SCALE).astype(BF16)
        back = [dot(grad_scores, q_ref[0, :, lanes_of(a)]), dot_nt(low, grad)]
        for c in range(2):
            grad_ref[a, c] += dot_tn(windows[c], back[c].astype(BF16)).reshape(3, HD, HD)

    pipelined([(a,) for a in range(heads)], front, rest)
    branch_t_ref[...] = jnp.where(valid, cot_ref[0], jnp.zeros_like(cot_ref[0])).T

    @pl.when(s == pl.num_programs(0) - 1)
    def _():
        ranks, deep, _ = rows_ref.shape
        share = HD // ranks
        rows_ref[...] = jnp.zeros_like(rows_ref)
        for a in range(heads):
            for n in range(6):
                piece = 6 * a + n
                at, group = piece % (deep // share) * share, piece // (deep // share)
                rows_ref[:, at : at + share, group * HD : (group + 1) * HD] = grad_ref[a, n // 3, n % 3].reshape(ranks, share, HD)


def rebuild(lengths, q, memory, compressed, conv, cot, ranks, columns):
    model = cot.shape[2]
    streams, rows, width = q.shape
    heads = width // HD
    slots = memory.shape[2]
    cache = pl.BlockSpec((1, 2, slots, width), lambda s, *_: (s, 0, 0, 0))
    return call(
        rebuild_body,
        (streams,),
        [per_stream(rows, width), cache, cache, whole(conv.shape), per_stream(rows, model)],
        [cache, pl.BlockSpec((ranks, model // ranks, columns), lambda *_: (0, 0, 0)), turned(rows, model)],
        [
            jax.ShapeDtypeStruct(compressed.shape, BF16),
            jax.ShapeDtypeStruct((ranks, model // ranks, columns), F32),
            jax.ShapeDtypeStruct((model, streams * rows), BF16),
        ],
        scratch=[pltpu.VMEM((heads, 2, 3 * SLOTS, HD), F32), pltpu.VMEM(conv.shape, F32)],
        prefetch=1,
        cover=True,
        name="rebuild",
    )(lengths, q, memory, compressed, conv, cot)


def per_device(
    inputs,
    cotangent,
    lengths,
    memory,
    compressed,
    query_key_value_weight,
    output_weight,
    up_weight,
    down_weight,
    gain_one,
    gain_two,
    slope_rates,
    conv_weight,
):
    streams, rows, model = inputs.shape
    tokens = streams * rows
    heads = slope_rates.shape[0]
    width = heads * HD
    ranks = lax.axis_size("dp")
    rank_bits = bits_of(ranks)
    me = lax.axis_index("dp").astype(jnp.int32)
    me_array = me.reshape(1)
    later = tuple(range(2, rank_bits))
    x_first, x_then_z, y_then_z = (0, 1) + later, (0,) + later + (1,), (1,) + later + (0,)
    y_then_mixed = (1, 2, 0) + later[1:]
    gain_1, gain_2 = gain_one.reshape(1, model), gain_two.reshape(1, model)
    qkv = query_key_value_weight.transpose(1, 0, 2)

    normed_t, q, memory_next = project(lengths, inputs, gain_1, qkv)
    mixed, exact, lse, part = attend(lengths, slope_rates, q, compressed, memory, memory_next, output_weight)
    own, other = pair_over_head(part)
    step = min(512, up_weight.shape[1])
    compressed_next, conv, branch_t = rebuild(after(lengths, part), q, memory, compressed, conv_weight, cotangent, ranks, step)
    conv = conv.reshape(model, step)
    mid, normed_two_t, active, before = rise(after(lengths, conv), inputs, own, other, gain_2, up_weight)
    sources = [(branch_t, active.reshape(tokens, -1)), (None, conv)]
    keep, send = weight_gradient(me_array, x_then_z, sources, step, "grad_down")
    down = Halving(keep, send, x_then_z, ranks, cut=up_weight.shape[1])
    grad_hidden, *backs = fall(after(lengths, send), cotangent, before, up_weight, down_weight)
    owns, others = zip(*[pair_over_head(back) for back in backs])
    keep, send = weight_gradient(me_array, y_then_z, [(normed_two_t, grad_hidden.reshape(tokens, -1))], step, "grad_up")
    up = Halving(keep, send, y_then_z, ranks)
    grad_middle, attended_t, grad_mixed = middle_back(
        after(lengths, send), owns, others, mid, cotangent, gain_2, output_weight
    )
    token = advance([down], grad_mixed)

    groups = 2 if heads % 2 == 0 else 1
    each = heads // groups
    pieces, sides, rounds = [], [], []
    for g in range(groups):
        piece, slopes = attend_back(
            g * each, each, after(lengths, token), slope_rates, q, compressed, memory, memory_next, exact, lse, grad_mixed
        )
        pieces.append(piece)
        sides.append(slopes)
        order = x_first if g else y_then_mixed
        sources = [(normed_t, piece.reshape(3, tokens, each * HD))]
        if g == 0:
            sources.append((attended_t, mixed.reshape(tokens, width)))
        final = g == groups - 1
        token = piece
        if final:
            part = lower(after(lengths, token), pieces, qkv)
            own, other = pair_over_head(part)
            token = part
        made = weight_gradient(after(me_array, token), order, sources, each * HD, "grad_joint", sides if final else ())
        keep, send = made[:2]
        rounds.append(Halving(keep, send, order, ranks, made[2] if final else None))
        token = advance([up, down], send) if g == 0 else send
    early, late = rounds[0], rounds[-1]
    both = rounds[::-1]

    token = advance([early, up, down] if groups > 1 else [up, down], token)
    branch = leave(after(lengths, token), active, down_weight)
    token = advance([late, down], branch)
    branch, branch_other = pair_over_head(after(branch, token))
    grad_inputs, outputs = None, None
    parts = 2 if streams % 2 == 0 else 1
    count = streams // parts
    for p in range(parts):
        grad_inputs = in_part(
            inputs_body, p * count, count, grad_inputs, after(lengths, token), [inputs, own, other, grad_middle], gain_1, mid, "inputs_back"
        )
        token = advance(both + ([] if p else [up]), grad_inputs)
    up.send(after(up.sent, token))
    spans = [(0, streams - 1), (streams - 1, 1)] if streams > 1 else [(0, 1)]
    for first, count in spans:
        if first + count == streams:
            unfinished = lambda: [r for r in both + [up] if r.stage + 1 < len(r.order)] + [r for r in [down] if r.total is None]
            while unfinished():
                token = advance(unfinished(), token)
            total_qkv, total_out, slopes, total_up, gains = finish(me_array, rounds, up, token, each * HD, qkv, up_weight)
            token = total_qkv
        outputs = in_part(
            outputs_body, first, count, outputs, after(lengths, token), [mid, branch, branch_other], None, mid, "outputs"
        )
        token = outputs

    total_down, conv_rows = down.total
    total_conv = conv_share(conv_rows, conv_weight, ranks, model)
    portion = model // ranks
    mine = lambda a: lax.dynamic_slice_in_dim(a, me * portion, portion, 0)
    head_count = lax.axis_size("head")
    for bit in range(bits_of(head_count)):
        gains = gains + lax.ppermute(gains, "head", flip_pairs(head_count, bit))
    total_gain_one = gains[0, :portion] / mine(gain_one)
    total_gain_two = gains[1, :portion] / mine(gain_two)

    return (
        outputs,
        grad_inputs,
        memory_next,
        compressed_next,
        total_qkv.transpose(1, 0, 2),
        total_out.T,
        total_up,
        total_down.T,
        total_gain_one,
        total_gain_two,
        slopes[:heads, 0],
        total_conv,
    )


def solution(mesh):
    placed = (
        P("dp", None, None),
        P("dp", None, None),
        P("dp"),
        P("dp", None, None, "head"),
        P("dp", None, None, "head"),
        P(None, None, "head"),
        P("head", None),
        P(None, "head"),
        P("head", None),
        P(),
        P(),
        P("head"),
        P("head", None, None, None, None),
    )
    return jax.shard_map(
        per_device,
        mesh=mesh,
        in_specs=placed,
        out_specs=(
            P("dp", None, None),
            P("dp", None, None),
            P("dp", None, None, "head"),
            P("dp", None, None, "head"),
            P("dp", None, "head"),
            P("head", "dp"),
            P("dp", "head"),
            P("head", "dp"),
            P("dp"),
            P("dp"),
            P("head"),
            P("head", None, None, "dp", None),
        ),
        check_vma=False,
    )
```

```python
import functools
import math

import jax
import jax.numpy as jnp
from jax import lax
from jax.experimental import pallas as pl
from jax.experimental.pallas import tpu as pltpu
from jax.sharding import PartitionSpec as P

HD = 128
CE = 170
EPS = 1e-05
LOG2E = 1.0 / math.log(2.0)
HEAD_SCALE = 1.0 / math.sqrt(HD)
BASE2 = HEAD_SCALE * LOG2E
F32 = jnp.float32
BF16 = jnp.bfloat16
KEEP = BF16
VMEM_LIMIT = 67043328


def bits_of(count):
    return count.bit_length() - 1


def flip_pairs(count, bit):
    return [(i, i ^ (1 << bit)) for i in range(count)]


def call(body, grid, in_specs, out_specs, out_shape, scratch=(), prefetch=0, cover=False, name=None, aliases=None):
    return pl.pallas_call(
        body,
        grid_spec=pltpu.PrefetchScalarGridSpec(
            num_scalar_prefetch=prefetch,
            grid=grid,
            in_specs=in_specs,
            out_specs=out_specs,
            scratch_shapes=list(scratch),
        ),
        out_shape=out_shape,
        input_output_aliases=aliases or {},
        compiler_params=pltpu.CompilerParams(dimension_semantics=("arbitrary",) * len(grid), vmem_limit_bytes=VMEM_LIMIT),
        cost_estimate=pl.CostEstimate(flops=10**13 if cover else 0, bytes_accessed=0, transcendentals=0),
        name=name,
    )


def whole(shape):
    zeros = (0,) * len(shape)
    return pl.BlockSpec(shape, lambda *_: zeros, pipeline_mode=pl.Buffered(1))


def per_stream(rows, n):
    return pl.BlockSpec((1, rows, n), lambda s, *_: (s, 0, 0))


def turned(rows, n):
    return pl.BlockSpec((n, rows), lambda s, *_: (0, s))


def like(streams, rows, n, kind):
    return jax.ShapeDtypeStruct((streams, rows, n), kind)


def dot(a, b):
    return jnp.dot(a, b, preferred_element_type=F32)


def dot_nt(a, b):
    return lax.dot_general(a, b, (((1,), (1,)), ((), ())), preferred_element_type=F32)


def dot_tn(a, b):
    return lax.dot_general(a, b, (((0,), (0,)), ((), ())), preferred_element_type=F32)


def statistics(v):
    centred = v - jnp.mean(v, axis=-1, keepdims=True)
    spread = jnp.mean(centred * centred, axis=-1, keepdims=True)
    return centred, lax.rsqrt(spread + EPS)


def norm_back(v, e):
    centred = v - jnp.mean(v, axis=-1, keepdims=True)
    spread = jnp.mean(centred * centred, axis=-1, keepdims=True)
    middle = jnp.mean(e, axis=-1, keepdims=True)
    along = jnp.mean(e * centred, axis=-1, keepdims=True)
    scale = lax.rsqrt(spread + EPS)
    return scale * (e - middle - centred * (scale * scale * along))


def by_rows(rows, step, body, together=8):
    def one(i, carry):
        for j in range(together):
            body(pl.multiple_of((i * together + j) * step, step))
        return carry

    if rows == step * together:
        for j in range(together):
            body(j * step)
    else:
        lax.fori_loop(0, rows // (step * together), one, 0)


def row_ids(start, step):
    return start + lax.broadcasted_iota(jnp.int32, (step, 1), 0)


def project_body(len_ref, x_ref, gain_ref, w_ref, normed_t_ref, q_ref, kv_ref, normed_ref):
    rows = q_ref.shape[1]
    length = len_ref[pl.program_id(0)]

    def norm(r):
        centred, scale = statistics(x_ref[0, pl.ds(r, 16), :].astype(F32))
        normed_ref[pl.ds(r, 16), :] = (centred * scale * gain_ref[...]).astype(BF16)

    by_rows(rows, 16, norm, rows // 16)
    normed_t_ref[...] = normed_ref[...].T
    valid = row_ids(0, rows) < length
    normed = normed_ref[...]
    q_ref[0] = dot(normed, w_ref[0]).astype(BF16)
    for c in range(2):
        now = dot(normed, w_ref[c + 1])
        kv_ref[0, c] = jnp.where(valid, now, 0.0).astype(BF16)


def project(lengths, x, gain, w):
    streams, rows, model = x.shape
    width = w.shape[2]
    per = lambda *tail: pl.BlockSpec((1,) + tail, lambda s, *_: (s,) + (0,) * len(tail))
    return call(
        project_body,
        (streams,),
        [per(rows, model), whole((1, model)), whole(w.shape)],
        [pl.BlockSpec((model, rows), lambda s, *_: (0, s)), per(rows, width), per(2, rows, width)],
        [
            jax.ShapeDtypeStruct((model, streams * rows), BF16),
            jax.ShapeDtypeStruct((streams, rows, width), BF16),
            jax.ShapeDtypeStruct((streams, 2, rows, width), BF16),
        ],
        scratch=[pltpu.VMEM((rows, model), BF16)],
        prefetch=1,
        name="project",
    )(lengths, x, gain, w)


def position_columns(keys):
    centre = keys // 2
    lane = lax.broadcasted_iota(jnp.int32, (keys, HD), 1)
    place = lax.broadcasted_iota(jnp.int32, (keys, HD), 0) - centre
    fine = place & 7
    coarse = place - fine
    value = jnp.where(lane < 6, jnp.where((lane & 1) == 0, coarse, fine), jnp.where(lane == 6, 1, 0))
    return value.astype(F32).astype(BF16)


def slope_columns(slope, rows):
    exact = jnp.full((8, HD), slope, F32) * (1.0 / HEAD_SCALE)
    first = exact.astype(BF16).astype(F32)
    second = (exact - first).astype(BF16).astype(F32)
    third = exact - first - second
    lane = lax.broadcasted_iota(jnp.int32, (8, HD), 1)
    value = jnp.where(lane < 2, first, jnp.where(lane < 4, second, jnp.where(lane < 6, third, 0.0)))
    return jnp.broadcast_to(value[:1], (rows, HD)).astype(BF16)


def one_column(keys):
    lane = lax.broadcasted_iota(jnp.int32, (keys, HD), 1)
    return jnp.where(lane == 0, 1.0, 0.0).astype(BF16)


def diagonal_mask(block, start, length):
    row = lax.broadcasted_iota(jnp.int32, (block, block), 0)
    col = lax.broadcasted_iota(jnp.int32, (block, block), 1)
    return col <= jnp.minimum(row, length - 1 - start)


def pipelined(chains, front, rest):
    following = front(*chains[0])
    for n, chain in enumerate(chains):
        current = following
        if n + 1 < len(chains):
            following = front(*chains[n + 1])
        rest(*chain, *current)


def lanes_of(a):
    return slice(a * HD, (a + 1) * HD)


def attend_body(len_ref, slope_ref, q_ref, old_ref, mem_ref, now_ref, wo_ref, mix_ref, exact_ref, lse_ref, part_ref, kbuf, vbuf):
    s = pl.program_id(0)
    rows, heads = q_ref.shape[1], q_ref.shape[2] // HD
    old, mem = old_ref.shape[2], mem_ref.shape[2]
    past = old + mem
    keys = past + rows
    block = rows // 2
    length = len_ref[s]

    @pl.when(s == 0)
    def _():
        for a in range(heads):
            kbuf[a, :, HD:] = position_columns(keys)
            vbuf[a, :, HD:] = one_column(keys)

    for a in range(heads):
        for buf, c in ((kbuf, 0), (vbuf, 1)):
            buf[a, :old, :HD] = old_ref[0, c, :, lanes_of(a)]
            buf[a, old:past, :HD] = mem_ref[0, c, :, lanes_of(a)]
            buf[a, past:, :HD] = now_ref[0, c, :, lanes_of(a)]

    def front(a, i):
        side = slope_columns(slope_ref[a], block)
        wide = jnp.concatenate([q_ref[0, i * block : (i + 1) * block, lanes_of(a)], side], axis=1)
        return (dot_nt(wide, kbuf[a, : past + (i + 1) * block]),)

    def rest(a, i, scores):
        high = (i + 1) * block
        here = slice(i * block, high)
        allowed = diagonal_mask(block, i * block, length)
        last = jnp.where(allowed, scores[:, past + i * block :], -1e30)
        scores = jnp.concatenate([scores[:, : past + i * block], last], axis=1)
        top = jnp.max(scores, axis=1, keepdims=True)
        weights = jnp.exp2((scores - top) * BASE2).astype(BF16)
        both = dot(weights, vbuf[a, : past + high])
        total = both[:, HD : HD + 1]
        mixed = both[:, :HD] / total
        exact_ref[0, here, lanes_of(a)] = mixed
        mix_ref[0, here, lanes_of(a)] = mixed.astype(BF16)
        lse_ref[0, here, lanes_of(a)] = jnp.broadcast_to(top * BASE2 + jnp.log2(total), (block, HD))

    @pl.when(length > block)
    def _():
        pipelined([(a, i) for a in range(heads) for i in range(2)], front, rest)

    @pl.when(length <= block)
    def _():
        pipelined([(a, 0) for a in range(heads)], front, rest)
        exact_ref[0, block:, :] = jnp.zeros((rows - block, heads * HD), F32)
        mix_ref[0, block:, :] = jnp.zeros((rows - block, heads * HD), BF16)
        lse_ref[0, block:, :] = jnp.zeros((rows - block, heads * HD), F32)

    part_ref[0] = dot(mix_ref[0], wo_ref[...]).astype(BF16)


def attend(lengths, slopes, q, compressed, memory, now, wo):
    streams, rows, width = q.shape
    heads = width // HD
    model = wo.shape[1]
    keys = compressed.shape[2] + memory.shape[2] + rows
    cache = lambda a: pl.BlockSpec((1, 2, a.shape[2], width), lambda s, *_: (s, 0, 0, 0))
    return call(
        attend_body,
        (streams,),
        [per_stream(rows, width), cache(compressed), cache(memory), cache(now), whole(wo.shape)],
        [per_stream(rows, width), per_stream(rows, width), per_stream(rows, width), per_stream(rows, model)],
        [
            jax.ShapeDtypeStruct((streams, rows, width), BF16),
            jax.ShapeDtypeStruct((streams, rows, width), F32),
            jax.ShapeDtypeStruct((streams, rows, width), F32),
            jax.ShapeDtypeStruct((streams, rows, model), BF16),
        ],
        scratch=[pltpu.VMEM((heads, keys, 2 * HD), BF16), pltpu.VMEM((heads, keys, 2 * HD), BF16)],
        prefetch=2,
        name="attend",
    )(lengths, slopes, q, compressed, memory, now, wo)


def attend_back_body(first, len_ref, slope_ref, q_ref, old_ref, mem_ref, now_ref, exact_ref, lse_ref, grad_ref, out_ref, slope_out_ref, kbuf, vbuf):
    s = pl.program_id(0)
    rows, heads = q_ref.shape[1], q_ref.shape[2] // HD
    old, mem = old_ref.shape[2], mem_ref.shape[2]
    past = old + mem
    keys = past + rows
    block = rows // 2
    length = len_ref[s]

    @pl.when(s == 0)
    def _():
        for a in range(heads):
            kbuf[a, :, HD:] = position_columns(keys)
        slope_out_ref[...] = jnp.zeros_like(slope_out_ref)

    for a in range(heads):
        kbuf[a, :old, :HD] = old_ref[0, 0, :, lanes_of(a)]
        kbuf[a, old:past, :HD] = mem_ref[0, 0, :, lanes_of(a)]
        kbuf[a, past:, :HD] = now_ref[0, 0, :, lanes_of(a)]
        vbuf[a, :old] = old_ref[0, 1, :, lanes_of(a)]
        vbuf[a, old:past] = mem_ref[0, 1, :, lanes_of(a)]
        vbuf[a, past:] = now_ref[0, 1, :, lanes_of(a)]

    def here(i):
        return slice(i * block, (i + 1) * block)

    def front(a, i):
        side = slope_columns(slope_ref[first + a], block)
        wide = jnp.concatenate([q_ref[0, here(i), lanes_of(a)], side], axis=1)
        reach = past + (i + 1) * block
        return dot_nt(wide, kbuf[a, :reach]), dot_nt(grad_ref[0, here(i), lanes_of(a)], vbuf[a, :reach])

    def run(blocks):
        sums = {}

        def rest(a, i, scores, grad_probs):
            reach = past + (i + 1) * block
            q, grad = q_ref[0, here(i), lanes_of(a)], grad_ref[0, here(i), lanes_of(a)]
            exact = jnp.exp2(scores * BASE2 - lse_ref[0, here(i), a * HD : a * HD + 1])
            allowed = diagonal_mask(block, i * block, length)
            last = jnp.where(allowed, exact[:, reach - block :], 0.0)
            exact = jnp.concatenate([exact[:, : reach - block], last], axis=1)
            inner = jnp.sum(grad.astype(F32) * exact_ref[0, here(i), lanes_of(a)], axis=1, keepdims=True)
            grad_scores = (exact * (grad_probs - inner)).astype(BF16)
            wide = dot(grad_scores, kbuf[a, :reach])
            out_ref[0, 0, here(i), lanes_of(a)] = (wide[:, :HD] * HEAD_SCALE).astype(BF16)
            coarse, fine, total = (wide[:, HD + n : HD + n + 1] for n in (0, 1, 6))
            distance = (past + i * block - keys // 2 + lax.broadcasted_iota(jnp.int32, (block, 1), 0)).astype(F32)
            moment = jnp.sum(coarse + fine - distance * total, axis=0, keepdims=True)
            grad_keys = dot_tn(grad_scores[:, past:], q)
            grad_values = dot_tn(exact[:, past:].astype(BF16), grad)
            if i > 0:
                moment = moment + sums[a][0]
                done = sums[a][1].shape[0]
                join = lambda before, now: jnp.concatenate([before + now[:done], now[done:]], axis=0)
                grad_keys, grad_values = join(sums[a][1], grad_keys), join(sums[a][2], grad_values)
            sums[a] = moment, grad_keys, grad_values
            if i == blocks - 1:
                high = blocks * block
                out_ref[1, 0, :high, lanes_of(a)] = (grad_keys * HEAD_SCALE).astype(BF16)
                out_ref[2, 0, :high, lanes_of(a)] = grad_values.astype(BF16)
                slope_out_ref[first + a : first + a + 1, :] += jnp.broadcast_to(moment, (1, HD))

        pipelined([(a, i) for a in range(heads) for i in range(blocks)], front, rest)

    @pl.when(length > block)
    def _():
        run(2)

    @pl.when(length <= block)
    def _():
        run(1)
        for c in range(3):
            out_ref[c, 0, block:, :] = jnp.zeros((rows - block, heads * HD), BF16)


def attend_back(first, heads, lengths, slopes, q, compressed, memory, now, exact, lse, grad):
    streams, rows, width = q.shape
    keys = compressed.shape[2] + memory.shape[2] + rows
    group = first // heads
    cache = lambda a: pl.BlockSpec((1, 2, a.shape[2], heads * HD), lambda s, *_: (s, 0, 0, group))
    some = pl.BlockSpec((1, rows, heads * HD), lambda s, *_: (s, 0, group))
    return call(
        functools.partial(attend_back_body, first),
        (streams,),
        [some, cache(compressed), cache(memory), cache(now), some, some, some],
        [pl.BlockSpec((3, 1, rows, heads * HD), lambda s, *_: (0, s, 0, 0)), pl.BlockSpec((8, HD), lambda *_: (0, 0))],
        [jax.ShapeDtypeStruct((3, streams, rows, heads * HD), BF16), jax.ShapeDtypeStruct((8, HD), F32)],
        scratch=[pltpu.VMEM((heads, keys, 2 * HD), BF16), pltpu.VMEM((heads, keys, HD), BF16)],
        prefetch=2,
        cover=True,
        name="attend_back",
    )(lengths, slopes, q, compressed, memory, now, exact, lse, grad)


GELU_K = math.sqrt(2.0 / math.pi)
GELU_C = 0.044715


def gate_of(v):
    square = v * v
    rate = -2.0 * GELU_K * LOG2E
    return 1.0 / (1.0 + jnp.exp2(v * (rate + (rate * GELU_C) * square))), square


def gelu_slope(v):
    gate, square = gate_of(v)
    lean = v * (2.0 * GELU_K + (6.0 * GELU_K * GELU_C) * square)
    return gate * (1.0 + lean * (1.0 - gate))


def rise_body(len_ref, x_ref, own_ref, other_ref, gain_ref, up_ref, mid_ref, normed_t_ref, active_ref, before_ref, normed):
    rows = x_ref.shape[1]
    hidden_width = up_ref.shape[1]
    length = len_ref[pl.program_id(0)]

    def norm(r):
        here = pl.ds(r, 16)
        valid = (row_ids(r, 16) < length).astype(F32)
        attended = own_ref[0, here, :].astype(F32) + other_ref[0, here, :].astype(F32)
        middle = x_ref[0, here, :].astype(F32) + attended * valid
        mid_ref[0, here, :] = middle.astype(BF16)
        centred, scale = statistics(middle)
        normed[here, :] = (centred * scale * gain_ref[...]).astype(BF16)

    by_rows(rows, 16, norm, rows // 16)
    normed_t_ref[...] = normed[...].T
    chunk = min(512, hidden_width)
    columns = [slice(f, f + chunk) for f in range(0, hidden_width, chunk)]

    def front(cols):
        return (dot(normed[...], up_ref[:, cols]),)

    def rest(cols, v):
        active_ref[0, :, cols] = (v * gate_of(v)[0]).astype(BF16)
        before_ref[0, :, cols] = v.astype(BF16)

    pipelined([(cols,) for cols in columns], front, rest)


def rise(lengths, x, own, other, gain, up):
    streams, rows, model = x.shape
    hidden = up.shape[1]
    tokens = streams * rows
    return call(
        rise_body,
        (streams,),
        [per_stream(rows, model)] * 3 + [whole((1, model)), whole(up.shape)],
        [per_stream(rows, model), turned(rows, model), per_stream(rows, hidden), per_stream(rows, hidden)],
        [
            like(streams, rows, model, BF16),
            jax.ShapeDtypeStruct((model, tokens), BF16),
            like(streams, rows, hidden, BF16),
            like(streams, rows, hidden, BF16),
        ],
        scratch=[pltpu.VMEM((rows, model), BF16)],
        prefetch=1,
        name="rise",
    )(lengths, x, own, other, gain, up)


def fall_body(len_ref, cot_ref, before_ref, up_ref, down_ref, hidden_ref, *back_refs):
    rows = cot_ref.shape[1]
    hidden_width = up_ref.shape[1]
    valid = row_ids(0, rows) < len_ref[pl.program_id(0)]
    branch = jnp.where(valid, cot_ref[0].astype(F32), 0.0).astype(BF16)
    chunk = min(1024, hidden_width)
    back = []

    def front(cols):
        return (dot_nt(branch, down_ref[cols, :]),)

    def rest(cols, grad_active):
        grad_hidden = (grad_active * gelu_slope(before_ref[0, :, cols].astype(F32))).astype(BF16)
        hidden_ref[0, :, cols] = grad_hidden
        back.append(dot_nt(grad_hidden, up_ref[:, cols]))

    pipelined([(slice(f, f + chunk),) for f in range(0, hidden_width, chunk)], front, rest)
    total = sum(back[1:], back[0]).astype(BF16)
    part = total.shape[1] // len(back_refs)
    for n, back_ref in enumerate(back_refs):
        back_ref[0] = total[:, n * part : (n + 1) * part]


PIECES = 4


def fall(lengths, cot, slope, up, down):
    streams, rows, model = cot.shape
    hidden = up.shape[1]
    tokens = streams * rows
    return call(
        fall_body,
        (streams,),
        [per_stream(rows, model), per_stream(rows, hidden), whole(up.shape), whole(down.shape)],
        [per_stream(rows, hidden)] + [per_stream(rows, model // PIECES)] * PIECES,
        [like(streams, rows, hidden, BF16)] + [like(streams, rows, model // PIECES, BF16)] * PIECES,
        prefetch=1,
        name="fall",
    )(lengths, cot, slope, up, down)


def leave_body(_, active_ref, down_ref, part_ref):
    part_ref[0] = dot(active_ref[0], down_ref[...]).astype(BF16)


def leave(lengths, active, down):
    streams, rows, hidden = active.shape
    model = down.shape[1]
    return call(
        leave_body,
        (streams,),
        [per_stream(rows, hidden), whole(down.shape)],
        per_stream(rows, model),
        like(streams, rows, model, BF16),
        prefetch=1,
        cover=True,
        name="leave",
    )(lengths, active, down)


def outputs_body(start, len_ref, mid_ref, own_ref, other_ref, out_ref):
    rows = mid_ref.shape[1]
    length = len_ref[start + pl.program_id(0)]

    def one(r):
        here = pl.ds(r, 16)
        valid = (row_ids(r, 16) < length).astype(F32)
        branch = own_ref[0, here, :].astype(F32) + other_ref[0, here, :].astype(F32)
        out_ref[0, here, :] = mid_ref[0, here, :].astype(F32) + valid * branch

    by_rows(rows, 16, one, 4)


def in_part(body, first, count, into, lengths, args, gain, like_this, name):
    rows, model = like_this.shape[1:]
    per = pl.BlockSpec((1, rows, model), lambda s, *_: (s + first, 0, 0))
    extra = [] if gain is None else [whole(gain.shape)]
    held = [] if into is None else [into]

    def inner(len_ref, *refs):
        body(first, len_ref, *refs[: len(args) + len(extra)], refs[-1])

    return call(
        inner,
        (count,),
        [per] * len(args) + extra + [pl.BlockSpec(memory_space=pl.ANY)] * len(held),
        per,
        jax.ShapeDtypeStruct(like_this.shape, F32),
        prefetch=1,
        cover=first > 0 or gain is None,
        aliases={1 + len(args) + len(extra): 0} if held else {},
        name=name,
    )(lengths, *args, *([] if gain is None else [gain]), *held)


def chunk_at(place, order, me):
    apart = 0
    for i, bit in enumerate(order):
        apart |= ((place >> (len(order) - 1 - i)) & 1) << bit
    return apart ^ me


def send_order(source, order, me, first, count):
    deep = source.shape[0] // (1 << len(order))
    lines = []
    for p in range(first, first + count):
        lines.append(source[pl.ds(pl.multiple_of(chunk_at(p, order, me) * deep, deep), deep), :])
    return jnp.concatenate(lines, axis=0)


def weight_body(spans, extra, order, me_ref, *refs):
    products = sum(span[2] for span in spans)
    xts, ys = list(refs[:products]), refs[products : products + len(spans)]
    sides, outs = refs[products + len(spans) :], refs[-3 if extra else -2 :]
    sides, keep_ref, send_ref = sides[: -len(outs)], outs[0], outs[1]
    me = me_ref[0]
    j = pl.program_id(0)
    places = 1 << len(order)
    half = keep_ref.shape[0]
    for y, (start, stop, product) in zip(ys, spans):
        xt = xts.pop(0) if product else None

        @pl.when((j >= start) & (j < stop))
        def _(xt=xt, y=y):
            for n, out in enumerate((keep_ref, send_ref)):
                rows = send_order(y if xt is None else xt, order, me, n * places // 2, places // 2)
                if xt is not None:
                    rows = dot(rows, y[...] if len(y.shape) == 2 else y[0])
                out[:half, :] = rows.astype(out.dtype)

    if extra:
        total = sum(side[...] for side in sides)
        first = total.astype(BF16).astype(F32)
        both = jnp.concatenate([first, total - first], axis=0).astype(BF16)
        times = send_ref.shape[1] // HD
        send_ref[half:, :] = jnp.concatenate([both] * times, axis=1)
        outs[2][...] = jnp.concatenate([total] * times, axis=1)


def weight_gradient(me, order, sources, step, name, sides=()):
    xts = [xt for xt, _ in sources if xt is not None]
    model, tokens = xts[0].shape
    spans, specs, at = [], [], 0
    for xt, y in sources:
        n = y.shape[-1] // step
        blocks = n * (y.shape[0] if y.ndim == 3 else 1)
        spans.append((at, at + blocks, xt is not None))
        if y.ndim == 3:
            pick = lambda j, *_, at=at, n=n, blocks=blocks: (jnp.clip(j - at, 0, blocks - 1) // n, 0, jnp.clip(j - at, 0, blocks - 1) % n)
            specs.append(pl.BlockSpec((1, y.shape[1], step), pick))
        else:
            specs.append(pl.BlockSpec((y.shape[0], step), lambda j, *_, at=at, blocks=blocks: (0, jnp.clip(j - at, 0, blocks - 1))))
        at += blocks
    columns = at * step
    extra = 16 if sides else 0
    heights = (model // 2, model // 2 + extra) + ((8,) if sides else ())
    return call(
        functools.partial(weight_body, spans, extra, order),
        (at,),
        [whole(xt.shape) for xt in xts] + specs + [whole(side.shape) for side in sides],
        [pl.BlockSpec((n, step), lambda j, *_: (0, j)) for n in heights],
        [jax.ShapeDtypeStruct((n, columns), kind) for n, kind in zip(heights, (KEEP, BF16, F32))],
        prefetch=1,
        name=name,
    )(me, *xts, *[y for _, y in sources], *sides)


class Halving:
    def __init__(self, keep, send, order, count, side=None, cut=None):
        self.order, self.count, self.stage, self.total = order, count, 0, None
        self.cuts = (0, cut or keep.shape[1], keep.shape[1])
        self.keep, self.side = keep, side
        self.send(send)

    def send(self, what):
        self.sent = what
        self.came = lax.ppermute(what, "dp", flip_pairs(self.count, self.order[self.stage]))


def sum_of(keep, came, rows, columns=slice(None)):
    return keep[rows, columns].astype(F32) + came[rows, columns].astype(F32)


def side_sum(before, came, high):
    both = came[high:, :].astype(F32)
    return before[...] + (both[:8] + both[8:])


def advance_body(items, *refs):
    refs = list(refs)
    ins = [[refs.pop(0) for _ in range(3 if side else 2)] for _, side in items]
    for (cuts, side), (keep, came, *before) in zip(items, ins):
        high = keep.shape[0]
        half = high // 2
        if cuts:
            parts = [(refs.pop(0), slice(a, b)) for a, b in zip(cuts, cuts[1:]) if a < b]

            @pl.when(pl.program_id(0) == 0)
            def _(keep=keep, came=came, parts=parts, high=high):
                for out, columns in parts:
                    out[...] = sum_of(keep, came, slice(0, high), columns)

        else:
            stay, go = refs.pop(0), refs.pop(0)
            stay[...] = sum_of(keep, came, slice(0, half)).astype(stay.dtype)
            go[:half, :] = sum_of(keep, came, slice(half, high)).astype(BF16)
            if side:
                total = side_sum(before[0], came, high)
                refs.pop(0)[...] = total
                first = total.astype(BF16).astype(F32)
                go[half:, :] = jnp.concatenate([first, total - first], axis=0).astype(BF16)


def advance(rounds, token):
    rounds = [r for r in rounds if r.total is None]
    if not rounds:
        return token
    turns = 4 if all(r.keep.shape[1] % (4 * HD) == 0 for r in rounds) else 2
    blocks = lambda a: pl.BlockSpec((a.shape[0], a.shape[1] // turns), lambda j: (0, j))
    items, args, outs, in_specs, out_specs = [], [], [], [], []
    for r in rounds:
        final, side = r.stage + 1 == len(r.order), r.side is not None
        high, columns = r.keep.shape
        items.append((r.cuts if final else None, side))
        mine = [r.keep, after(r.came, token)] + ([r.side] if side else [])
        if final:
            made = [jax.ShapeDtypeStruct((high, b - a), F32) for a, b in zip(r.cuts, r.cuts[1:]) if a < b]
        else:
            made = [
                jax.ShapeDtypeStruct((high // 2, columns), KEEP),
                jax.ShapeDtypeStruct((high // 2 + (16 if side else 0), columns), BF16),
            ] + ([jax.ShapeDtypeStruct(r.side.shape, F32)] if side else [])
        args += mine
        outs += made
        in_specs += [whole(a.shape) if final else blocks(a) for a in mine]
        out_specs += [pl.BlockSpec(a.shape, lambda j: (0, 0)) if final else blocks(a) for a in made]
    got = list(call(functools.partial(advance_body, items), (turns,), in_specs, out_specs, outs, name="advance")(*args))
    token = got[0]
    for r, (cuts, side) in zip(rounds, items):
        r.stage += 1
        if cuts:
            r.total = [got.pop(0) for a, b in zip(cuts, cuts[1:]) if a < b]
            continue
        r.keep, send = got.pop(0), got.pop(0)
        if side:
            r.side = got.pop(0)
        r.send(send)
    return token


def finish_body(share, _, *refs):
    *ins, before, keep_up, came_up, w_ref, up_w_ref, qkv_ref, out_ref, side_ref, up_ref, gain_ref = refs
    high = keep_up.shape[0]
    rows = slice(0, high)
    for g in range(len(ins) // 2):
        keep, came = ins[2 * g], ins[2 * g + 1]
        for c in range(3):
            qkv_ref[c, :, g * share : (g + 1) * share] = sum_of(keep, came, rows, slice(c * share, (c + 1) * share))
        if g == 0:
            out_ref[...] = sum_of(keep, came, rows, slice(3 * share, keep.shape[1]))
    side_ref[...] = side_sum(before, ins[-1], high)[:, :HD]
    total = sum_of(keep_up, came_up, rows)
    up_ref[...] = total
    ahead = sum(jnp.sum(qkv_ref[c] * w_ref[c].astype(F32), axis=1, keepdims=True) for c in range(3))
    rising = jnp.sum(total * up_w_ref[...].astype(F32), axis=1, keepdims=True)
    lane = lax.broadcasted_iota(jnp.int32, (high, HD), 1)
    both = jnp.where(lane == 0, ahead, rising)
    gain_ref[...] = jnp.concatenate([both, jnp.zeros((HD - high, HD), F32)], axis=0).T[:8]


def finish(me, rounds, up, token, share, w, up_weight):
    high = up.keep.shape[0]
    width = share * len(rounds)
    args = [a for r in rounds for a in (r.keep, after(r.came, token))] + [rounds[-1].side, up.keep, after(up.came, token)]
    hidden = up_weight.shape[1]
    mine = [pl.BlockSpec((3, high, width), lambda j, me: (0, me[0], 0)), pl.BlockSpec((high, hidden), lambda j, me: (me[0], 0))]
    made = [(3, high, width), (high, width), (8, HD), (high, hidden), (8, HD)]
    return call(
        functools.partial(finish_body, share),
        (1,),
        [whole(a.shape) for a in args] + mine,
        [whole(a) for a in made],
        [jax.ShapeDtypeStruct(a, F32) for a in made],
        prefetch=1,
        name="finish",
    )(me, *args, w, up_weight)


def after(value, token):
    return lax.optimization_barrier((value, token))[0]


def conv_share(total, like, ranks, model):
    share = like.shape[3] // ranks
    pieces = math.prod(like.shape[:3])
    groups = -(-pieces * HD // model)
    total = total[:, : groups * HD].reshape(model // HD, share, groups, HD).transpose(2, 0, 1, 3)
    return total.reshape(groups * (model // HD), share, HD)[:pieces].reshape(like.shape[:3] + (share, HD))


def pair_over_head(part):
    count = lax.axis_size("head")
    for bit in range(bits_of(count)):
        came = lax.ppermute(part, "head", flip_pairs(count, bit))
        if bit == bits_of(count) - 1:
            return part, came
        part = (part.astype(F32) + came.astype(F32)).astype(part.dtype)
    return part, jnp.zeros_like(part)


def middle_body(len_ref, *refs):
    owns, others = refs[:PIECES], refs[PIECES : 2 * PIECES]
    mid_ref, cot_ref, gain_ref, wo_ref, grad_ref, turned_ref, mixed_ref, attended = refs[2 * PIECES :]
    rows = mid_ref.shape[1]
    s = pl.program_id(0)
    length = len_ref[s]

    def one(r):
        here = pl.ds(r, 16)
        valid = (row_ids(r, 16) < length).astype(F32)
        middle = mid_ref[0, here, :].astype(F32)
        sums = [own[0, here, :].astype(F32) + other[0, here, :].astype(F32) for own, other in zip(owns, others)]
        grad = jnp.concatenate(sums, axis=1)
        total = cot_ref[0, here, :].astype(F32) + norm_back(middle, grad * gain_ref[...])
        grad_ref[0, here, :] = total.astype(BF16)
        attended[here, :] = (total * valid).astype(BF16)

    by_rows(rows, 16, one)
    turned_ref[...] = attended[...].T
    mixed_ref[0] = dot_nt(attended[...], wo_ref[...]).astype(BF16)


def middle_back(lengths, owns, others, mid, cot, gain, wo):
    streams, rows, model = mid.shape
    width = wo.shape[0]
    return call(
        middle_body,
        (streams,),
        [per_stream(rows, model // PIECES)] * (2 * PIECES) + [per_stream(rows, model)] * 2 + [whole((1, model)), whole(wo.shape)],
        [per_stream(rows, model), turned(rows, model), per_stream(rows, width)],
        [
            jax.ShapeDtypeStruct(mid.shape, BF16),
            jax.ShapeDtypeStruct((model, streams * rows), BF16),
            like(streams, rows, width, BF16),
        ],
        scratch=[pltpu.VMEM((rows, model), BF16)],
        prefetch=1,
        name="middle_back",
    )(lengths, *owns, *others, mid, cot, gain, wo)


def lower_body(_, *refs):
    pieces, (w_ref, part_ref) = refs[:-2], refs[-2:]
    total = None
    for c in range(3):
        more = dot_nt(jnp.concatenate([piece[c, 0] for piece in pieces], axis=1), w_ref[c])
        total = more if total is None else total + more
    part_ref[0] = total.astype(BF16)


def lower(lengths, pieces, w):
    model = w.shape[1]
    _, streams, rows, _ = pieces[0].shape
    joint = lambda a: pl.BlockSpec((3, 1, rows, a.shape[3]), lambda s, *_: (0, s, 0, 0))
    return call(
        lower_body,
        (streams,),
        [joint(a) for a in pieces] + [whole(w.shape)],
        per_stream(rows, model),
        like(streams, rows, model, BF16),
        prefetch=1,
        name="lower",
    )(lengths, *pieces, w)


def inputs_body(_, __, x_ref, own_ref, other_ref, grad_ref, gain_ref, out_ref):
    rows = x_ref.shape[1]

    def one(r):
        here = pl.ds(r, 16)
        e = (own_ref[0, here, :].astype(F32) + other_ref[0, here, :].astype(F32)) * gain_ref[...]
        out_ref[0, here, :] = grad_ref[0, here, :].astype(F32) + norm_back(x_ref[0, here, :].astype(F32), e)

    by_rows(rows, 16, one)


SLOTS = 256


def rebuild_body(len_ref, q_ref, mem_ref, old_ref, conv_ref, cot_ref, next_ref, rows_ref, branch_t_ref, wide, grad_ref):
    s = pl.program_id(0)
    rows, heads = q_ref.shape[1], q_ref.shape[2] // HD
    slots = mem_ref.shape[2]
    made = slots // 3
    valid = row_ids(0, rows) < len_ref[s]
    valid_lane = lax.broadcasted_iota(jnp.int32, (1, rows), 1) < len_ref[s]
    row = lax.broadcasted_iota(jnp.int32, (slots, HD), 0)

    @pl.when(s == 0)
    def _():
        grad_ref[...] = jnp.zeros_like(grad_ref)
        wide[...] = jnp.zeros_like(wide)

    def front(a):
        windows, packed = [], []
        for c in range(2):
            wide[a, c, :slots] = mem_ref[0, c, :, lanes_of(a)].astype(F32)
            taps = [wide[a, c, pl.ds(t, SLOTS, stride=3), :].astype(BF16) for t in range(3)]
            windows.append(jnp.concatenate(taps, axis=1))
            squeezed = dot(windows[c], conv_ref[a, c].reshape(3 * HD, HD))
            packed.append(squeezed.astype(BF16))
            tail = jnp.concatenate([squeezed, jnp.zeros((slots - SLOTS, HD), F32)], axis=0)
            kept = pltpu.roll(old_ref[0, c, :, lanes_of(a)].astype(F32), slots - made, 0)
            tail = pltpu.roll(tail, slots - made, 0)
            next_ref[0, c, :, lanes_of(a)] = jnp.where(row < slots - made, kept, tail).astype(BF16)
        q = q_ref[0, :, lanes_of(a)]
        return windows, packed, dot_nt(mem_ref[0, 0, :, lanes_of(a)], q), dot_nt(packed[0], q)

    def soft(scores, count):
        start = count // 8 * 8
        key = start + lax.broadcasted_iota(jnp.int32, (scores.shape[0] - start, rows), 0)
        last = jnp.where(key < count, scores[start:], -1e30)
        scores = jnp.concatenate([scores[:start], last], axis=0)
        weights = jnp.exp2((scores - jnp.max(scores, axis=0, keepdims=True)) * BASE2)
        return weights, 1.0 / jnp.sum(weights, axis=0, keepdims=True)

    def rest(a, windows, packed, scores, few_scores):
        weights, share = soft(few_scores, made)
        probs = weights * share
        low = probs.astype(BF16)
        approach = dot(packed[1].T, low)
        weights, share = soft(scores, 3 * made)
        target = dot(mem_ref[0, 1, :, lanes_of(a)].T, weights.astype(BF16)) * share
        grad = jnp.where(valid_lane, (approach - target) * (2.0 / rows), 0.0).astype(BF16)
        grad_probs = dot(packed[1], grad)
        inner = jnp.sum(probs * grad_probs, axis=0, keepdims=True)
        grad_scores = (probs * (grad_probs - inner) * HEAD_SCALE).astype(BF16)
        back = [dot(grad_scores, q_ref[0, :, lanes_of(a)]), dot_nt(low, grad)]
        for c in range(2):
            grad_ref[a, c] += dot_tn(windows[c], back[c].astype(BF16)).reshape(3, HD, HD)

    pipelined([(a,) for a in range(heads)], front, rest)
    branch_t_ref[...] = jnp.where(valid, cot_ref[0], jnp.zeros_like(cot_ref[0])).T

    @pl.when(s == pl.num_programs(0) - 1)
    def _():
        ranks, deep, _ = rows_ref.shape
        share = HD // ranks
        rows_ref[...] = jnp.zeros_like(rows_ref)
        for a in range(heads):
            for n in range(6):
                piece = 6 * a + n
                at, group = piece % (deep // share) * share, piece // (deep // share)
                rows_ref[:, at : at + share, group * HD : (group + 1) * HD] = grad_ref[a, n // 3, n % 3].reshape(ranks, share, HD)


def rebuild(lengths, q, memory, compressed, conv, cot, ranks, columns):
    model = cot.shape[2]
    streams, rows, width = q.shape
    heads = width // HD
    slots = memory.shape[2]
    cache = pl.BlockSpec((1, 2, slots, width), lambda s, *_: (s, 0, 0, 0))
    return call(
        rebuild_body,
        (streams,),
        [per_stream(rows, width), cache, cache, whole(conv.shape), per_stream(rows, model)],
        [cache, pl.BlockSpec((ranks, model // ranks, columns), lambda *_: (0, 0, 0)), turned(rows, model)],
        [
            jax.ShapeDtypeStruct(compressed.shape, BF16),
            jax.ShapeDtypeStruct((ranks, model // ranks, columns), F32),
            jax.ShapeDtypeStruct((model, streams * rows), BF16),
        ],
        scratch=[pltpu.VMEM((heads, 2, 3 * SLOTS, HD), F32), pltpu.VMEM(conv.shape, F32)],
        prefetch=1,
        cover=True,
        name="rebuild",
    )(lengths, q, memory, compressed, conv, cot)


def per_device(
    inputs,
    cotangent,
    lengths,
    memory,
    compressed,
    query_key_value_weight,
    output_weight,
    up_weight,
    down_weight,
    gain_one,
    gain_two,
    slope_rates,
    conv_weight,
):
    streams, rows, model = inputs.shape
    tokens = streams * rows
    heads = slope_rates.shape[0]
    width = heads * HD
    ranks = lax.axis_size("dp")
    rank_bits = bits_of(ranks)
    me = lax.axis_index("dp").astype(jnp.int32)
    me_array = me.reshape(1)
    later = tuple(range(2, rank_bits))
    x_first, x_then_z, y_then_z = (0, 1) + later, (0,) + later + (1,), (1,) + later + (0,)
    y_then_mixed = (1, 2, 0) + later[1:]
    gain_1, gain_2 = gain_one.reshape(1, model), gain_two.reshape(1, model)
    qkv = query_key_value_weight.transpose(1, 0, 2)

    normed_t, q, memory_next = project(lengths, inputs, gain_1, qkv)
    mixed, exact, lse, part = attend(lengths, slope_rates, q, compressed, memory, memory_next, output_weight)
    own, other = pair_over_head(part)
    step = min(512, up_weight.shape[1])
    compressed_next, conv, branch_t = rebuild(after(lengths, part), q, memory, compressed, conv_weight, cotangent, ranks, step)
    conv = conv.reshape(model, step)
    mid, normed_two_t, active, before = rise(after(lengths, conv), inputs, own, other, gain_2, up_weight)
    sources = [(branch_t, active.reshape(tokens, -1)), (None, conv)]
    keep, send = weight_gradient(me_array, x_then_z, sources, step, "grad_down")
    down = Halving(keep, send, x_then_z, ranks, cut=up_weight.shape[1])
    grad_hidden, *backs = fall(after(lengths, send), cotangent, before, up_weight, down_weight)
    owns, others = zip(*[pair_over_head(back) for back in backs])
    keep, send = weight_gradient(me_array, y_then_z, [(normed_two_t, grad_hidden.reshape(tokens, -1))], step, "grad_up")
    up = Halving(keep, send, y_then_z, ranks)
    grad_middle, attended_t, grad_mixed = middle_back(
        after(lengths, send), owns, others, mid, cotangent, gain_2, output_weight
    )
    token = advance([down], grad_mixed)

    groups = 2 if heads % 2 == 0 else 1
    each = heads // groups
    pieces, sides, rounds = [], [], []
    for g in range(groups):
        piece, slopes = attend_back(
            g * each, each, after(lengths, token), slope_rates, q, compressed, memory, memory_next, exact, lse, grad_mixed
        )
        pieces.append(piece)
        sides.append(slopes)
        order = x_first if g else y_then_mixed
        sources = [(normed_t, piece.reshape(3, tokens, each * HD))]
        if g == 0:
            sources.append((attended_t, mixed.reshape(tokens, width)))
        final = g == groups - 1
        token = piece
        if final:
            part = lower(after(lengths, token), pieces, qkv)
            own, other = pair_over_head(part)
            token = part
        made = weight_gradient(after(me_array, token), order, sources, each * HD, "grad_joint", sides if final else ())
        keep, send = made[:2]
        rounds.append(Halving(keep, send, order, ranks, made[2] if final else None))
        token = advance([up, down], send) if g == 0 else send
    early, late = rounds[0], rounds[-1]
    both = rounds[::-1]

    token = advance([early, up, down] if groups > 1 else [up, down], token)
    branch = leave(after(lengths, token), active, down_weight)
    token = advance([late, down], branch)
    branch, branch_other = pair_over_head(after(branch, token))
    grad_inputs = None
    parts = 2 if streams % 2 == 0 else 1
    count = streams // parts
    for p in range(parts):
        grad_inputs = in_part(
            inputs_body, p * count, count, grad_inputs, after(lengths, token), [inputs, own, other, grad_middle], gain_1, mid, "inputs_back"
        )
        token = advance(both + ([] if p else [up]), grad_inputs)
    up.send(after(up.sent, token))
    outputs = in_part(
        outputs_body, 0, streams, None, after(lengths, token), [mid, branch, branch_other], None, mid, "outputs"
    )
    token = outputs
    unfinished = lambda: [r for r in both + [up] if r.stage + 1 < len(r.order)] + [r for r in [down] if r.total is None]
    while unfinished():
        token = advance(unfinished(), token)
    total_qkv, total_out, slopes, total_up, gains = finish(me_array, rounds, up, token, each * HD, qkv, up_weight)

    total_down, conv_rows = down.total
    total_conv = conv_share(conv_rows, conv_weight, ranks, model)
    portion = model // ranks
    mine = lambda a: lax.dynamic_slice_in_dim(a, me * portion, portion, 0)
    head_count = lax.axis_size("head")
    for bit in range(bits_of(head_count)):
        gains = gains + lax.ppermute(gains, "head", flip_pairs(head_count, bit))
    total_gain_one = gains[0, :portion] / mine(gain_one)
    total_gain_two = gains[1, :portion] / mine(gain_two)

    return (
        outputs,
        grad_inputs,
        memory_next,
        compressed_next,
        total_qkv.transpose(1, 0, 2),
        total_out.T,
        total_up,
        total_down.T,
        total_gain_one,
        total_gain_two,
        slopes[:heads, 0],
        total_conv,
    )


def solution(mesh):
    placed = (
        P("dp", None, None),
        P("dp", None, None),
        P("dp"),
        P("dp", None, None, "head"),
        P("dp", None, None, "head"),
        P(None, None, "head"),
        P("head", None),
        P(None, "head"),
        P("head", None),
        P(),
        P(),
        P("head"),
        P("head", None, None, None, None),
    )
    return jax.shard_map(
        per_device,
        mesh=mesh,
        in_specs=placed,
        out_specs=(
            P("dp", None, None),
            P("dp", None, None),
            P("dp", None, None, "head"),
            P("dp", None, None, "head"),
            P("dp", None, "head"),
            P("head", "dp"),
            P("dp", "head"),
            P("head", "dp"),
            P("dp"),
            P("dp"),
            P("head"),
            P("head", None, None, "dp", None),
        ),
        check_vma=False,
    )
```

```python
import functools
import math

import jax
import jax.numpy as jnp
from jax import lax
from jax.experimental import pallas as pl
from jax.experimental.pallas import tpu as pltpu
from jax.sharding import PartitionSpec as P

HD = 128
CE = 170
EPS = 1e-05
LOG2E = 1.0 / math.log(2.0)
HEAD_SCALE = 1.0 / math.sqrt(HD)
BASE2 = HEAD_SCALE * LOG2E
F32 = jnp.float32
BF16 = jnp.bfloat16
KEEP = BF16
VMEM_LIMIT = 67043328


def bits_of(count):
    return count.bit_length() - 1


def flip_pairs(count, bit):
    return [(i, i ^ (1 << bit)) for i in range(count)]


def call(body, grid, in_specs, out_specs, out_shape, scratch=(), prefetch=0, cover=False, name=None, aliases=None):
    return pl.pallas_call(
        body,
        grid_spec=pltpu.PrefetchScalarGridSpec(
            num_scalar_prefetch=prefetch,
            grid=grid,
            in_specs=in_specs,
            out_specs=out_specs,
            scratch_shapes=list(scratch),
        ),
        out_shape=out_shape,
        input_output_aliases=aliases or {},
        compiler_params=pltpu.CompilerParams(dimension_semantics=("arbitrary",) * len(grid), vmem_limit_bytes=VMEM_LIMIT),
        cost_estimate=pl.CostEstimate(flops=10**13 if cover else 0, bytes_accessed=0, transcendentals=0),
        name=name,
    )


def whole(shape):
    zeros = (0,) * len(shape)
    return pl.BlockSpec(shape, lambda *_: zeros, pipeline_mode=pl.Buffered(1))


def per_stream(rows, n):
    return pl.BlockSpec((1, rows, n), lambda s, *_: (s, 0, 0))


def turned(rows, n):
    return pl.BlockSpec((n, rows), lambda s, *_: (0, s))


def like(streams, rows, n, kind):
    return jax.ShapeDtypeStruct((streams, rows, n), kind)


def dot(a, b):
    return jnp.dot(a, b, preferred_element_type=F32)


def dot_nt(a, b):
    return lax.dot_general(a, b, (((1,), (1,)), ((), ())), preferred_element_type=F32)


def dot_tn(a, b):
    return lax.dot_general(a, b, (((0,), (0,)), ((), ())), preferred_element_type=F32)


def statistics(v):
    centred = v - jnp.mean(v, axis=-1, keepdims=True)
    spread = jnp.mean(centred * centred, axis=-1, keepdims=True)
    return centred, lax.rsqrt(spread + EPS)


def norm_back(v, e):
    centred = v - jnp.mean(v, axis=-1, keepdims=True)
    spread = jnp.mean(centred * centred, axis=-1, keepdims=True)
    middle = jnp.mean(e, axis=-1, keepdims=True)
    along = jnp.mean(e * centred, axis=-1, keepdims=True)
    scale = lax.rsqrt(spread + EPS)
    return scale * (e - middle - centred * (scale * scale * along))


def by_rows(rows, step, body, together=8):
    def one(i, carry):
        for j in range(together):
            body(pl.multiple_of((i * together + j) * step, step))
        return carry

    if rows == step * together:
        for j in range(together):
            body(j * step)
    else:
        lax.fori_loop(0, rows // (step * together), one, 0)


def row_ids(start, step):
    return start + lax.broadcasted_iota(jnp.int32, (step, 1), 0)


def project_body(len_ref, x_ref, gain_ref, w_ref, normed_t_ref, q_ref, kv_ref, normed_ref):
    rows = q_ref.shape[1]
    length = len_ref[pl.program_id(0)]

    def norm(r):
        centred, scale = statistics(x_ref[0, pl.ds(r, 16), :].astype(F32))
        normed_ref[pl.ds(r, 16), :] = (centred * scale * gain_ref[...]).astype(BF16)

    by_rows(rows, 16, norm, rows // 16)
    normed_t_ref[...] = normed_ref[...].T
    valid = row_ids(0, rows) < length
    normed = normed_ref[...]
    q_ref[0] = dot(normed, w_ref[0]).astype(BF16)
    for c in range(2):
        now = dot(normed, w_ref[c + 1])
        kv_ref[0, c] = jnp.where(valid, now, 0.0).astype(BF16)


def project(lengths, x, gain, w):
    streams, rows, model = x.shape
    width = w.shape[2]
    per = lambda *tail: pl.BlockSpec((1,) + tail, lambda s, *_: (s,) + (0,) * len(tail))
    return call(
        project_body,
        (streams,),
        [per(rows, model), whole((1, model)), whole(w.shape)],
        [pl.BlockSpec((model, rows), lambda s, *_: (0, s)), per(rows, width), per(2, rows, width)],
        [
            jax.ShapeDtypeStruct((model, streams * rows), BF16),
            jax.ShapeDtypeStruct((streams, rows, width), BF16),
            jax.ShapeDtypeStruct((streams, 2, rows, width), BF16),
        ],
        scratch=[pltpu.VMEM((rows, model), BF16)],
        prefetch=1,
        name="project",
    )(lengths, x, gain, w)


def position_columns(keys):
    centre = keys // 2
    lane = lax.broadcasted_iota(jnp.int32, (keys, HD), 1)
    place = lax.broadcasted_iota(jnp.int32, (keys, HD), 0) - centre
    fine = place & 7
    coarse = place - fine
    value = jnp.where(lane < 6, jnp.where((lane & 1) == 0, coarse, fine), jnp.where(lane == 6, 1, 0))
    return value.astype(F32).astype(BF16)


def slope_columns(slope, rows):
    exact = jnp.full((8, HD), slope, F32) * (1.0 / HEAD_SCALE)
    first = exact.astype(BF16).astype(F32)
    second = (exact - first).astype(BF16).astype(F32)
    third = exact - first - second
    lane = lax.broadcasted_iota(jnp.int32, (8, HD), 1)
    value = jnp.where(lane < 2, first, jnp.where(lane < 4, second, jnp.where(lane < 6, third, 0.0)))
    return jnp.broadcast_to(value[:1], (rows, HD)).astype(BF16)


def one_column(keys):
    lane = lax.broadcasted_iota(jnp.int32, (keys, HD), 1)
    return jnp.where(lane == 0, 1.0, 0.0).astype(BF16)


def diagonal_mask(block, start, length):
    row = lax.broadcasted_iota(jnp.int32, (block, block), 0)
    col = lax.broadcasted_iota(jnp.int32, (block, block), 1)
    return col <= jnp.minimum(row, length - 1 - start)


def pipelined(chains, front, rest):
    following = front(*chains[0])
    for n, chain in enumerate(chains):
        current = following
        if n + 1 < len(chains):
            following = front(*chains[n + 1])
        rest(*chain, *current)


def lanes_of(a):
    return slice(a * HD, (a + 1) * HD)


def attend_body(len_ref, slope_ref, q_ref, old_ref, mem_ref, now_ref, wo_ref, mix_ref, exact_ref, lse_ref, part_ref, kbuf, vbuf):
    s = pl.program_id(0)
    rows, heads = q_ref.shape[1], q_ref.shape[2] // HD
    old, mem = old_ref.shape[2], mem_ref.shape[2]
    past = old + mem
    keys = past + rows
    block = rows // 2
    length = len_ref[s]

    @pl.when(s == 0)
    def _():
        for a in range(heads):
            kbuf[a, :, HD:] = position_columns(keys)
            vbuf[a, :, HD:] = one_column(keys)

    for a in range(heads):
        for buf, c in ((kbuf, 0), (vbuf, 1)):
            buf[a, :old, :HD] = old_ref[0, c, :, lanes_of(a)]
            buf[a, old:past, :HD] = mem_ref[0, c, :, lanes_of(a)]
            buf[a, past:, :HD] = now_ref[0, c, :, lanes_of(a)]

    def front(a, i):
        side = slope_columns(slope_ref[a], block)
        wide = jnp.concatenate([q_ref[0, i * block : (i + 1) * block, lanes_of(a)], side], axis=1)
        return (dot_nt(wide, kbuf[a, : past + (i + 1) * block]),)

    def rest(a, i, scores):
        high = (i + 1) * block
        here = slice(i * block, high)
        allowed = diagonal_mask(block, i * block, length)
        last = jnp.where(allowed, scores[:, past + i * block :], -1e30)
        scores = jnp.concatenate([scores[:, : past + i * block], last], axis=1)
        top = jnp.max(scores, axis=1, keepdims=True)
        weights = jnp.exp2((scores - top) * BASE2).astype(BF16)
        both = dot(weights, vbuf[a, : past + high])
        total = both[:, HD : HD + 1]
        mixed = both[:, :HD] / total
        exact_ref[0, here, lanes_of(a)] = mixed
        mix_ref[0, here, lanes_of(a)] = mixed.astype(BF16)
        lse_ref[0, here, lanes_of(a)] = jnp.broadcast_to(top * BASE2 + jnp.log2(total), (block, HD))

    @pl.when(length > block)
    def _():
        pipelined([(a, i) for a in range(heads) for i in range(2)], front, rest)

    @pl.when(length <= block)
    def _():
        pipelined([(a, 0) for a in range(heads)], front, rest)
        exact_ref[0, block:, :] = jnp.zeros((rows - block, heads * HD), F32)
        mix_ref[0, block:, :] = jnp.zeros((rows - block, heads * HD), BF16)
        lse_ref[0, block:, :] = jnp.zeros((rows - block, heads * HD), F32)

    part_ref[0] = dot(mix_ref[0], wo_ref[...]).astype(BF16)


def attend(lengths, slopes, q, compressed, memory, now, wo):
    streams, rows, width = q.shape
    heads = width // HD
    model = wo.shape[1]
    keys = compressed.shape[2] + memory.shape[2] + rows
    cache = lambda a: pl.BlockSpec((1, 2, a.shape[2], width), lambda s, *_: (s, 0, 0, 0))
    return call(
        attend_body,
        (streams,),
        [per_stream(rows, width), cache(compressed), cache(memory), cache(now), whole(wo.shape)],
        [per_stream(rows, width), per_stream(rows, width), per_stream(rows, width), per_stream(rows, model)],
        [
            jax.ShapeDtypeStruct((streams, rows, width), BF16),
            jax.ShapeDtypeStruct((streams, rows, width), F32),
            jax.ShapeDtypeStruct((streams, rows, width), F32),
            jax.ShapeDtypeStruct((streams, rows, model), BF16),
        ],
        scratch=[pltpu.VMEM((heads, keys, 2 * HD), BF16), pltpu.VMEM((heads, keys, 2 * HD), BF16)],
        prefetch=2,
        name="attend",
    )(lengths, slopes, q, compressed, memory, now, wo)


def attend_back_body(first, len_ref, slope_ref, q_ref, old_ref, mem_ref, now_ref, exact_ref, lse_ref, grad_ref, out_ref, slope_out_ref, kbuf, vbuf):
    s = pl.program_id(0)
    rows, heads = q_ref.shape[1], q_ref.shape[2] // HD
    old, mem = old_ref.shape[2], mem_ref.shape[2]
    past = old + mem
    keys = past + rows
    block = rows // 2
    length = len_ref[s]

    @pl.when(s == 0)
    def _():
        for a in range(heads):
            kbuf[a, :, HD:] = position_columns(keys)
        slope_out_ref[...] = jnp.zeros_like(slope_out_ref)

    for a in range(heads):
        kbuf[a, :old, :HD] = old_ref[0, 0, :, lanes_of(a)]
        kbuf[a, old:past, :HD] = mem_ref[0, 0, :, lanes_of(a)]
        kbuf[a, past:, :HD] = now_ref[0, 0, :, lanes_of(a)]
        vbuf[a, :old] = old_ref[0, 1, :, lanes_of(a)]
        vbuf[a, old:past] = mem_ref[0, 1, :, lanes_of(a)]
        vbuf[a, past:] = now_ref[0, 1, :, lanes_of(a)]

    def here(i):
        return slice(i * block, (i + 1) * block)

    def front(a, i):
        side = slope_columns(slope_ref[first + a], block)
        wide = jnp.concatenate([q_ref[0, here(i), lanes_of(a)], side], axis=1)
        reach = past + (i + 1) * block
        return dot_nt(wide, kbuf[a, :reach]), dot_nt(grad_ref[0, here(i), lanes_of(a)], vbuf[a, :reach])

    def run(blocks):
        sums = {}

        def rest(a, i, scores, grad_probs):
            reach = past + (i + 1) * block
            q, grad = q_ref[0, here(i), lanes_of(a)], grad_ref[0, here(i), lanes_of(a)]
            exact = jnp.exp2(scores * BASE2 - lse_ref[0, here(i), a * HD : a * HD + 1])
            allowed = diagonal_mask(block, i * block, length)
            last = jnp.where(allowed, exact[:, reach - block :], 0.0)
            exact = jnp.concatenate([exact[:, : reach - block], last], axis=1)
            inner = jnp.sum(grad.astype(F32) * exact_ref[0, here(i), lanes_of(a)], axis=1, keepdims=True)
            grad_scores = (exact * (grad_probs - inner)).astype(BF16)
            wide = dot(grad_scores, kbuf[a, :reach])
            out_ref[0, 0, here(i), lanes_of(a)] = (wide[:, :HD] * HEAD_SCALE).astype(BF16)
            coarse, fine, total = (wide[:, HD + n : HD + n + 1] for n in (0, 1, 6))
            distance = (past + i * block - keys // 2 + lax.broadcasted_iota(jnp.int32, (block, 1), 0)).astype(F32)
            moment = jnp.sum(coarse + fine - distance * total, axis=0, keepdims=True)
            grad_keys = dot_tn(grad_scores[:, past:], q)
            grad_values = dot_tn(exact[:, past:].astype(BF16), grad)
            if i > 0:
                moment = moment + sums[a][0]
                done = sums[a][1].shape[0]
                join = lambda before, now: jnp.concatenate([before + now[:done], now[done:]], axis=0)
                grad_keys, grad_values = join(sums[a][1], grad_keys), join(sums[a][2], grad_values)
            sums[a] = moment, grad_keys, grad_values
            if i == blocks - 1:
                high = blocks * block
                out_ref[1, 0, :high, lanes_of(a)] = (grad_keys * HEAD_SCALE).astype(BF16)
                out_ref[2, 0, :high, lanes_of(a)] = grad_values.astype(BF16)
                slope_out_ref[first + a : first + a + 1, :] += jnp.broadcast_to(moment, (1, HD))

        pipelined([(a, i) for a in range(heads) for i in range(blocks)], front, rest)

    @pl.when(length > block)
    def _():
        run(2)

    @pl.when(length <= block)
    def _():
        run(1)
        for c in range(3):
            out_ref[c, 0, block:, :] = jnp.zeros((rows - block, heads * HD), BF16)


def attend_back(first, heads, lengths, slopes, q, compressed, memory, now, exact, lse, grad):
    streams, rows, width = q.shape
    keys = compressed.shape[2] + memory.shape[2] + rows
    group = first // heads
    cache = lambda a: pl.BlockSpec((1, 2, a.shape[2], heads * HD), lambda s, *_: (s, 0, 0, group))
    some = pl.BlockSpec((1, rows, heads * HD), lambda s, *_: (s, 0, group))
    return call(
        functools.partial(attend_back_body, first),
        (streams,),
        [some, cache(compressed), cache(memory), cache(now), some, some, some],
        [pl.BlockSpec((3, 1, rows, heads * HD), lambda s, *_: (0, s, 0, 0)), pl.BlockSpec((8, HD), lambda *_: (0, 0))],
        [jax.ShapeDtypeStruct((3, streams, rows, heads * HD), BF16), jax.ShapeDtypeStruct((8, HD), F32)],
        scratch=[pltpu.VMEM((heads, keys, 2 * HD), BF16), pltpu.VMEM((heads, keys, HD), BF16)],
        prefetch=2,
        cover=True,
        name="attend_back",
    )(lengths, slopes, q, compressed, memory, now, exact, lse, grad)


GELU_K = math.sqrt(2.0 / math.pi)
GELU_C = 0.044715


def gate_of(v):
    square = v * v
    rate = -2.0 * GELU_K * LOG2E
    return 1.0 / (1.0 + jnp.exp2(v * (rate + (rate * GELU_C) * square))), square


def gelu_slope(v):
    gate, square = gate_of(v)
    lean = v * (2.0 * GELU_K + (6.0 * GELU_K * GELU_C) * square)
    return gate * (1.0 + lean * (1.0 - gate))


def rise_body(len_ref, x_ref, own_ref, other_ref, gain_ref, up_ref, mid_ref, normed_t_ref, active_ref, before_ref, normed):
    rows = x_ref.shape[1]
    hidden_width = up_ref.shape[1]
    length = len_ref[pl.program_id(0)]

    def norm(r):
        here = pl.ds(r, 16)
        valid = (row_ids(r, 16) < length).astype(F32)
        attended = own_ref[0, here, :].astype(F32) + other_ref[0, here, :].astype(F32)
        middle = x_ref[0, here, :].astype(F32) + attended * valid
        mid_ref[0, here, :] = middle.astype(BF16)
        centred, scale = statistics(middle)
        normed[here, :] = (centred * scale * gain_ref[...]).astype(BF16)

    by_rows(rows, 16, norm, rows // 16)
    normed_t_ref[...] = normed[...].T
    chunk = min(512, hidden_width)
    columns = [slice(f, f + chunk) for f in range(0, hidden_width, chunk)]

    def front(cols):
        return (dot(normed[...], up_ref[:, cols]),)

    def rest(cols, v):
        active_ref[0, :, cols] = (v * gate_of(v)[0]).astype(BF16)
        before_ref[0, :, cols] = v.astype(BF16)

    pipelined([(cols,) for cols in columns], front, rest)


def rise(lengths, x, own, other, gain, up):
    streams, rows, model = x.shape
    hidden = up.shape[1]
    tokens = streams * rows
    return call(
        rise_body,
        (streams,),
        [per_stream(rows, model)] * 3 + [whole((1, model)), whole(up.shape)],
        [per_stream(rows, model), turned(rows, model), per_stream(rows, hidden), per_stream(rows, hidden)],
        [
            like(streams, rows, model, BF16),
            jax.ShapeDtypeStruct((model, tokens), BF16),
            like(streams, rows, hidden, BF16),
            like(streams, rows, hidden, BF16),
        ],
        scratch=[pltpu.VMEM((rows, model), BF16)],
        prefetch=1,
        name="rise",
    )(lengths, x, own, other, gain, up)


def fall_body(len_ref, cot_ref, before_ref, up_ref, down_ref, hidden_ref, *back_refs):
    rows = cot_ref.shape[1]
    hidden_width = up_ref.shape[1]
    valid = row_ids(0, rows) < len_ref[pl.program_id(0)]
    branch = jnp.where(valid, cot_ref[0].astype(F32), 0.0).astype(BF16)
    chunk = min(1024, hidden_width)
    back = []

    def front(cols):
        return (dot_nt(branch, down_ref[cols, :]),)

    def rest(cols, grad_active):
        grad_hidden = (grad_active * gelu_slope(before_ref[0, :, cols].astype(F32))).astype(BF16)
        hidden_ref[0, :, cols] = grad_hidden
        back.append(dot_nt(grad_hidden, up_ref[:, cols]))

    pipelined([(slice(f, f + chunk),) for f in range(0, hidden_width, chunk)], front, rest)
    total = sum(back[1:], back[0]).astype(BF16)
    part = total.shape[1] // len(back_refs)
    for n, back_ref in enumerate(back_refs):
        back_ref[0] = total[:, n * part : (n + 1) * part]


PIECES = 2


def fall(lengths, cot, slope, up, down):
    streams, rows, model = cot.shape
    hidden = up.shape[1]
    tokens = streams * rows
    return call(
        fall_body,
        (streams,),
        [per_stream(rows, model), per_stream(rows, hidden), whole(up.shape), whole(down.shape)],
        [per_stream(rows, hidden)] + [per_stream(rows, model // PIECES)] * PIECES,
        [like(streams, rows, hidden, BF16)] + [like(streams, rows, model // PIECES, BF16)] * PIECES,
        prefetch=1,
        name="fall",
    )(lengths, cot, slope, up, down)


def leave_body(_, active_ref, down_ref, part_ref):
    part_ref[0] = dot(active_ref[0], down_ref[...]).astype(BF16)


def leave(lengths, active, down):
    streams, rows, hidden = active.shape
    model = down.shape[1]
    return call(
        leave_body,
        (streams,),
        [per_stream(rows, hidden), whole(down.shape)],
        per_stream(rows, model),
        like(streams, rows, model, BF16),
        prefetch=1,
        cover=True,
        name="leave",
    )(lengths, active, down)


def outputs_body(start, len_ref, mid_ref, own_ref, other_ref, out_ref):
    rows = mid_ref.shape[1]
    length = len_ref[start + pl.program_id(0)]

    def one(r):
        here = pl.ds(r, 16)
        valid = (row_ids(r, 16) < length).astype(F32)
        branch = own_ref[0, here, :].astype(F32) + other_ref[0, here, :].astype(F32)
        out_ref[0, here, :] = mid_ref[0, here, :].astype(F32) + valid * branch

    by_rows(rows, 16, one, 4)


def in_part(body, first, count, into, lengths, args, gain, like_this, name):
    rows, model = like_this.shape[1:]
    per = pl.BlockSpec((1, rows, model), lambda s, *_: (s + first, 0, 0))
    extra = [] if gain is None else [whole(gain.shape)]
    held = [] if into is None else [into]

    def inner(len_ref, *refs):
        body(first, len_ref, *refs[: len(args) + len(extra)], refs[-1])

    return call(
        inner,
        (count,),
        [per] * len(args) + extra + [pl.BlockSpec(memory_space=pl.ANY)] * len(held),
        per,
        jax.ShapeDtypeStruct(like_this.shape, F32),
        prefetch=1,
        cover=first > 0 or gain is None,
        aliases={1 + len(args) + len(extra): 0} if held else {},
        name=name,
    )(lengths, *args, *([] if gain is None else [gain]), *held)


def chunk_at(place, order, me):
    apart = 0
    for i, bit in enumerate(order):
        apart |= ((place >> (len(order) - 1 - i)) & 1) << bit
    return apart ^ me


def send_order(source, order, me, first, count):
    deep = source.shape[0] // (1 << len(order))
    lines = []
    for p in range(first, first + count):
        lines.append(source[pl.ds(pl.multiple_of(chunk_at(p, order, me) * deep, deep), deep), :])
    return jnp.concatenate(lines, axis=0)


def weight_body(spans, extra, order, me_ref, *refs):
    products = sum(span[2] for span in spans)
    xts, ys = list(refs[:products]), refs[products : products + len(spans)]
    sides, outs = refs[products + len(spans) :], refs[-3 if extra else -2 :]
    sides, keep_ref, send_ref = sides[: -len(outs)], outs[0], outs[1]
    me = me_ref[0]
    j = pl.program_id(0)
    places = 1 << len(order)
    half = keep_ref.shape[0]
    for y, (start, stop, product) in zip(ys, spans):
        xt = xts.pop(0) if product else None

        @pl.when((j >= start) & (j < stop))
        def _(xt=xt, y=y):
            for n, out in enumerate((keep_ref, send_ref)):
                rows = send_order(y if xt is None else xt, order, me, n * places // 2, places // 2)
                if xt is not None:
                    rows = dot(rows, y[...] if len(y.shape) == 2 else y[0])
                out[:half, :] = rows.astype(out.dtype)

    if extra:
        total = sum(side[...] for side in sides)
        first = total.astype(BF16).astype(F32)
        both = jnp.concatenate([first, total - first], axis=0).astype(BF16)
        times = send_ref.shape[1] // HD
        send_ref[half:, :] = jnp.concatenate([both] * times, axis=1)
        outs[2][...] = jnp.concatenate([total] * times, axis=1)


def weight_gradient(me, order, sources, step, name, sides=()):
    xts = [xt for xt, _ in sources if xt is not None]
    model, tokens = xts[0].shape
    spans, specs, at = [], [], 0
    for xt, y in sources:
        n = y.shape[-1] // step
        blocks = n * (y.shape[0] if y.ndim == 3 else 1)
        spans.append((at, at + blocks, xt is not None))
        if y.ndim == 3:
            pick = lambda j, *_, at=at, n=n, blocks=blocks: (jnp.clip(j - at, 0, blocks - 1) // n, 0, jnp.clip(j - at, 0, blocks - 1) % n)
            specs.append(pl.BlockSpec((1, y.shape[1], step), pick))
        else:
            specs.append(pl.BlockSpec((y.shape[0], step), lambda j, *_, at=at, blocks=blocks: (0, jnp.clip(j - at, 0, blocks - 1))))
        at += blocks
    columns = at * step
    extra = 16 if sides else 0
    heights = (model // 2, model // 2 + extra) + ((8,) if sides else ())
    return call(
        functools.partial(weight_body, spans, extra, order),
        (at,),
        [whole(xt.shape) for xt in xts] + specs + [whole(side.shape) for side in sides],
        [pl.BlockSpec((n, step), lambda j, *_: (0, j)) for n in heights],
        [jax.ShapeDtypeStruct((n, columns), kind) for n, kind in zip(heights, (KEEP, BF16, F32))],
        prefetch=1,
        name=name,
    )(me, *xts, *[y for _, y in sources], *sides)


class Halving:
    def __init__(self, keep, send, order, count, side=None, cut=None):
        self.order, self.count, self.stage, self.total = order, count, 0, None
        self.cuts = (0, cut or keep.shape[1], keep.shape[1])
        self.keep, self.side = keep, side
        self.send(send)

    def send(self, what):
        self.sent = what
        self.came = lax.ppermute(what, "dp", flip_pairs(self.count, self.order[self.stage]))


def sum_of(keep, came, rows, columns=slice(None)):
    return keep[rows, columns].astype(F32) + came[rows, columns].astype(F32)


def side_sum(before, came, high):
    both = came[high:, :].astype(F32)
    return before[...] + (both[:8] + both[8:])


def advance_body(items, *refs):
    refs = list(refs)
    ins = [[refs.pop(0) for _ in range(3 if side else 2)] for _, side in items]
    for (cuts, side), (keep, came, *before) in zip(items, ins):
        high = keep.shape[0]
        half = high // 2
        if cuts:
            parts = [(refs.pop(0), slice(a, b)) for a, b in zip(cuts, cuts[1:]) if a < b]

            @pl.when(pl.program_id(0) == 0)
            def _(keep=keep, came=came, parts=parts, high=high):
                for out, columns in parts:
                    out[...] = sum_of(keep, came, slice(0, high), columns)

        else:
            stay, go = refs.pop(0), refs.pop(0)
            stay[...] = sum_of(keep, came, slice(0, half)).astype(stay.dtype)
            go[:half, :] = sum_of(keep, came, slice(half, high)).astype(BF16)
            if side:
                total = side_sum(before[0], came, high)
                refs.pop(0)[...] = total
                first = total.astype(BF16).astype(F32)
                go[half:, :] = jnp.concatenate([first, total - first], axis=0).astype(BF16)


def advance(rounds, token):
    rounds = [r for r in rounds if r.total is None]
    if not rounds:
        return token
    turns = 4 if all(r.keep.shape[1] % (4 * HD) == 0 for r in rounds) else 2
    blocks = lambda a: pl.BlockSpec((a.shape[0], a.shape[1] // turns), lambda j: (0, j))
    items, args, outs, in_specs, out_specs = [], [], [], [], []
    for r in rounds:
        final, side = r.stage + 1 == len(r.order), r.side is not None
        high, columns = r.keep.shape
        items.append((r.cuts if final else None, side))
        mine = [r.keep, after(r.came, token)] + ([r.side] if side else [])
        if final:
            made = [jax.ShapeDtypeStruct((high, b - a), F32) for a, b in zip(r.cuts, r.cuts[1:]) if a < b]
        else:
            made = [
                jax.ShapeDtypeStruct((high // 2, columns), KEEP),
                jax.ShapeDtypeStruct((high // 2 + (16 if side else 0), columns), BF16),
            ] + ([jax.ShapeDtypeStruct(r.side.shape, F32)] if side else [])
        args += mine
        outs += made
        in_specs += [whole(a.shape) if final else blocks(a) for a in mine]
        out_specs += [pl.BlockSpec(a.shape, lambda j: (0, 0)) if final else blocks(a) for a in made]
    got = list(call(functools.partial(advance_body, items), (turns,), in_specs, out_specs, outs, name="advance")(*args))
    token = got[0]
    for r, (cuts, side) in zip(rounds, items):
        r.stage += 1
        if cuts:
            r.total = [got.pop(0) for a, b in zip(cuts, cuts[1:]) if a < b]
            continue
        r.keep, send = got.pop(0), got.pop(0)
        if side:
            r.side = got.pop(0)
        r.send(send)
    return token


def finish_body(share, _, *refs):
    *ins, before, keep_up, came_up, w_ref, up_w_ref, qkv_ref, out_ref, up_ref, gain_ref = refs
    high = keep_up.shape[0]
    rows = slice(0, high)
    for g in range(len(ins) // 2):
        keep, came = ins[2 * g], ins[2 * g + 1]
        for c in range(3):
            qkv_ref[c, :, g * share : (g + 1) * share] = sum_of(keep, came, rows, slice(c * share, (c + 1) * share))
        if g == 0:
            out_ref[...] = sum_of(keep, came, rows, slice(3 * share, keep.shape[1]))
    side = side_sum(before, ins[-1], high)[:, :HD]
    total = sum_of(keep_up, came_up, rows)
    up_ref[...] = total
    ahead = sum(jnp.sum(qkv_ref[c] * w_ref[c].astype(F32), axis=1, keepdims=True) for c in range(3))
    rising = jnp.sum(total * up_w_ref[...].astype(F32), axis=1, keepdims=True)
    lane = lax.broadcasted_iota(jnp.int32, (high, HD), 1)
    side = jnp.concatenate([side, jnp.zeros((high - 8, HD), F32)], axis=0)
    columns = jnp.where(lane == 0, ahead, jnp.where(lane == 1, rising, side))
    gain_ref[...] = jnp.concatenate([columns, jnp.zeros((HD - high, HD), F32)], axis=0).T[:8]


def finish(me, rounds, up, token, share, w, up_weight):
    high = up.keep.shape[0]
    width = share * len(rounds)
    args = [a for r in rounds for a in (r.keep, after(r.came, token))] + [rounds[-1].side, up.keep, after(up.came, token)]
    hidden = up_weight.shape[1]
    mine = [pl.BlockSpec((3, high, width), lambda j, me: (0, me[0], 0)), pl.BlockSpec((high, hidden), lambda j, me: (me[0], 0))]
    made = [(3, high, width), (high, width), (high, hidden), (8, HD)]
    return call(
        functools.partial(finish_body, share),
        (1,),
        [whole(a.shape) for a in args] + mine,
        [whole(a) for a in made],
        [jax.ShapeDtypeStruct(a, F32) for a in made],
        prefetch=1,
        name="finish",
    )(me, *args, w, up_weight)


def after(value, token):
    return lax.optimization_barrier((value, token))[0]


def conv_share(total, like, ranks, model):
    share = like.shape[3] // ranks
    pieces = math.prod(like.shape[:3])
    groups = -(-pieces * HD // model)
    total = total[:, : groups * HD].reshape(model // HD, share, groups, HD).transpose(2, 0, 1, 3)
    return total.reshape(groups * (model // HD), share, HD)[:pieces].reshape(like.shape[:3] + (share, HD))


def pair_over_head(part):
    count = lax.axis_size("head")
    for bit in range(bits_of(count)):
        came = lax.ppermute(part, "head", flip_pairs(count, bit))
        if bit == bits_of(count) - 1:
            return part, came
        part = (part.astype(F32) + came.astype(F32)).astype(part.dtype)
    return part, jnp.zeros_like(part)


def middle_body(len_ref, *refs):
    owns, others = refs[:PIECES], refs[PIECES : 2 * PIECES]
    mid_ref, cot_ref, gain_ref, wo_ref, grad_ref, turned_ref, mixed_ref, attended = refs[2 * PIECES :]
    rows = mid_ref.shape[1]
    s = pl.program_id(0)
    length = len_ref[s]

    def one(r):
        here = pl.ds(r, 16)
        valid = (row_ids(r, 16) < length).astype(F32)
        middle = mid_ref[0, here, :].astype(F32)
        sums = [own[0, here, :].astype(F32) + other[0, here, :].astype(F32) for own, other in zip(owns, others)]
        grad = jnp.concatenate(sums, axis=1)
        total = cot_ref[0, here, :].astype(F32) + norm_back(middle, grad * gain_ref[...])
        grad_ref[0, here, :] = total.astype(BF16)
        attended[here, :] = (total * valid).astype(BF16)

    by_rows(rows, 16, one)
    turned_ref[...] = attended[...].T
    mixed_ref[0] = dot_nt(attended[...], wo_ref[...]).astype(BF16)


def middle_back(lengths, owns, others, mid, cot, gain, wo):
    streams, rows, model = mid.shape
    width = wo.shape[0]
    return call(
        middle_body,
        (streams,),
        [per_stream(rows, model // PIECES)] * (2 * PIECES) + [per_stream(rows, model)] * 2 + [whole((1, model)), whole(wo.shape)],
        [per_stream(rows, model), turned(rows, model), per_stream(rows, width)],
        [
            jax.ShapeDtypeStruct(mid.shape, BF16),
            jax.ShapeDtypeStruct((model, streams * rows), BF16),
            like(streams, rows, width, BF16),
        ],
        scratch=[pltpu.VMEM((rows, model), BF16)],
        prefetch=1,
        name="middle_back",
    )(lengths, *owns, *others, mid, cot, gain, wo)


def lower_body(_, *refs):
    pieces, (w_ref, part_ref) = refs[:-2], refs[-2:]
    total = None
    for c in range(3):
        more = dot_nt(jnp.concatenate([piece[c, 0] for piece in pieces], axis=1), w_ref[c])
        total = more if total is None else total + more
    part_ref[0] = total.astype(BF16)


def lower(lengths, pieces, w):
    model = w.shape[1]
    _, streams, rows, _ = pieces[0].shape
    joint = lambda a: pl.BlockSpec((3, 1, rows, a.shape[3]), lambda s, *_: (0, s, 0, 0))
    return call(
        lower_body,
        (streams,),
        [joint(a) for a in pieces] + [whole(w.shape)],
        per_stream(rows, model),
        like(streams, rows, model, BF16),
        prefetch=1,
        name="lower",
    )(lengths, *pieces, w)


def inputs_body(_, __, x_ref, own_ref, other_ref, grad_ref, gain_ref, out_ref):
    rows = x_ref.shape[1]

    def one(r):
        here = pl.ds(r, 16)
        e = (own_ref[0, here, :].astype(F32) + other_ref[0, here, :].astype(F32)) * gain_ref[...]
        out_ref[0, here, :] = grad_ref[0, here, :].astype(F32) + norm_back(x_ref[0, here, :].astype(F32), e)

    by_rows(rows, 16, one)


SLOTS = 256


def rebuild_body(len_ref, q_ref, mem_ref, old_ref, conv_ref, cot_ref, next_ref, rows_ref, branch_t_ref, wide, grad_ref):
    s = pl.program_id(0)
    rows, heads = q_ref.shape[1], q_ref.shape[2] // HD
    slots = mem_ref.shape[2]
    made = slots // 3
    valid = row_ids(0, rows) < len_ref[s]
    valid_lane = lax.broadcasted_iota(jnp.int32, (1, rows), 1) < len_ref[s]
    row = lax.broadcasted_iota(jnp.int32, (slots, HD), 0)

    @pl.when(s == 0)
    def _():
        grad_ref[...] = jnp.zeros_like(grad_ref)
        wide[...] = jnp.zeros_like(wide)

    def front(a):
        windows, packed = [], []
        for c in range(2):
            wide[a, c, :slots] = mem_ref[0, c, :, lanes_of(a)].astype(F32)
            taps = [wide[a, c, pl.ds(t, SLOTS, stride=3), :].astype(BF16) for t in range(3)]
            windows.append(jnp.concatenate(taps, axis=1))
            squeezed = dot(windows[c], conv_ref[a, c].reshape(3 * HD, HD))
            packed.append(squeezed.astype(BF16))
            tail = jnp.concatenate([squeezed, jnp.zeros((slots - SLOTS, HD), F32)], axis=0)
            kept = pltpu.roll(old_ref[0, c, :, lanes_of(a)].astype(F32), slots - made, 0)
            tail = pltpu.roll(tail, slots - made, 0)
            next_ref[0, c, :, lanes_of(a)] = jnp.where(row < slots - made, kept, tail).astype(BF16)
        q = q_ref[0, :, lanes_of(a)]
        return windows, packed, dot_nt(mem_ref[0, 0, :, lanes_of(a)], q), dot_nt(packed[0], q)

    def soft(scores, count):
        start = count // 8 * 8
        key = start + lax.broadcasted_iota(jnp.int32, (scores.shape[0] - start, rows), 0)
        last = jnp.where(key < count, scores[start:], -1e30)
        scores = jnp.concatenate([scores[:start], last], axis=0)
        weights = jnp.exp2((scores - jnp.max(scores, axis=0, keepdims=True)) * BASE2)
        return weights, 1.0 / jnp.sum(weights, axis=0, keepdims=True)

    def rest(a, windows, packed, scores, few_scores):
        weights, share = soft(few_scores, made)
        probs = weights * share
        low = probs.astype(BF16)
        approach = dot(packed[1].T, low)
        weights, share = soft(scores, 3 * made)
        target = dot(mem_ref[0, 1, :, lanes_of(a)].T, weights.astype(BF16)) * share
        grad = jnp.where(valid_lane, (approach - target) * (2.0 / rows), 0.0).astype(BF16)
        grad_probs = dot(packed[1], grad)
        inner = jnp.sum(probs * grad_probs, axis=0, keepdims=True)
        grad_scores = (probs * (grad_probs - inner) * HEAD_SCALE).astype(BF16)
        back = [dot(grad_scores, q_ref[0, :, lanes_of(a)]), dot_nt(low, grad)]
        for c in range(2):
            grad_ref[a, c] += dot_tn(windows[c], back[c].astype(BF16)).reshape(3, HD, HD)

    pipelined([(a,) for a in range(heads)], front, rest)
    branch_t_ref[...] = jnp.where(valid, cot_ref[0], jnp.zeros_like(cot_ref[0])).T

    @pl.when(s == pl.num_programs(0) - 1)
    def _():
        ranks, deep, _ = rows_ref.shape
        share = HD // ranks
        rows_ref[...] = jnp.zeros_like(rows_ref)
        for a in range(heads):
            for n in range(6):
                piece = 6 * a + n
                at, group = piece % (deep // share) * share, piece // (deep // share)
                rows_ref[:, at : at + share, group * HD : (group + 1) * HD] = grad_ref[a, n // 3, n % 3].reshape(ranks, share, HD)


def rebuild(lengths, q, memory, compressed, conv, cot, ranks, columns):
    model = cot.shape[2]
    streams, rows, width = q.shape
    heads = width // HD
    slots = memory.shape[2]
    cache = pl.BlockSpec((1, 2, slots, width), lambda s, *_: (s, 0, 0, 0))
    return call(
        rebuild_body,
        (streams,),
        [per_stream(rows, width), cache, cache, whole(conv.shape), per_stream(rows, model)],
        [cache, pl.BlockSpec((ranks, model // ranks, columns), lambda *_: (0, 0, 0)), turned(rows, model)],
        [
            jax.ShapeDtypeStruct(compressed.shape, BF16),
            jax.ShapeDtypeStruct((ranks, model // ranks, columns), F32),
            jax.ShapeDtypeStruct((model, streams * rows), BF16),
        ],
        scratch=[pltpu.VMEM((heads, 2, 3 * SLOTS, HD), F32), pltpu.VMEM(conv.shape, F32)],
        prefetch=1,
        cover=True,
        name="rebuild",
    )(lengths, q, memory, compressed, conv, cot)


def per_device(
    inputs,
    cotangent,
    lengths,
    memory,
    compressed,
    query_key_value_weight,
    output_weight,
    up_weight,
    down_weight,
    gain_one,
    gain_two,
    slope_rates,
    conv_weight,
):
    streams, rows, model = inputs.shape
    tokens = streams * rows
    heads = slope_rates.shape[0]
    width = heads * HD
    ranks = lax.axis_size("dp")
    rank_bits = bits_of(ranks)
    me = lax.axis_index("dp").astype(jnp.int32)
    me_array = me.reshape(1)
    later = tuple(range(2, rank_bits))
    x_first, x_then_z, y_then_z = (0, 1) + later, (0,) + later + (1,), (1,) + later + (0,)
    y_then_mixed = (1, 2, 0) + later[1:]
    gain_1, gain_2 = gain_one.reshape(1, model), gain_two.reshape(1, model)
    qkv = query_key_value_weight.transpose(1, 0, 2)

    normed_t, q, memory_next = project(lengths, inputs, gain_1, qkv)
    mixed, exact, lse, part = attend(lengths, slope_rates, q, compressed, memory, memory_next, output_weight)
    own, other = pair_over_head(part)
    step = min(512, up_weight.shape[1])
    compressed_next, conv, branch_t = rebuild(after(lengths, part), q, memory, compressed, conv_weight, cotangent, ranks, step)
    conv = conv.reshape(model, step)
    mid, normed_two_t, active, before = rise(after(lengths, conv), inputs, own, other, gain_2, up_weight)
    sources = [(branch_t, active.reshape(tokens, -1)), (None, conv)]
    keep, send = weight_gradient(me_array, x_then_z, sources, step, "grad_down")
    down = Halving(keep, send, x_then_z, ranks, cut=up_weight.shape[1])
    grad_hidden, *backs = fall(after(lengths, send), cotangent, before, up_weight, down_weight)
    owns, others = zip(*[pair_over_head(back) for back in backs])
    keep, send = weight_gradient(me_array, y_then_z, [(normed_two_t, grad_hidden.reshape(tokens, -1))], step, "grad_up")
    up = Halving(keep, send, y_then_z, ranks)
    grad_middle, attended_t, grad_mixed = middle_back(
        after(lengths, send), owns, others, mid, cotangent, gain_2, output_weight
    )
    token = advance([down], grad_mixed)

    groups = 2 if heads % 2 == 0 else 1
    each = heads // groups
    pieces, sides, rounds = [], [], []
    for g in range(groups):
        piece, slopes = attend_back(
            g * each, each, after(lengths, token), slope_rates, q, compressed, memory, memory_next, exact, lse, grad_mixed
        )
        pieces.append(piece)
        sides.append(slopes)
        order = x_first if g else y_then_mixed
        sources = [(normed_t, piece.reshape(3, tokens, each * HD))]
        if g == 0:
            sources.append((attended_t, mixed.reshape(tokens, width)))
        final = g == groups - 1
        token = piece
        if final:
            part = lower(after(lengths, token), pieces, qkv)
            own, other = pair_over_head(part)
            token = part
        made = weight_gradient(after(me_array, token), order, sources, each * HD, "grad_joint", sides if final else ())
        keep, send = made[:2]
        rounds.append(Halving(keep, send, order, ranks, made[2] if final else None))
        token = advance([up, down], send) if g == 0 else send
    early, late = rounds[0], rounds[-1]
    both = rounds[::-1]

    token = advance([early, up, down] if groups > 1 else [up, down], token)
    branch = leave(after(lengths, token), active, down_weight)
    token = advance([late, down], branch)
    branch, branch_other = pair_over_head(after(branch, token))
    grad_inputs = None
    parts = 2 if streams % 2 == 0 else 1
    count = streams // parts
    for p in range(parts):
        grad_inputs = in_part(
            inputs_body, p * count, count, grad_inputs, after(lengths, token), [inputs, own, other, grad_middle], gain_1, mid, "inputs_back"
        )
        token = advance(both + ([] if p else [up]), grad_inputs)
    up.send(after(up.sent, token))
    outputs = in_part(
        outputs_body, 0, streams, None, after(lengths, token), [mid, branch, branch_other], None, mid, "outputs"
    )
    token = outputs
    unfinished = lambda: [r for r in both + [up] if r.stage + 1 < len(r.order)] + [r for r in [down] if r.total is None]
    while unfinished():
        token = advance(unfinished(), token)
    total_qkv, total_out, total_up, gains = finish(me_array, rounds, up, token, each * HD, qkv, up_weight)

    total_down, conv_rows = down.total
    total_conv = conv_share(conv_rows, conv_weight, ranks, model)
    portion = model // ranks
    mine = lambda a: lax.dynamic_slice_in_dim(a, me * portion, portion, 0)
    slopes = gains[2, :heads]
    head_count = lax.axis_size("head")
    for bit in range(bits_of(head_count)):
        gains = gains + lax.ppermute(gains, "head", flip_pairs(head_count, bit))
    total_gain_one = gains[0, :portion] / mine(gain_one)
    total_gain_two = gains[1, :portion] / mine(gain_two)

    return (
        outputs,
        grad_inputs,
        memory_next,
        compressed_next,
        total_qkv.transpose(1, 0, 2),
        total_out.T,
        total_up,
        total_down.T,
        total_gain_one,
        total_gain_two,
        slopes,
        total_conv,
    )


def solution(mesh):
    placed = (
        P("dp", None, None),
        P("dp", None, None),
        P("dp"),
        P("dp", None, None, "head"),
        P("dp", None, None, "head"),
        P(None, None, "head"),
        P("head", None),
        P(None, "head"),
        P("head", None),
        P(),
        P(),
        P("head"),
        P("head", None, None, None, None),
    )
    return jax.shard_map(
        per_device,
        mesh=mesh,
        in_specs=placed,
        out_specs=(
            P("dp", None, None),
            P("dp", None, None),
            P("dp", None, None, "head"),
            P("dp", None, None, "head"),
            P("dp", None, "head"),
            P("head", "dp"),
            P("dp", "head"),
            P("head", "dp"),
            P("dp"),
            P("dp"),
            P("head"),
            P("head", None, None, "dp", None),
        ),
        check_vma=False,
    )
```

```python
import functools
import math

import jax
import jax.numpy as jnp
from jax import lax
from jax.experimental import pallas as pl
from jax.experimental.pallas import tpu as pltpu
from jax.sharding import PartitionSpec as P

HD = 128
CE = 170
EPS = 1e-05
LOG2E = 1.0 / math.log(2.0)
HEAD_SCALE = 1.0 / math.sqrt(HD)
BASE2 = HEAD_SCALE * LOG2E
F32 = jnp.float32
BF16 = jnp.bfloat16
KEEP = BF16
VMEM_LIMIT = 67043328


def bits_of(count):
    return count.bit_length() - 1


def flip_pairs(count, bit):
    return [(i, i ^ (1 << bit)) for i in range(count)]


def call(body, grid, in_specs, out_specs, out_shape, scratch=(), prefetch=0, cover=False, name=None, aliases=None):
    return pl.pallas_call(
        body,
        grid_spec=pltpu.PrefetchScalarGridSpec(
            num_scalar_prefetch=prefetch,
            grid=grid,
            in_specs=in_specs,
            out_specs=out_specs,
            scratch_shapes=list(scratch),
        ),
        out_shape=out_shape,
        input_output_aliases=aliases or {},
        compiler_params=pltpu.CompilerParams(dimension_semantics=("arbitrary",) * len(grid), vmem_limit_bytes=VMEM_LIMIT),
        cost_estimate=pl.CostEstimate(flops=10**13 if cover else 0, bytes_accessed=0, transcendentals=0),
        name=name,
    )


def whole(shape):
    zeros = (0,) * len(shape)
    return pl.BlockSpec(shape, lambda *_: zeros, pipeline_mode=pl.Buffered(1))


def per_stream(rows, n):
    return pl.BlockSpec((1, rows, n), lambda s, *_: (s, 0, 0))


def turned(rows, n):
    return pl.BlockSpec((n, rows), lambda s, *_: (0, s))


def like(streams, rows, n, kind):
    return jax.ShapeDtypeStruct((streams, rows, n), kind)


def dot(a, b):
    return jnp.dot(a, b, preferred_element_type=F32)


def dot_nt(a, b):
    return lax.dot_general(a, b, (((1,), (1,)), ((), ())), preferred_element_type=F32)


def dot_tn(a, b):
    return lax.dot_general(a, b, (((0,), (0,)), ((), ())), preferred_element_type=F32)


def statistics(v):
    centred = v - jnp.mean(v, axis=-1, keepdims=True)
    spread = jnp.mean(centred * centred, axis=-1, keepdims=True)
    return centred, lax.rsqrt(spread + EPS)


def norm_back(v, e):
    centred = v - jnp.mean(v, axis=-1, keepdims=True)
    spread = jnp.mean(centred * centred, axis=-1, keepdims=True)
    middle = jnp.mean(e, axis=-1, keepdims=True)
    along = jnp.mean(e * centred, axis=-1, keepdims=True)
    scale = lax.rsqrt(spread + EPS)
    return scale * (e - middle - centred * (scale * scale * along))


def by_rows(rows, step, body, together=8):
    def one(i, carry):
        for j in range(together):
            body(pl.multiple_of((i * together + j) * step, step))
        return carry

    if rows == step * together:
        for j in range(together):
            body(j * step)
    else:
        lax.fori_loop(0, rows // (step * together), one, 0)


def row_ids(start, step):
    return start + lax.broadcasted_iota(jnp.int32, (step, 1), 0)


def project_body(len_ref, x_ref, gain_ref, w_ref, normed_t_ref, q_ref, kv_ref, normed_ref):
    rows = q_ref.shape[1]
    length = len_ref[pl.program_id(0)]

    def norm(r):
        centred, scale = statistics(x_ref[0, pl.ds(r, 16), :].astype(F32))
        normed_ref[pl.ds(r, 16), :] = (centred * scale * gain_ref[...]).astype(BF16)

    by_rows(rows, 16, norm, rows // 16)
    normed_t_ref[...] = normed_ref[...].T
    valid = row_ids(0, rows) < length
    normed = normed_ref[...]
    q_ref[0] = dot(normed, w_ref[0]).astype(BF16)
    for c in range(2):
        now = dot(normed, w_ref[c + 1])
        kv_ref[0, c] = jnp.where(valid, now, 0.0).astype(BF16)


def project(lengths, x, gain, w):
    streams, rows, model = x.shape
    width = w.shape[2]
    per = lambda *tail: pl.BlockSpec((1,) + tail, lambda s, *_: (s,) + (0,) * len(tail))
    return call(
        project_body,
        (streams,),
        [per(rows, model), whole((1, model)), whole(w.shape)],
        [pl.BlockSpec((model, rows), lambda s, *_: (0, s)), per(rows, width), per(2, rows, width)],
        [
            jax.ShapeDtypeStruct((model, streams * rows), BF16),
            jax.ShapeDtypeStruct((streams, rows, width), BF16),
            jax.ShapeDtypeStruct((streams, 2, rows, width), BF16),
        ],
        scratch=[pltpu.VMEM((rows, model), BF16)],
        prefetch=1,
        name="project",
    )(lengths, x, gain, w)


def position_columns(keys):
    centre = keys // 2
    lane = lax.broadcasted_iota(jnp.int32, (keys, HD), 1)
    place = lax.broadcasted_iota(jnp.int32, (keys, HD), 0) - centre
    fine = place & 7
    coarse = place - fine
    value = jnp.where(lane < 6, jnp.where((lane & 1) == 0, coarse, fine), jnp.where(lane == 6, 1, 0))
    return value.astype(F32).astype(BF16)


def slope_columns(slope, rows):
    exact = jnp.full((8, HD), slope, F32) * (1.0 / HEAD_SCALE)
    first = exact.astype(BF16).astype(F32)
    second = (exact - first).astype(BF16).astype(F32)
    third = exact - first - second
    lane = lax.broadcasted_iota(jnp.int32, (8, HD), 1)
    value = jnp.where(lane < 2, first, jnp.where(lane < 4, second, jnp.where(lane < 6, third, 0.0)))
    return jnp.broadcast_to(value[:1], (rows, HD)).astype(BF16)


def one_column(keys):
    lane = lax.broadcasted_iota(jnp.int32, (keys, HD), 1)
    return jnp.where(lane == 0, 1.0, 0.0).astype(BF16)


def diagonal_mask(block, start, length):
    row = lax.broadcasted_iota(jnp.int32, (block, block), 0)
    col = lax.broadcasted_iota(jnp.int32, (block, block), 1)
    return col <= jnp.minimum(row, length - 1 - start)


def pipelined(chains, front, rest):
    following = front(*chains[0])
    for n, chain in enumerate(chains):
        current = following
        if n + 1 < len(chains):
            following = front(*chains[n + 1])
        rest(*chain, *current)


def lanes_of(a):
    return slice(a * HD, (a + 1) * HD)


def attend_body(len_ref, slope_ref, q_ref, old_ref, mem_ref, now_ref, wo_ref, mix_ref, exact_ref, lse_ref, part_ref, kbuf, vbuf):
    s = pl.program_id(0)
    rows, heads = q_ref.shape[1], q_ref.shape[2] // HD
    old, mem = old_ref.shape[2], mem_ref.shape[2]
    past = old + mem
    keys = past + rows
    block = rows // 2
    length = len_ref[s]

    @pl.when(s == 0)
    def _():
        for a in range(heads):
            kbuf[a, :, HD:] = position_columns(keys)
            vbuf[a, :, HD:] = one_column(keys)

    for a in range(heads):
        for buf, c in ((kbuf, 0), (vbuf, 1)):
            buf[a, :old, :HD] = old_ref[0, c, :, lanes_of(a)]
            buf[a, old:past, :HD] = mem_ref[0, c, :, lanes_of(a)]
            buf[a, past:, :HD] = now_ref[0, c, :, lanes_of(a)]

    def front(a, i):
        side = slope_columns(slope_ref[a], block)
        wide = jnp.concatenate([q_ref[0, i * block : (i + 1) * block, lanes_of(a)], side], axis=1)
        return (dot_nt(wide, kbuf[a, : past + (i + 1) * block]),)

    def rest(a, i, scores):
        high = (i + 1) * block
        here = slice(i * block, high)
        allowed = diagonal_mask(block, i * block, length)
        last = jnp.where(allowed, scores[:, past + i * block :], -1e30)
        scores = jnp.concatenate([scores[:, : past + i * block], last], axis=1)
        top = jnp.max(scores, axis=1, keepdims=True)
        weights = jnp.exp2((scores - top) * BASE2).astype(BF16)
        both = dot(weights, vbuf[a, : past + high])
        total = both[:, HD : HD + 1]
        mixed = both[:, :HD] / total
        exact_ref[0, here, lanes_of(a)] = mixed
        mix_ref[0, here, lanes_of(a)] = mixed.astype(BF16)
        lse_ref[0, here, lanes_of(a)] = jnp.broadcast_to(top * BASE2 + jnp.log2(total), (block, HD))

    @pl.when(length > block)
    def _():
        pipelined([(a, i) for a in range(heads) for i in range(2)], front, rest)

    @pl.when(length <= block)
    def _():
        pipelined([(a, 0) for a in range(heads)], front, rest)
        exact_ref[0, block:, :] = jnp.zeros((rows - block, heads * HD), F32)
        mix_ref[0, block:, :] = jnp.zeros((rows - block, heads * HD), BF16)
        lse_ref[0, block:, :] = jnp.zeros((rows - block, heads * HD), F32)

    part_ref[0] = dot(mix_ref[0], wo_ref[...]).astype(BF16)


def attend(lengths, slopes, q, compressed, memory, now, wo):
    streams, rows, width = q.shape
    heads = width // HD
    model = wo.shape[1]
    keys = compressed.shape[2] + memory.shape[2] + rows
    cache = lambda a: pl.BlockSpec((1, 2, a.shape[2], width), lambda s, *_: (s, 0, 0, 0))
    return call(
        attend_body,
        (streams,),
        [per_stream(rows, width), cache(compressed), cache(memory), cache(now), whole(wo.shape)],
        [per_stream(rows, width), per_stream(rows, width), per_stream(rows, width), per_stream(rows, model)],
        [
            jax.ShapeDtypeStruct((streams, rows, width), BF16),
            jax.ShapeDtypeStruct((streams, rows, width), F32),
            jax.ShapeDtypeStruct((streams, rows, width), F32),
            jax.ShapeDtypeStruct((streams, rows, model), BF16),
        ],
        scratch=[pltpu.VMEM((heads, keys, 2 * HD), BF16), pltpu.VMEM((heads, keys, 2 * HD), BF16)],
        prefetch=2,
        name="attend",
    )(lengths, slopes, q, compressed, memory, now, wo)


def attend_back_body(first, len_ref, slope_ref, q_ref, old_ref, mem_ref, now_ref, exact_ref, lse_ref, grad_ref, out_ref, slope_out_ref, kbuf, vbuf):
    s = pl.program_id(0)
    rows, heads = q_ref.shape[1], q_ref.shape[2] // HD
    old, mem = old_ref.shape[2], mem_ref.shape[2]
    past = old + mem
    keys = past + rows
    block = rows // 2
    length = len_ref[s]

    @pl.when(s == 0)
    def _():
        for a in range(heads):
            kbuf[a, :, HD:] = position_columns(keys)
        slope_out_ref[...] = jnp.zeros_like(slope_out_ref)

    for a in range(heads):
        kbuf[a, :old, :HD] = old_ref[0, 0, :, lanes_of(a)]
        kbuf[a, old:past, :HD] = mem_ref[0, 0, :, lanes_of(a)]
        kbuf[a, past:, :HD] = now_ref[0, 0, :, lanes_of(a)]
        vbuf[a, :old] = old_ref[0, 1, :, lanes_of(a)]
        vbuf[a, old:past] = mem_ref[0, 1, :, lanes_of(a)]
        vbuf[a, past:] = now_ref[0, 1, :, lanes_of(a)]

    def here(i):
        return slice(i * block, (i + 1) * block)

    def front(a, i):
        side = slope_columns(slope_ref[first + a], block)
        wide = jnp.concatenate([q_ref[0, here(i), lanes_of(a)], side], axis=1)
        reach = past + (i + 1) * block
        return dot_nt(wide, kbuf[a, :reach]), dot_nt(grad_ref[0, here(i), lanes_of(a)], vbuf[a, :reach])

    def run(blocks):
        sums = {}

        def rest(a, i, scores, grad_probs):
            reach = past + (i + 1) * block
            q, grad = q_ref[0, here(i), lanes_of(a)], grad_ref[0, here(i), lanes_of(a)]
            exact = jnp.exp2(scores * BASE2 - lse_ref[0, here(i), a * HD : a * HD + 1])
            allowed = diagonal_mask(block, i * block, length)
            last = jnp.where(allowed, exact[:, reach - block :], 0.0)
            exact = jnp.concatenate([exact[:, : reach - block], last], axis=1)
            inner = jnp.sum(grad.astype(F32) * exact_ref[0, here(i), lanes_of(a)], axis=1, keepdims=True)
            grad_scores = (exact * (grad_probs - inner)).astype(BF16)
            wide = dot(grad_scores, kbuf[a, :reach])
            out_ref[0, 0, here(i), lanes_of(a)] = (wide[:, :HD] * HEAD_SCALE).astype(BF16)
            coarse, fine, total = (wide[:, HD + n : HD + n + 1] for n in (0, 1, 6))
            distance = (past + i * block - keys // 2 + lax.broadcasted_iota(jnp.int32, (block, 1), 0)).astype(F32)
            moment = jnp.sum(coarse + fine - distance * total, axis=0, keepdims=True)
            grad_keys = dot_tn(grad_scores[:, past:], q)
            grad_values = dot_tn(exact[:, past:].astype(BF16), grad)
            if i > 0:
                moment = moment + sums[a][0]
                done = sums[a][1].shape[0]
                join = lambda before, now: jnp.concatenate([before + now[:done], now[done:]], axis=0)
                grad_keys, grad_values = join(sums[a][1], grad_keys), join(sums[a][2], grad_values)
            sums[a] = moment, grad_keys, grad_values
            if i == blocks - 1:
                high = blocks * block
                out_ref[1, 0, :high, lanes_of(a)] = (grad_keys * HEAD_SCALE).astype(BF16)
                out_ref[2, 0, :high, lanes_of(a)] = grad_values.astype(BF16)
                slope_out_ref[first + a : first + a + 1, :] += jnp.broadcast_to(moment, (1, HD))

        pipelined([(a, i) for a in range(heads) for i in range(blocks)], front, rest)

    @pl.when(length > block)
    def _():
        run(2)

    @pl.when(length <= block)
    def _():
        run(1)
        for c in range(3):
            out_ref[c, 0, block:, :] = jnp.zeros((rows - block, heads * HD), BF16)


def attend_back(first, heads, lengths, slopes, q, compressed, memory, now, exact, lse, grad):
    streams, rows, width = q.shape
    keys = compressed.shape[2] + memory.shape[2] + rows
    group = first // heads
    cache = lambda a: pl.BlockSpec((1, 2, a.shape[2], heads * HD), lambda s, *_: (s, 0, 0, group))
    some = pl.BlockSpec((1, rows, heads * HD), lambda s, *_: (s, 0, group))
    return call(
        functools.partial(attend_back_body, first),
        (streams,),
        [some, cache(compressed), cache(memory), cache(now), some, some, some],
        [pl.BlockSpec((3, 1, rows, heads * HD), lambda s, *_: (0, s, 0, 0)), pl.BlockSpec((8, HD), lambda *_: (0, 0))],
        [jax.ShapeDtypeStruct((3, streams, rows, heads * HD), BF16), jax.ShapeDtypeStruct((8, HD), F32)],
        scratch=[pltpu.VMEM((heads, keys, 2 * HD), BF16), pltpu.VMEM((heads, keys, HD), BF16)],
        prefetch=2,
        cover=True,
        name="attend_back",
    )(lengths, slopes, q, compressed, memory, now, exact, lse, grad)


GELU_K = math.sqrt(2.0 / math.pi)
GELU_C = 0.044715


def gate_of(v):
    square = v * v
    rate = -2.0 * GELU_K * LOG2E
    return 1.0 / (1.0 + jnp.exp2(v * (rate + (rate * GELU_C) * square))), square


def gelu_slope(v):
    gate, square = gate_of(v)
    lean = v * (2.0 * GELU_K + (6.0 * GELU_K * GELU_C) * square)
    return gate * (1.0 + lean * (1.0 - gate))


def rise_body(len_ref, x_ref, own_ref, other_ref, gain_ref, up_ref, mid_ref, normed_t_ref, active_ref, before_ref, normed):
    rows = x_ref.shape[1]
    hidden_width = up_ref.shape[1]
    length = len_ref[pl.program_id(0)]

    def norm(r):
        here = pl.ds(r, 16)
        valid = (row_ids(r, 16) < length).astype(F32)
        attended = own_ref[0, here, :].astype(F32) + other_ref[0, here, :].astype(F32)
        middle = x_ref[0, here, :].astype(F32) + attended * valid
        mid_ref[0, here, :] = middle.astype(BF16)
        centred, scale = statistics(middle)
        normed[here, :] = (centred * scale * gain_ref[...]).astype(BF16)

    by_rows(rows, 16, norm, rows // 16)
    normed_t_ref[...] = normed[...].T
    chunk = min(512, hidden_width)
    columns = [slice(f, f + chunk) for f in range(0, hidden_width, chunk)]

    def front(cols):
        return (dot(normed[...], up_ref[:, cols]),)

    def rest(cols, v):
        active_ref[0, :, cols] = (v * gate_of(v)[0]).astype(BF16)
        before_ref[0, :, cols] = v.astype(BF16)

    pipelined([(cols,) for cols in columns], front, rest)


def rise(lengths, x, own, other, gain, up):
    streams, rows, model = x.shape
    hidden = up.shape[1]
    tokens = streams * rows
    return call(
        rise_body,
        (streams,),
        [per_stream(rows, model)] * 3 + [whole((1, model)), whole(up.shape)],
        [per_stream(rows, model), turned(rows, model), per_stream(rows, hidden), per_stream(rows, hidden)],
        [
            like(streams, rows, model, BF16),
            jax.ShapeDtypeStruct((model, tokens), BF16),
            like(streams, rows, hidden, BF16),
            like(streams, rows, hidden, BF16),
        ],
        scratch=[pltpu.VMEM((rows, model), BF16)],
        prefetch=1,
        name="rise",
    )(lengths, x, own, other, gain, up)


def fall_body(len_ref, cot_ref, before_ref, up_ref, down_ref, hidden_ref, *back_refs):
    rows = cot_ref.shape[1]
    hidden_width = up_ref.shape[1]
    valid = row_ids(0, rows) < len_ref[pl.program_id(0)]
    branch = jnp.where(valid, cot_ref[0].astype(F32), 0.0).astype(BF16)
    chunk = min(1024, hidden_width)
    back = []

    def front(cols):
        return (dot_nt(branch, down_ref[cols, :]),)

    def rest(cols, grad_active):
        grad_hidden = (grad_active * gelu_slope(before_ref[0, :, cols].astype(F32))).astype(BF16)
        hidden_ref[0, :, cols] = grad_hidden
        back.append(dot_nt(grad_hidden, up_ref[:, cols]))

    pipelined([(slice(f, f + chunk),) for f in range(0, hidden_width, chunk)], front, rest)
    total = sum(back[1:], back[0]).astype(BF16)
    part = total.shape[1] // len(back_refs)
    for n, back_ref in enumerate(back_refs):
        back_ref[0] = total[:, n * part : (n + 1) * part]


PIECES = 2


def fall(lengths, cot, slope, up, down):
    streams, rows, model = cot.shape
    hidden = up.shape[1]
    tokens = streams * rows
    return call(
        fall_body,
        (streams,),
        [per_stream(rows, model), per_stream(rows, hidden), whole(up.shape), whole(down.shape)],
        [per_stream(rows, hidden)] + [per_stream(rows, model // PIECES)] * PIECES,
        [like(streams, rows, hidden, BF16)] + [like(streams, rows, model // PIECES, BF16)] * PIECES,
        prefetch=1,
        name="fall",
    )(lengths, cot, slope, up, down)


def leave_body(_, active_ref, down_ref, part_ref):
    part_ref[0] = dot(active_ref[0], down_ref[...]).astype(BF16)


def leave(lengths, active, down):
    streams, rows, hidden = active.shape
    model = down.shape[1]
    return call(
        leave_body,
        (streams,),
        [per_stream(rows, hidden), whole(down.shape)],
        per_stream(rows, model),
        like(streams, rows, model, BF16),
        prefetch=1,
        cover=True,
        name="leave",
    )(lengths, active, down)


def outputs_body(start, len_ref, mid_ref, own_ref, other_ref, out_ref):
    rows = mid_ref.shape[1]
    length = len_ref[start + pl.program_id(0)]

    def one(r):
        here = pl.ds(r, 16)
        valid = (row_ids(r, 16) < length).astype(F32)
        branch = own_ref[0, here, :].astype(F32) + other_ref[0, here, :].astype(F32)
        out_ref[0, here, :] = mid_ref[0, here, :].astype(F32) + valid * branch

    by_rows(rows, 16, one, 4)


def in_part(body, first, count, into, lengths, args, gain, like_this, name):
    rows, model = like_this.shape[1:]
    per = pl.BlockSpec((1, rows, model), lambda s, *_: (s + first, 0, 0))
    extra = [] if gain is None else [whole(gain.shape)]
    held = [] if into is None else [into]

    def inner(len_ref, *refs):
        body(first, len_ref, *refs[: len(args) + len(extra)], refs[-1])

    return call(
        inner,
        (count,),
        [per] * len(args) + extra + [pl.BlockSpec(memory_space=pl.ANY)] * len(held),
        per,
        jax.ShapeDtypeStruct(like_this.shape, F32),
        prefetch=1,
        cover=first > 0 or gain is None,
        aliases={1 + len(args) + len(extra): 0} if held else {},
        name=name,
    )(lengths, *args, *([] if gain is None else [gain]), *held)


def chunk_at(place, order, me):
    apart = 0
    for i, bit in enumerate(order):
        apart |= ((place >> (len(order) - 1 - i)) & 1) << bit
    return apart ^ me


def send_order(source, order, me, first, count):
    deep = source.shape[0] // (1 << len(order))
    lines = []
    for p in range(first, first + count):
        lines.append(source[pl.ds(pl.multiple_of(chunk_at(p, order, me) * deep, deep), deep), :])
    return jnp.concatenate(lines, axis=0)


def weight_body(spans, extra, order, me_ref, *refs):
    products = sum(span[2] for span in spans)
    xts, ys = list(refs[:products]), refs[products : products + len(spans)]
    sides, outs = refs[products + len(spans) :], refs[-3 if extra else -2 :]
    sides, keep_ref, send_ref = sides[: -len(outs)], outs[0], outs[1]
    me = me_ref[0]
    j = pl.program_id(0)
    places = 1 << len(order)
    half = keep_ref.shape[0]
    for y, (start, stop, product) in zip(ys, spans):
        xt = xts.pop(0) if product else None

        @pl.when((j >= start) & (j < stop))
        def _(xt=xt, y=y):
            for n, out in enumerate((keep_ref, send_ref)):
                rows = send_order(y if xt is None else xt, order, me, n * places // 2, places // 2)
                if xt is not None:
                    rows = dot(rows, y[...] if len(y.shape) == 2 else y[0])
                out[:half, :] = rows.astype(out.dtype)

    if extra:
        total = sum(side[...] for side in sides)
        first = total.astype(BF16).astype(F32)
        both = jnp.concatenate([first, total - first], axis=0).astype(BF16)
        times = send_ref.shape[1] // HD
        send_ref[half:, :] = jnp.concatenate([both] * times, axis=1)
        outs[2][...] = jnp.concatenate([total] * times, axis=1)


def weight_gradient(me, order, sources, step, name, sides=()):
    xts = [xt for xt, _ in sources if xt is not None]
    model, tokens = xts[0].shape
    spans, specs, at = [], [], 0
    for xt, y in sources:
        n = y.shape[-1] // step
        blocks = n * (y.shape[0] if y.ndim == 3 else 1)
        spans.append((at, at + blocks, xt is not None))
        if y.ndim == 3:
            pick = lambda j, *_, at=at, n=n, blocks=blocks: (jnp.clip(j - at, 0, blocks - 1) // n, 0, jnp.clip(j - at, 0, blocks - 1) % n)
            specs.append(pl.BlockSpec((1, y.shape[1], step), pick))
        else:
            specs.append(pl.BlockSpec((y.shape[0], step), lambda j, *_, at=at, blocks=blocks: (0, jnp.clip(j - at, 0, blocks - 1))))
        at += blocks
    columns = at * step
    extra = 16 if sides else 0
    heights = (model // 2, model // 2 + extra) + ((8,) if sides else ())
    return call(
        functools.partial(weight_body, spans, extra, order),
        (at,),
        [whole(xt.shape) for xt in xts] + specs + [whole(side.shape) for side in sides],
        [pl.BlockSpec((n, step), lambda j, *_: (0, j)) for n in heights],
        [jax.ShapeDtypeStruct((n, columns), kind) for n, kind in zip(heights, (KEEP, BF16, F32))],
        prefetch=1,
        name=name,
    )(me, *xts, *[y for _, y in sources], *sides)


class Halving:
    def __init__(self, keep, send, order, count, side=None, cut=None):
        self.order, self.count, self.stage, self.total = order, count, 0, None
        self.cuts = (0, cut or keep.shape[1], keep.shape[1])
        self.keep, self.side = keep, side
        self.send(send)

    def send(self, what):
        self.sent = what
        self.came = lax.ppermute(what, "dp", flip_pairs(self.count, self.order[self.stage]))


def sum_of(keep, came, rows, columns=slice(None)):
    return keep[rows, columns].astype(F32) + came[rows, columns].astype(F32)


def side_sum(before, came, high):
    both = came[high:, :].astype(F32)
    return before[...] + (both[:8] + both[8:])


def advance_body(items, *refs):
    refs = list(refs)
    ins = [[refs.pop(0) for _ in range(3 if side else 2)] for _, side in items]
    for (cuts, side), (keep, came, *before) in zip(items, ins):
        high = keep.shape[0]
        half = high // 2
        if cuts:
            parts = [(refs.pop(0), slice(a, b)) for a, b in zip(cuts, cuts[1:]) if a < b]

            @pl.when(pl.program_id(0) == 0)
            def _(keep=keep, came=came, parts=parts, high=high):
                for out, columns in parts:
                    out[...] = sum_of(keep, came, slice(0, high), columns)

        else:
            stay, go = refs.pop(0), refs.pop(0)
            stay[...] = sum_of(keep, came, slice(0, half)).astype(stay.dtype)
            go[:half, :] = sum_of(keep, came, slice(half, high)).astype(BF16)
            if side:
                total = side_sum(before[0], came, high)
                refs.pop(0)[...] = total
                first = total.astype(BF16).astype(F32)
                go[half:, :] = jnp.concatenate([first, total - first], axis=0).astype(BF16)


def advance(rounds, token):
    rounds = [r for r in rounds if r.total is None]
    if not rounds:
        return token
    turns = 4 if all(r.keep.shape[1] % (4 * HD) == 0 for r in rounds) else 2
    blocks = lambda a: pl.BlockSpec((a.shape[0], a.shape[1] // turns), lambda j: (0, j))
    items, args, outs, in_specs, out_specs = [], [], [], [], []
    for r in rounds:
        final, side = r.stage + 1 == len(r.order), r.side is not None
        high, columns = r.keep.shape
        items.append((r.cuts if final else None, side))
        mine = [r.keep, after(r.came, token)] + ([r.side] if side else [])
        if final:
            made = [jax.ShapeDtypeStruct((high, b - a), F32) for a, b in zip(r.cuts, r.cuts[1:]) if a < b]
        else:
            made = [
                jax.ShapeDtypeStruct((high // 2, columns), KEEP),
                jax.ShapeDtypeStruct((high // 2 + (16 if side else 0), columns), BF16),
            ] + ([jax.ShapeDtypeStruct(r.side.shape, F32)] if side else [])
        args += mine
        outs += made
        in_specs += [whole(a.shape) if final else blocks(a) for a in mine]
        out_specs += [pl.BlockSpec(a.shape, lambda j: (0, 0)) if final else blocks(a) for a in made]
    got = list(call(functools.partial(advance_body, items), (turns,), in_specs, out_specs, outs, name="advance")(*args))
    token = got[0]
    for r, (cuts, side) in zip(rounds, items):
        r.stage += 1
        if cuts:
            r.total = [got.pop(0) for a, b in zip(cuts, cuts[1:]) if a < b]
            continue
        r.keep, send = got.pop(0), got.pop(0)
        if side:
            r.side = got.pop(0)
        r.send(send)
    return token


def finish_body(share, _, *refs):
    *ins, before, keep_up, came_up, w_ref, up_w_ref, qkv_ref, out_ref, up_ref, gain_ref = refs
    high = keep_up.shape[0]
    rows = slice(0, high)
    for g in range(len(ins) // 2):
        keep, came = ins[2 * g], ins[2 * g + 1]
        for c in range(3):
            qkv_ref[c, :, g * share : (g + 1) * share] = sum_of(keep, came, rows, slice(c * share, (c + 1) * share))
        if g == 0:
            out_ref[...] = sum_of(keep, came, rows, slice(3 * share, keep.shape[1]))
    side = side_sum(before, ins[-1], high)[:, :HD]
    total = sum_of(keep_up, came_up, rows)
    up_ref[...] = total
    ahead = sum(jnp.sum(qkv_ref[c] * w_ref[c].astype(F32), axis=1, keepdims=True) for c in range(3))
    rising = jnp.sum(total * up_w_ref[...].astype(F32), axis=1, keepdims=True)
    lane = lax.broadcasted_iota(jnp.int32, (high, HD), 1)
    side = jnp.concatenate([side, jnp.zeros((high - 8, HD), F32)], axis=0)
    columns = jnp.where(lane == 0, ahead, jnp.where(lane == 1, rising, side))
    gain_ref[...] = jnp.concatenate([columns, jnp.zeros((HD - high, HD), F32)], axis=0).T[:8]


def finish(me, rounds, up, token, share, w, up_weight):
    high = up.keep.shape[0]
    width = share * len(rounds)
    args = [a for r in rounds for a in (r.keep, after(r.came, token))] + [rounds[-1].side, up.keep, after(up.came, token)]
    hidden = up_weight.shape[1]
    mine = [pl.BlockSpec((3, high, width), lambda j, me: (0, me[0], 0)), pl.BlockSpec((high, hidden), lambda j, me: (me[0], 0))]
    made = [(3, high, width), (high, width), (high, hidden), (8, HD)]
    return call(
        functools.partial(finish_body, share),
        (1,),
        [whole(a.shape) for a in args] + mine,
        [whole(a) for a in made],
        [jax.ShapeDtypeStruct(a, F32) for a in made],
        prefetch=1,
        name="finish",
    )(me, *args, w, up_weight)


def after(value, token):
    return lax.optimization_barrier((value, token))[0]


def conv_share(total, like, ranks, model):
    share = like.shape[3] // ranks
    pieces = math.prod(like.shape[:3])
    groups = -(-pieces * HD // model)
    total = total[:, : groups * HD].reshape(model // HD, share, groups, HD).transpose(2, 0, 1, 3)
    return total.reshape(groups * (model // HD), share, HD)[:pieces].reshape(like.shape[:3] + (share, HD))


def pair_over_head(part):
    count = lax.axis_size("head")
    for bit in range(bits_of(count)):
        came = lax.ppermute(part, "head", flip_pairs(count, bit))
        if bit == bits_of(count) - 1:
            return part, came
        part = (part.astype(F32) + came.astype(F32)).astype(part.dtype)
    return part, jnp.zeros_like(part)


def middle_body(len_ref, *refs):
    owns, others = refs[:PIECES], refs[PIECES : 2 * PIECES]
    mid_ref, cot_ref, gain_ref, wo_ref, grad_ref, turned_ref, mixed_ref, attended = refs[2 * PIECES :]
    rows = mid_ref.shape[1]
    s = pl.program_id(0)
    length = len_ref[s]

    def one(r):
        here = pl.ds(r, 16)
        valid = (row_ids(r, 16) < length).astype(F32)
        middle = mid_ref[0, here, :].astype(F32)
        sums = [own[0, here, :].astype(F32) + other[0, here, :].astype(F32) for own, other in zip(owns, others)]
        grad = jnp.concatenate(sums, axis=1)
        total = cot_ref[0, here, :].astype(F32) + norm_back(middle, grad * gain_ref[...])
        grad_ref[0, here, :] = total.astype(BF16)
        attended[here, :] = (total * valid).astype(BF16)

    by_rows(rows, 16, one)
    turned_ref[...] = attended[...].T
    mixed_ref[0] = dot_nt(attended[...], wo_ref[...]).astype(BF16)


def middle_back(lengths, owns, others, mid, cot, gain, wo):
    streams, rows, model = mid.shape
    width = wo.shape[0]
    return call(
        middle_body,
        (streams,),
        [per_stream(rows, model // PIECES)] * (2 * PIECES) + [per_stream(rows, model)] * 2 + [whole((1, model)), whole(wo.shape)],
        [per_stream(rows, model), turned(rows, model), per_stream(rows, width)],
        [
            jax.ShapeDtypeStruct(mid.shape, BF16),
            jax.ShapeDtypeStruct((model, streams * rows), BF16),
            like(streams, rows, width, BF16),
        ],
        scratch=[pltpu.VMEM((rows, model), BF16)],
        prefetch=1,
        name="middle_back",
    )(lengths, *owns, *others, mid, cot, gain, wo)


def lower_body(_, *refs):
    pieces, (w_ref, part_ref) = refs[:-2], refs[-2:]
    total = None
    for c in range(3):
        more = dot_nt(jnp.concatenate([piece[c, 0] for piece in pieces], axis=1), w_ref[c])
        total = more if total is None else total + more
    part_ref[0] = total.astype(BF16)


def lower(lengths, pieces, w):
    model = w.shape[1]
    _, streams, rows, _ = pieces[0].shape
    joint = lambda a: pl.BlockSpec((3, 1, rows, a.shape[3]), lambda s, *_: (0, s, 0, 0))
    return call(
        lower_body,
        (streams,),
        [joint(a) for a in pieces] + [whole(w.shape)],
        per_stream(rows, model),
        like(streams, rows, model, BF16),
        prefetch=1,
        name="lower",
    )(lengths, *pieces, w)


def inputs_body(_, __, x_ref, own_ref, other_ref, grad_ref, gain_ref, out_ref):
    rows = x_ref.shape[1]

    def one(r):
        here = pl.ds(r, 16)
        e = (own_ref[0, here, :].astype(F32) + other_ref[0, here, :].astype(F32)) * gain_ref[...]
        out_ref[0, here, :] = grad_ref[0, here, :].astype(F32) + norm_back(x_ref[0, here, :].astype(F32), e)

    by_rows(rows, 16, one)


SLOTS = 256


def rebuild_body(len_ref, q_ref, mem_ref, old_ref, conv_ref, cot_ref, next_ref, rows_ref, branch_t_ref, wide, grad_ref):
    s = pl.program_id(0)
    rows, heads = q_ref.shape[1], q_ref.shape[2] // HD
    slots = mem_ref.shape[2]
    made = slots // 3
    valid = row_ids(0, rows) < len_ref[s]
    valid_lane = lax.broadcasted_iota(jnp.int32, (1, rows), 1) < len_ref[s]
    row = lax.broadcasted_iota(jnp.int32, (slots, HD), 0)

    @pl.when(s == 0)
    def _():
        grad_ref[...] = jnp.zeros_like(grad_ref)
        wide[...] = jnp.zeros_like(wide)

    def front(a):
        windows, packed = [], []
        for c in range(2):
            wide[a, c, :slots] = mem_ref[0, c, :, lanes_of(a)].astype(F32)
            taps = [wide[a, c, pl.ds(t, SLOTS, stride=3), :].astype(BF16) for t in range(3)]
            windows.append(jnp.concatenate(taps, axis=1))
            squeezed = dot(windows[c], conv_ref[a, c].reshape(3 * HD, HD))
            packed.append(squeezed.astype(BF16))
            tail = jnp.concatenate([squeezed, jnp.zeros((slots - SLOTS, HD), F32)], axis=0)
            kept = pltpu.roll(old_ref[0, c, :, lanes_of(a)].astype(F32), slots - made, 0)
            tail = pltpu.roll(tail, slots - made, 0)
            next_ref[0, c, :, lanes_of(a)] = jnp.where(row < slots - made, kept, tail).astype(BF16)
        q = q_ref[0, :, lanes_of(a)]
        return windows, packed, dot_nt(mem_ref[0, 0, :, lanes_of(a)], q), dot_nt(packed[0], q)

    def soft(scores, count):
        start = count // 8 * 8
        key = start + lax.broadcasted_iota(jnp.int32, (scores.shape[0] - start, rows), 0)
        last = jnp.where(key < count, scores[start:], -1e30)
        scores = jnp.concatenate([scores[:start], last], axis=0)
        weights = jnp.exp2((scores - jnp.max(scores, axis=0, keepdims=True)) * BASE2)
        return weights, 1.0 / jnp.sum(weights, axis=0, keepdims=True)

    def rest(a, windows, packed, scores, few_scores):
        weights, share = soft(few_scores, made)
        probs = weights * share
        low = probs.astype(BF16)
        approach = dot(packed[1].T, low)
        weights, share = soft(scores, 3 * made)
        target = dot(mem_ref[0, 1, :, lanes_of(a)].T, weights.astype(BF16)) * share
        grad = jnp.where(valid_lane, (approach - target) * (2.0 / rows), 0.0).astype(BF16)
        grad_probs = dot(packed[1], grad)
        inner = jnp.sum(probs * grad_probs, axis=0, keepdims=True)
        grad_scores = (probs * (grad_probs - inner) * HEAD_SCALE).astype(BF16)
        back = [dot(grad_scores, q_ref[0, :, lanes_of(a)]), dot_nt(low, grad)]
        for c in range(2):
            grad_ref[a, c] += dot_tn(windows[c], back[c].astype(BF16)).reshape(3, HD, HD)

    pipelined([(a,) for a in range(heads)], front, rest)
    branch_t_ref[...] = jnp.where(valid, cot_ref[0], jnp.zeros_like(cot_ref[0])).T

    @pl.when(s == pl.num_programs(0) - 1)
    def _():
        ranks, deep, _ = rows_ref.shape
        share = HD // ranks
        rows_ref[...] = jnp.zeros_like(rows_ref)
        for a in range(heads):
            for n in range(6):
                piece = 6 * a + n
                at, group = piece % (deep // share) * share, piece // (deep // share)
                rows_ref[:, at : at + share, group * HD : (group + 1) * HD] = grad_ref[a, n // 3, n % 3].reshape(ranks, share, HD)


def rebuild(lengths, q, memory, compressed, conv, cot, ranks, columns):
    model = cot.shape[2]
    streams, rows, width = q.shape
    heads = width // HD
    slots = memory.shape[2]
    cache = pl.BlockSpec((1, 2, slots, width), lambda s, *_: (s, 0, 0, 0))
    return call(
        rebuild_body,
        (streams,),
        [per_stream(rows, width), cache, cache, whole(conv.shape), per_stream(rows, model)],
        [cache, pl.BlockSpec((ranks, model // ranks, columns), lambda *_: (0, 0, 0)), turned(rows, model)],
        [
            jax.ShapeDtypeStruct(compressed.shape, BF16),
            jax.ShapeDtypeStruct((ranks, model // ranks, columns), F32),
            jax.ShapeDtypeStruct((model, streams * rows), BF16),
        ],
        scratch=[pltpu.VMEM((heads, 2, 3 * SLOTS, HD), F32), pltpu.VMEM(conv.shape, F32)],
        prefetch=1,
        cover=True,
        name="rebuild",
    )(lengths, q, memory, compressed, conv, cot)


def per_device(
    inputs,
    cotangent,
    lengths,
    memory,
    compressed,
    query_key_value_weight,
    output_weight,
    up_weight,
    down_weight,
    gain_one,
    gain_two,
    slope_rates,
    conv_weight,
):
    streams, rows, model = inputs.shape
    tokens = streams * rows
    heads = slope_rates.shape[0]
    width = heads * HD
    ranks = lax.axis_size("dp")
    rank_bits = bits_of(ranks)
    me = lax.axis_index("dp").astype(jnp.int32)
    me_array = me.reshape(1)
    later = tuple(range(2, rank_bits))
    x_first, x_then_z, y_first = (0, 1) + later, (0,) + later + (1,), (1, 0) + later
    y_then_mixed = (1, 2, 0) + later[1:]
    gain_1, gain_2 = gain_one.reshape(1, model), gain_two.reshape(1, model)
    qkv = query_key_value_weight.transpose(1, 0, 2)

    normed_t, q, memory_next = project(lengths, inputs, gain_1, qkv)
    mixed, exact, lse, part = attend(lengths, slope_rates, q, compressed, memory, memory_next, output_weight)
    own, other = pair_over_head(part)
    step = min(512, up_weight.shape[1])
    compressed_next, conv, branch_t = rebuild(after(lengths, part), q, memory, compressed, conv_weight, cotangent, ranks, step)
    conv = conv.reshape(model, step)
    mid, normed_two_t, active, before = rise(after(lengths, conv), inputs, own, other, gain_2, up_weight)
    sources = [(branch_t, active.reshape(tokens, -1)), (None, conv)]
    keep, send = weight_gradient(me_array, x_then_z, sources, step, "grad_down")
    down = Halving(keep, send, x_then_z, ranks, cut=up_weight.shape[1])
    grad_hidden, *backs = fall(after(lengths, send), cotangent, before, up_weight, down_weight)
    owns, others = zip(*[pair_over_head(back) for back in backs])
    keep, send = weight_gradient(me_array, y_first, [(normed_two_t, grad_hidden.reshape(tokens, -1))], step, "grad_up")
    up = Halving(keep, send, y_first, ranks)
    grad_middle, attended_t, grad_mixed = middle_back(
        after(lengths, send), owns, others, mid, cotangent, gain_2, output_weight
    )
    token = advance([down], grad_mixed)

    groups = 2 if heads % 2 == 0 else 1
    each = heads // groups
    pieces, sides, rounds = [], [], []
    for g in range(groups):
        piece, slopes = attend_back(
            g * each, each, after(lengths, token), slope_rates, q, compressed, memory, memory_next, exact, lse, grad_mixed
        )
        pieces.append(piece)
        sides.append(slopes)
        order = x_first if g else y_then_mixed
        sources = [(normed_t, piece.reshape(3, tokens, each * HD))]
        if g == 0:
            sources.append((attended_t, mixed.reshape(tokens, width)))
        final = g == groups - 1
        token = piece
        if final:
            part = lower(after(lengths, token), pieces, qkv)
            own, other = pair_over_head(part)
            token = part
        made = weight_gradient(after(me_array, token), order, sources, each * HD, "grad_joint", sides if final else ())
        keep, send = made[:2]
        rounds.append(Halving(keep, send, order, ranks, made[2] if final else None))
        token = advance([up, down], send) if g == 0 else send
    early, late = rounds[0], rounds[-1]
    both = rounds[::-1]

    token = advance([early, up, down] if groups > 1 else [up, down], token)
    branch = leave(after(lengths, token), active, down_weight)
    token = advance([late, down], branch)
    branch, branch_other = pair_over_head(after(branch, token))
    grad_inputs = None
    parts = 2 if streams % 2 == 0 else 1
    count = streams // parts
    for p in range(parts):
        grad_inputs = in_part(
            inputs_body, p * count, count, grad_inputs, after(lengths, token), [inputs, own, other, grad_middle], gain_1, mid, "inputs_back"
        )
        token = advance(both + ([] if p else [up]), grad_inputs)
    outputs = in_part(
        outputs_body, 0, streams, None, after(lengths, token), [mid, branch, branch_other], None, mid, "outputs"
    )
    token = outputs
    unfinished = lambda: [r for r in both + [up] if r.stage + 1 < len(r.order)] + [r for r in [down] if r.total is None]
    while unfinished():
        token = advance(unfinished(), token)
    total_qkv, total_out, total_up, gains = finish(me_array, rounds, up, token, each * HD, qkv, up_weight)

    total_down, conv_rows = down.total
    total_conv = conv_share(conv_rows, conv_weight, ranks, model)
    portion = model // ranks
    mine = lambda a: lax.dynamic_slice_in_dim(a, me * portion, portion, 0)
    slopes = gains[2, :heads]
    head_count = lax.axis_size("head")
    for bit in range(bits_of(head_count)):
        gains = gains + lax.ppermute(gains, "head", flip_pairs(head_count, bit))
    total_gain_one = gains[0, :portion] / mine(gain_one)
    total_gain_two = gains[1, :portion] / mine(gain_two)

    return (
        outputs,
        grad_inputs,
        memory_next,
        compressed_next,
        total_qkv.transpose(1, 0, 2),
        total_out.T,
        total_up,
        total_down.T,
        total_gain_one,
        total_gain_two,
        slopes,
        total_conv,
    )


def solution(mesh):
    placed = (
        P("dp", None, None),
        P("dp", None, None),
        P("dp"),
        P("dp", None, None, "head"),
        P("dp", None, None, "head"),
        P(None, None, "head"),
        P("head", None),
        P(None, "head"),
        P("head", None),
        P(),
        P(),
        P("head"),
        P("head", None, None, None, None),
    )
    return jax.shard_map(
        per_device,
        mesh=mesh,
        in_specs=placed,
        out_specs=(
            P("dp", None, None),
            P("dp", None, None),
            P("dp", None, None, "head"),
            P("dp", None, None, "head"),
            P("dp", None, "head"),
            P("head", "dp"),
            P("dp", "head"),
            P("head", "dp"),
            P("dp"),
            P("dp"),
            P("head"),
            P("head", None, None, "dp", None),
        ),
        check_vma=False,
    )
```
